32 devices in a mesh: dp: 2 (over x), ctx: 4 (over y, core), tp: 4 (over z).
Axes of the slice: x: 2, y: 2, z: 4, core: 2. Of those that a mesh axis runs over, the one named last changes fastest.
Arguments:
- block_in: bfloat16 [4, 2048, 2048], P(None, ('dp', 'ctx', 'tp')), may hold values from -6 to 6
- segments: int32 [4, 2048], P(None, 'dp'), may hold values from 0 to 1023, as said below
- positions: int32 [4, 2048], P(None, 'dp'), may hold values from 0 to 1023, as said below
- attention_gain: bfloat16 [2048], P(('dp', 'ctx')), may hold values from 0.5 to 1.5
- query_weight: bfloat16 [2048, 2048], P(('dp', 'ctx'), 'tp'), may hold values from -0.125 to 0.125
- key_weight: bfloat16 [2048, 512], P(('dp', 'ctx'), 'tp'), may hold values from -0.125 to 0.125
- value_weight: bfloat16 [2048, 512], P(('dp', 'ctx'), 'tp'), may hold values from -0.125 to 0.125
- query_gain: bfloat16 [64], replicated, may hold values from 1 to 2
- key_gain: bfloat16 [64], replicated, may hold values from 0.25 to 1.75
- output_weight: bfloat16 [2048, 2048], P('tp', ('dp', 'ctx')), may hold values from -0.75 to 0.75
- hidden_gain: bfloat16 [2048], P(('dp', 'ctx')), may hold values from 0.5 to 1.5
- gate_weight: bfloat16 [2048, 8192], P(('dp', 'ctx'), 'tp'), may hold values from -0.125 to 0.125
- up_weight: bfloat16 [2048, 8192], P(('dp', 'ctx'), 'tp'), may hold values from -0.125 to 0.125
- down_weight: bfloat16 [8192, 2048], P('tp', ('dp', 'ctx')), may hold values from -0.125 to 0.125
- cotangent: bfloat16 [4, 2048, 2048], P(None, ('dp', 'ctx', 'tp')), may hold values from -6 to 6
Outputs:
- block_out: bfloat16 [4, 2048, 2048], P(None, ('dp', 'ctx', 'tp'))
- input_grad: float32 [4, 2048, 2048], P(None, ('dp', 'ctx', 'tp'))
- attention_gain_grad: float32 [2048], P(('dp', 'ctx'))
- query_weight_grad: float32 [2048, 2048], P(('dp', 'ctx'), 'tp')
- key_weight_grad: float32 [2048, 512], P(('dp', 'ctx'), 'tp')
- value_weight_grad: float32 [2048, 512], P(('dp', 'ctx'), 'tp')
- query_gain_grad: float32 [64], replicated
- key_gain_grad: float32 [64], replicated
- output_weight_grad: float32 [2048, 2048], P('tp', ('dp', 'ctx'))
- hidden_gain_grad: float32 [2048], P(('dp', 'ctx'))
- gate_weight_grad: float32 [2048, 8192], P(('dp', 'ctx'), 'tp')
- up_weight_grad: float32 [2048, 8192], P(('dp', 'ctx'), 'tp')
- down_weight_grad: float32 [8192, 2048], P('tp', ('dp', 'ctx'))
The draws below stay inside these ranges and needn't reach their ends.
Inputs may be any that keep to these rules, and one draw needn't show every extreme that they name: `segments`: within each sequence of 1024 tokens a token's id is the place, counted from 0 in that sequence, of the first token of its document; ids never fall and a document is a run of equal ids. `positions`: each token's distance from the first token of its document.
All inputs are finite; a program needn't handle non-finite values.
Results may differ from the reference program's by a relative error of at most 0.019.
Values may be sent and summed in bfloat16 or wider, within the bound.
No kernel may reach another device: no remote copies, remote signals or barrier semaphores. Data moves between devices by JAX's collectives and lax.ppermute only.
A program may use at most 320 MiB of HBM per device.

```python
import math
import jax
import jax.numpy as jnp
from jax import lax

D = 2048
H = 32
KVH = 8
HD = 64
FF = 8192
LEN = 1024
MB = 4
SEQ_TOK = 2048
N_DP = 2


def doc_layout(seed_key):
    folded = jax.random.fold_in(seed_key, 7)
    pick_key, mark_key = jax.random.split(folded)
    seq_count = MB * N_DP
    periods = jnp.array([6, 40, 300, 4000], dtype=jnp.int32)
    chosen = jax.random.randint(pick_key, (seq_count, 1), 0, 4)
    period = jnp.sum(jnp.where(chosen == jnp.arange(4, dtype=jnp.int32)[None, :], periods[None, :], 0), axis=1, keepdims=True)
    marks = jax.random.randint(mark_key, (seq_count, LEN), 0, 1 << 20)
    places = jnp.arange(LEN, dtype=jnp.int32)[None, :]
    seq_rows = jnp.arange(seq_count, dtype=jnp.int32)[:, None]
    starts = (marks % period == 0) | (places == 0)
    starts = jnp.where(seq_rows == 0, places == 0, starts)
    starts = starts | (seq_rows == seq_count - 1) & (places == LEN - 1)
    first_place = lax.cummax(jnp.where(starts, places, 0), axis=1)
    position = places - first_place
    return (first_place.astype(jnp.int32).reshape(MB, N_DP * LEN), position.astype(jnp.int32).reshape(MB, N_DP * LEN))


def draw_segments(key, part):
    return doc_layout(key)[0]


def draw_positions(key, part):
    return doc_layout(key)[1]


def steps_of(own_key, extent, cuts, least, largest):
    factor_of, own = 1.0, jax.random.fold_in(own_key, 6)
    for dim, blocks in cuts:
        steps = jnp.exp(jax.random.uniform(jax.random.fold_in(own, dim), (blocks,), jnp.float32, least / len(cuts), largest / len(cuts)))
        factor_of = factor_of * jnp.repeat(steps, extent[dim] // blocks).reshape([-1 if axis == dim else 1 for axis in range(len(extent))])
    return factor_of


def scatter_about(rng, extent, scale, bound, pieces=(), kind=jnp.bfloat16):
    entries = scale * jax.random.normal(rng, extent, jnp.float32)
    if pieces:
        entries = entries * steps_of(rng, extent, pieces, -0.22, 0.18)
    return jnp.clip(entries, -bound, bound).astype(kind)


def setup_inputs(seed: int = 0) -> dict:
    streams_of = jax.random.split(jax.random.key(seed), 16)
    return {
        "block_in": scatter_about(streams_of[0], (MB, SEQ_TOK, D), 1.0, 6.0, ((1, 32),)),
        "segments": draw_segments(jax.random.fold_in(streams_of[15], 71), 0),
        "positions": draw_positions(jax.random.fold_in(streams_of[15], 71), 0),
        "attention_gain": jnp.clip(1.0 + 0.1 * jax.random.normal(streams_of[3], (D,), jnp.float32), 0.5, 1.5).astype(jnp.bfloat16),
        "query_weight": scatter_about(streams_of[4], (D, H * HD), D ** -0.5, 0.125, ((0, 8), (1, 4))),
        "key_weight": scatter_about(streams_of[5], (D, KVH * HD), D ** -0.5, 0.125, ((0, 8), (1, 4))),
        "value_weight": scatter_about(streams_of[6], (D, KVH * HD), D ** -0.5, 0.125, ((0, 8), (1, 4))),
        "query_gain": jnp.clip(jax.random.uniform(streams_of[7], (HD,), jnp.float32, 1.0, 2.0), 1.0, 2.0).astype(jnp.bfloat16),
        "key_gain": jnp.clip(1.0 + 0.15 * jax.random.normal(streams_of[8], (HD,), jnp.float32), 0.25, 1.75).astype(jnp.bfloat16),
        "output_weight": scatter_about(streams_of[9], (H * HD, D), (H * HD // 32) ** -0.5, 0.75, ((0, 4), (1, 8))),
        "hidden_gain": jnp.clip(1.0 + 0.1 * jax.random.normal(streams_of[10], (D,), jnp.float32), 0.5, 1.5).astype(jnp.bfloat16),
        "gate_weight": scatter_about(streams_of[11], (D, FF), D ** -0.5, 0.125, ((0, 8), (1, 4))),
        "up_weight": scatter_about(streams_of[12], (D, FF), D ** -0.5, 0.125, ((0, 8), (1, 4))),
        "down_weight": scatter_about(streams_of[13], (FF, D), (FF // 4) ** -0.5, 0.125, ((0, 4), (1, 8))),
        "cotangent": scatter_about(streams_of[14], (MB, SEQ_TOK, D), 1.0, 6.0, ((1, 32),)),
    }


NORM_EPS = 1e-05
ROPE_BASE = 1000000.0
MASKED = -1e+30
HIGHEST = lax.Precision.HIGHEST

@jax.custom_vjp
def low(v):
    return lax.optimization_barrier(v.astype(jnp.bfloat16)).astype(jnp.float32)

@jax.custom_vjp
def low_back(v):
    return v

def low_keep(v):
    return (low(v), None)

def low_pass(kept, grad):
    return (grad,)

def back_keep(v):
    return (v, None)

def back_low(kept, grad):
    return (low(grad),)
low.defvjp(low_keep, low_pass)
low_back.defvjp(back_keep, back_low)

def matmul(left_mat, right_mat):
    return jnp.dot(left_mat, right_mat, precision=HIGHEST, preferred_element_type=jnp.float32)

def rms_scale(values, gain_vec):
    return values * lax.rsqrt(lax.optimization_barrier(jnp.mean(values * values, axis=-1, keepdims=True)) + NORM_EPS) * gain_vec

def rotate(values, position):
    head_width = values.shape[-1]
    half_width = head_width // 2
    frequency = ROPE_BASE ** (-2.0 * jnp.arange(half_width, dtype=jnp.float32) / head_width)
    angles = position.astype(jnp.float32)[:, None, None] * frequency[None, None, :]
    cos_table = jnp.cos(angles)
    sin_table = jnp.sin(angles)
    former = values[..., :half_width]
    latter = values[..., half_width:]
    return jnp.concatenate([former * cos_table - latter * sin_table, latter * cos_table + former * sin_table], axis=-1)

def attend_one(operands):
    queries, key_vecs, values, segment = operands
    group_size = queries.shape[1] // key_vecs.shape[1]
    keys_all = jnp.repeat(key_vecs, group_size, axis=1)
    values_all = jnp.repeat(values, group_size, axis=1)
    inv_root = 1.0 / math.sqrt(queries.shape[-1])
    scores = low_back(jnp.einsum('qhd,khd->hqk', queries, keys_all, precision=HIGHEST) * inv_root)
    places = jnp.arange(queries.shape[0], dtype=jnp.int32)
    allowed = (segment[:, None] == segment[None, :]) & (places[:, None] >= places[None, :])
    scores = jnp.where(allowed[None], scores, MASKED)
    row_top = lax.optimization_barrier(jnp.max(scores, axis=-1, keepdims=True))
    exp_scores = jnp.exp(scores - row_top)
    probability = exp_scores / lax.optimization_barrier(jnp.sum(exp_scores, axis=-1, keepdims=True))
    return jnp.einsum('hqk,khd->qhd', low(probability), values_all, precision=HIGHEST)

def layer_step(weights, operands):
    attention_gain, query_weight, key_weight, value_weight, query_gain, key_gain, output_weight, hidden_gain, gate_weight, up_weight, down_weight = weights
    tokens, segment, position = operands
    seq_count, length, model_width = tokens.shape
    flat_rows = tokens.reshape(seq_count * length, model_width)
    normed = low(rms_scale(flat_rows, attention_gain))
    queries = low_back(matmul(normed, query_weight)).reshape(seq_count, length, -1, HD)
    key_vecs = low_back(matmul(normed, key_weight)).reshape(seq_count, length, -1, HD)
    values = low(low_back(matmul(normed, value_weight))).reshape(seq_count, length, -1, HD)
    queries = low(jax.vmap(rotate)(rms_scale(queries, query_gain), position))
    key_vecs = low(jax.vmap(rotate)(rms_scale(key_vecs, key_gain), position))
    attended = lax.map(jax.checkpoint(attend_one), (queries, key_vecs, values, segment))
    attended = low(low_back(attended.reshape(seq_count * length, -1)))
    hidden = flat_rows + low_back(matmul(attended, output_weight))
    hidden_normed = low(rms_scale(hidden, hidden_gain))
    gate_proj = low_back(matmul(hidden_normed, gate_weight))
    up_proj = low_back(matmul(hidden_normed, up_weight))
    activation = low(jax.nn.silu(gate_proj) * up_proj)
    output = hidden + low_back(matmul(activation, down_weight))
    return (weights, output.reshape(seq_count, length, model_width))

def forward(tokens, weights, segment, position):
    seq_total = tokens.shape[0]
    group_size = math.gcd(seq_total, max(1, 4096 // LEN))
    steps_count = seq_total // group_size
    grouped = (tokens.reshape((steps_count, group_size) + tokens.shape[1:]), segment.reshape(steps_count, group_size, LEN), position.reshape(steps_count, group_size, LEN))
    unused, output = lax.scan(jax.checkpoint(layer_step), weights, grouped)
    return output.reshape(tokens.shape)

def reference(block_in, segments, positions, attention_gain, query_weight, key_weight, value_weight, query_gain, key_gain, output_weight, hidden_gain, gate_weight, up_weight, down_weight, cotangent):
    seq_count = MB * N_DP
    tokens = block_in.astype(jnp.float32).reshape(seq_count, LEN, D)
    segment = segments.reshape(seq_count, LEN)
    position = positions.reshape(seq_count, LEN)
    weights = tuple((weight_arr.astype(jnp.float32) for weight_arr in (attention_gain, query_weight, key_weight, value_weight, query_gain, key_gain, output_weight, hidden_gain, gate_weight, up_weight, down_weight)))

    def whole_pass(tokens_in, *params):
        return forward(tokens_in, params, segment, position)
    output, pullback = jax.vjp(whole_pass, tokens, *weights)
    grads = pullback(cotangent.astype(jnp.float32).reshape(seq_count, LEN, D))
    block_out = output.astype(jnp.bfloat16).reshape(MB, N_DP * LEN, D)
    input_grad = grads[0].reshape(MB, N_DP * LEN, D)
    return (block_out, input_grad, grads[1], grads[2], grads[3], grads[4], grads[5], grads[6], grads[7], grads[8], grads[9], grads[10], grads[11])
```

```python
import math

import jax
import jax.numpy as jnp
from jax import lax
from jax.sharding import PartitionSpec as P

D = 2048
HD = 64


NORM_EPS = 1e-05
ROPE_BASE = 1000000.0
MASKED = -1e30


def matmul(left_mat, right_mat):
    return jnp.dot(left_mat, right_mat, preferred_element_type=jnp.float32)


def matmul_tn(left_mat, right_mat):
    return lax.dot_general(
        left_mat, right_mat, (((0,), (0,)), ((), ())), preferred_element_type=jnp.float32
    )


def matmul_nt(left_mat, right_mat):
    return lax.dot_general(
        left_mat, right_mat, (((1,), (1,)), ((), ())), preferred_element_type=jnp.float32
    )


def norm_forward(values, gain_vec):
    scale_rows = lax.rsqrt(jnp.mean(values * values, axis=-1, keepdims=True) + NORM_EPS)
    unit_rows = values * scale_rows
    return (unit_rows * gain_vec, unit_rows, scale_rows)


def norm_backward(grad_rows, unit_rows, scale_rows, gain_vec):
    scaled = grad_rows * gain_vec
    return scale_rows * (scaled - unit_rows * jnp.mean(scaled * unit_rows, axis=-1, keepdims=True))


def rope_tables(position, head_width):
    half_width = head_width // 2
    frequency = ROPE_BASE ** (-2.0 * jnp.arange(half_width, dtype=jnp.float32) / head_width)
    angles = position.astype(jnp.float32)[:, None, None] * frequency[None, None, :]
    return (jnp.cos(angles), jnp.sin(angles))


def rotate(values, cos_table, sin_table):
    half_width = values.shape[-1] // 2
    former = values[..., :half_width]
    latter = values[..., half_width:]
    return jnp.concatenate(
        [former * cos_table - latter * sin_table, latter * cos_table + former * sin_table], axis=-1
    )


def rotate_back(grad_rows, cos_table, sin_table):
    half_width = grad_rows.shape[-1] // 2
    former = grad_rows[..., :half_width]
    latter = grad_rows[..., half_width:]
    return jnp.concatenate(
        [former * cos_table + latter * sin_table, latter * cos_table - former * sin_table], axis=-1
    )


def ring_hop(values):
    count = lax.axis_size("tp")
    return lax.ppermute(values, "tp", [(i, (i + 1) % count) for i in range(count)])


def ring_gather(own):
    chunks = [own]
    for _ in range(lax.axis_size("tp") - 1):
        chunks.append(ring_hop(chunks[-1]))
    return chunks


def ring_sum(term):
    count = lax.axis_size("tp")
    total = term(1).astype(jnp.bfloat16)
    for place in range(2, count):
        total = (ring_hop(total).astype(jnp.float32) + term(place)).astype(jnp.bfloat16)
    return ring_hop(total).astype(jnp.float32) + term(0)


def ctx_swap(values, mask):
    count = lax.axis_size("ctx")
    return lax.ppermute(values, "ctx", [(i, i ^ mask) for i in range(count)])


def ctx_masks():
    masks = [0]
    bit = lax.axis_size("ctx") // 2
    while bit:
        masks = masks + [mask ^ bit for mask in masks]
        bit //= 2
    return masks


def ctx_gather(own):
    blocks = [own]
    bit = lax.axis_size("ctx") // 2
    while bit:
        blocks = blocks + [ctx_swap(block, bit) for block in blocks]
        bit //= 2
    return blocks


def ctx_sum(blocks):
    bit = 1
    while len(blocks) > 1:
        half = len(blocks) // 2
        blocks = [
            blocks[i] + ctx_swap(blocks[half + i].astype(jnp.bfloat16), bit).astype(jnp.float32)
            for i in range(half)
        ]
        bit *= 2
    return blocks[0]


def gather_weight(shard):
    return lax.all_gather(shard, ("dp", "ctx"), axis=0, tiled=True)


def scatter_grad(grad):
    return lax.psum_scatter(
        grad.astype(jnp.bfloat16), ("dp", "ctx"), scatter_dimension=0, tiled=True
    ).astype(jnp.float32)


def per_device(
    block_in,
    segments,
    positions,
    attention_gain,
    query_weight,
    key_weight,
    value_weight,
    query_gain,
    key_gain,
    output_weight,
    hidden_gain,
    gate_weight,
    up_weight,
    down_weight,
    cotangent,
):
    tp_count = lax.axis_size("tp")
    tp_index = lax.axis_index("tp")
    ctx_index = lax.axis_index("ctx")
    batch, own_rows, width = block_in.shape
    rows = batch * own_rows
    ctx_rows = own_rows * tp_count
    places = range(tp_count)
    q_cols = query_weight.shape[1]
    k_cols = key_weight.shape[1]
    q_heads = q_cols // HD
    k_heads = k_cols // HD
    group = q_heads // k_heads
    query_gain_f = query_gain.astype(jnp.float32)
    key_gain_f = key_gain.astype(jnp.float32)
    inv_root = 1.0 / math.sqrt(HD)

    gains = lax.all_gather(
        jnp.stack([attention_gain, hidden_gain]), ("dp", "ctx"), axis=1, tiled=True
    ).astype(jnp.float32)
    gain_attention, gain_hidden = gains[0], gains[1]
    full_qkv = gather_weight(jnp.concatenate([query_weight, key_weight, value_weight], axis=1))
    full_out_t = gather_weight(output_weight.T)
    full_gate = gather_weight(gate_weight)
    full_up = gather_weight(up_weight)
    full_down_t = gather_weight(down_weight.T)

    def chunk_start(place):
        owner = lax.rem(tp_index - place + tp_count, tp_count)
        return owner * own_rows

    def own_part(table, start):
        return lax.dynamic_slice_in_dim(table, start, own_rows, 1)

    tokens = block_in.reshape(rows, width).astype(jnp.float32)
    normed, unit_attention, scale_attention = norm_forward(tokens, gain_attention)
    normed_rows = ring_gather(normed.astype(jnp.bfloat16))

    query_rot, key_value, saved = [], [], []
    for place in places:
        raw = matmul(normed_rows[place], full_qkv)
        position = own_part(positions, ctx_index * ctx_rows + chunk_start(place)).reshape(-1)
        cos_table, sin_table = rope_tables(position, HD)
        query_raw = raw[:, :q_cols].reshape(rows, q_heads, HD)
        key_raw = raw[:, q_cols : q_cols + k_cols].reshape(rows, k_heads, HD)
        query_normed, query_unit, query_scale = norm_forward(query_raw, query_gain_f)
        key_normed, key_unit, key_scale = norm_forward(key_raw, key_gain_f)
        query_rot.append(rotate(query_normed, cos_table, sin_table).astype(jnp.bfloat16))
        key_rot = rotate(key_normed, cos_table, sin_table).astype(jnp.bfloat16)
        value_low = raw[:, q_cols + k_cols :].astype(jnp.bfloat16)
        key_value.append(jnp.stack([key_rot.reshape(rows, k_cols), value_low]))
        saved.append((query_unit, query_scale, key_unit, key_scale, cos_table, sin_table))

    blocks = ctx_gather(jnp.stack(key_value))
    masks = ctx_masks()
    kv = jnp.stack(blocks).reshape(len(masks), tp_count, 2, batch, own_rows, k_heads, HD)
    kv = kv.transpose(2, 3, 5, 0, 1, 4, 6).reshape(2, batch, k_heads, -1, HD)
    key_heads, value_heads = kv[0], kv[1]

    def to_heads(chunks):
        stacked = jnp.stack(chunks).reshape(tp_count, batch, own_rows, k_heads, group, HD)
        return stacked.transpose(1, 3, 4, 0, 2, 5).reshape(batch, k_heads, -1, HD)

    def from_heads(heads):
        split = heads.reshape(batch, k_heads, group, tp_count, own_rows, HD)
        split = split.transpose(3, 0, 4, 1, 2, 5).reshape(tp_count, rows, q_cols)
        return [split[place] for place in places]

    query_heads = to_heads([q.reshape(rows, q_cols) for q in query_rot])
    place_q, segment_q, place_k, segment_k = [], [], [], []
    iota = jnp.arange(own_rows, dtype=jnp.int32)
    for place in places:
        start = ctx_index * ctx_rows + chunk_start(place)
        place_q.append(start + iota)
        segment_q.append(own_part(segments, start))
    for mask in masks:
        for place in places:
            start = jnp.bitwise_xor(ctx_index, mask) * ctx_rows + chunk_start(place)
            place_k.append(start + iota)
            segment_k.append(own_part(segments, start))
    place_q = jnp.concatenate(place_q)
    place_k = jnp.concatenate(place_k)
    segment_q = jnp.concatenate(segment_q, axis=1)
    segment_k = jnp.concatenate(segment_k, axis=1)
    allowed = (segment_q[:, :, None] == segment_k[:, None, :]) & (
        place_q[:, None] >= place_k[None, :]
    )

    def score():
        scores = (
            jnp.einsum("bnqd,bnkd->bnqk", query_heads, key_heads, preferred_element_type=jnp.float32)
            * inv_root
        )
        scores = scores.reshape(batch, k_heads, group, ctx_rows, -1)
        return jnp.where(allowed[:, None, None], scores, MASKED)

    scores = score()
    row_top = jnp.max(scores, axis=-1, keepdims=True)
    exp_scores = jnp.exp(scores - row_top)
    row_total = jnp.sum(exp_scores, axis=-1, keepdims=True)
    probability = exp_scores / row_total
    prob_low = probability.astype(jnp.bfloat16).reshape(batch, k_heads, group * ctx_rows, -1)
    attended = jnp.einsum(
        "bnqk,bnkd->bnqd", prob_low, value_heads, preferred_element_type=jnp.float32
    )
    attended_rows = from_heads(attended.astype(jnp.bfloat16))

    mixed_in = ring_sum(lambda place: matmul_nt(attended_rows[place], full_out_t))
    hidden = tokens + mixed_in
    hidden_normed, unit_hidden, scale_hidden = norm_forward(hidden, gain_hidden)
    hidden_rows = ring_gather(hidden_normed.astype(jnp.bfloat16))
    grad_own = cotangent.reshape(rows, width)
    grad_rows = ring_gather(grad_own)

    activation, grad_gate_low, grad_up_low = [], [], []
    for place in places:
        gate_proj = matmul(hidden_rows[place], full_gate)
        up_proj = matmul(hidden_rows[place], full_up)
        sigmoid_gate = jax.nn.sigmoid(gate_proj)
        silu_gate = gate_proj * sigmoid_gate
        activation.append((silu_gate * up_proj).astype(jnp.bfloat16))
        grad_act = matmul(grad_rows[place], full_down_t)
        grad_gate_low.append(
            (
                grad_act * up_proj * sigmoid_gate * (1.0 + gate_proj * (1.0 - sigmoid_gate))
            ).astype(jnp.bfloat16)
        )
        grad_up_low.append((grad_act * silu_gate).astype(jnp.bfloat16))

    grad_hidden_normed = ring_sum(
        lambda place: matmul_nt(grad_gate_low[place], full_gate)
        + matmul_nt(grad_up_low[place], full_up)
    )
    feed_out = ring_sum(lambda place: matmul_nt(activation[place], full_down_t))
    block_out = (hidden + feed_out).astype(jnp.bfloat16).reshape(block_in.shape)

    all_grad = jnp.concatenate(grad_rows)
    all_hidden = jnp.concatenate(hidden_rows)
    down_grad = scatter_grad(matmul_tn(all_grad, jnp.concatenate(activation))).T
    gate_grad = scatter_grad(matmul_tn(all_hidden, jnp.concatenate(grad_gate_low)))
    up_grad = scatter_grad(matmul_tn(all_hidden, jnp.concatenate(grad_up_low)))

    hidden_gain_sum = jnp.sum(grad_hidden_normed * unit_hidden, axis=0)
    grad_hidden = grad_own.astype(jnp.float32) + norm_backward(
        grad_hidden_normed, unit_hidden, scale_hidden, gain_hidden
    )
    branch_rows = ring_gather(grad_hidden.astype(jnp.bfloat16))
    grad_att = to_heads([matmul(branch, full_out_t).astype(jnp.bfloat16) for branch in branch_rows])
    output_grad = scatter_grad(
        matmul_tn(jnp.concatenate(branch_rows), jnp.concatenate(attended_rows))
    ).T

    grad_prob = jnp.einsum(
        "bnqd,bnkd->bnqk", grad_att, value_heads, preferred_element_type=jnp.float32
    ).reshape(probability.shape)
    row_delta = jnp.sum(probability * grad_prob, axis=-1, keepdims=True)
    grad_scores = (
        (probability * (grad_prob - row_delta))
        .astype(jnp.bfloat16)
        .reshape(batch, k_heads, group * ctx_rows, -1)
    )
    grad_query = from_heads(
        jnp.einsum("bnqk,bnkd->bnqd", grad_scores, key_heads, preferred_element_type=jnp.float32)
        * inv_root
    )
    grad_key = (
        jnp.einsum("bnqk,bnqd->bnkd", grad_scores, query_heads, preferred_element_type=jnp.float32)
        * inv_root
    )
    grad_value = jnp.einsum(
        "bnqk,bnqd->bnkd", prob_low, grad_att, preferred_element_type=jnp.float32
    )
    grad_kv = jnp.stack([grad_key, grad_value]).reshape(
        2, batch, k_heads, len(masks), tp_count, own_rows, HD
    )
    grad_kv = grad_kv.transpose(3, 4, 0, 1, 5, 2, 6).reshape(len(masks), tp_count, 2, rows, k_cols)
    own_kv = ctx_sum([grad_kv[i] for i in range(len(masks))])

    query_gain_sum = jnp.zeros((HD,), jnp.float32)
    key_gain_sum = jnp.zeros((HD,), jnp.float32)
    grad_qkv = []
    for place in places:
        query_unit, query_scale, key_unit, key_scale, cos_table, sin_table = saved[place]
        grad_query_rot = rotate_back(grad_query[place].reshape(rows, -1, HD), cos_table, sin_table)
        query_gain_sum = query_gain_sum + jnp.sum(grad_query_rot * query_unit, axis=(0, 1))
        grad_key_rot = rotate_back(own_kv[place, 0].reshape(rows, -1, HD), cos_table, sin_table)
        key_gain_sum = key_gain_sum + jnp.sum(grad_key_rot * key_unit, axis=(0, 1))
        grad_query_raw = norm_backward(grad_query_rot, query_unit, query_scale, query_gain_f)
        grad_key_raw = norm_backward(grad_key_rot, key_unit, key_scale, key_gain_f)
        grad_qkv.append(
            jnp.concatenate(
                [
                    grad_query_raw.reshape(rows, -1).astype(jnp.bfloat16),
                    grad_key_raw.reshape(rows, -1).astype(jnp.bfloat16),
                    own_kv[place, 1].astype(jnp.bfloat16),
                ],
                axis=1,
            )
        )
    grad_normed = ring_sum(lambda place: matmul_nt(grad_qkv[place], full_qkv))
    qkv_grad = scatter_grad(matmul_tn(jnp.concatenate(normed_rows), jnp.concatenate(grad_qkv)))
    attention_gain_sum = jnp.sum(grad_normed * unit_attention, axis=0)
    input_grad = grad_hidden + norm_backward(
        grad_normed, unit_attention, scale_attention, gain_attention
    )

    gain_totals = lax.psum(
        (attention_gain_sum, hidden_gain_sum, query_gain_sum, key_gain_sum), ("dp", "ctx", "tp")
    )
    shard_width = attention_gain.shape[0]
    shard_start = (lax.axis_index("dp") * lax.axis_size("ctx") + ctx_index) * shard_width
    return (
        block_out,
        input_grad.reshape(block_in.shape),
        lax.dynamic_slice_in_dim(gain_totals[0], shard_start, shard_width, 0),
        qkv_grad[:, :q_cols],
        qkv_grad[:, q_cols : q_cols + k_cols],
        qkv_grad[:, q_cols + k_cols :],
        gain_totals[2],
        gain_totals[3],
        output_grad,
        lax.dynamic_slice_in_dim(gain_totals[1], shard_start, shard_width, 0),
        gate_grad,
        up_grad,
        down_grad,
    )


def solution(mesh):
    in_specs = (
        P(None, ("dp", "ctx", "tp"), None),
        P(None, "dp"),
        P(None, "dp"),
        P(("dp", "ctx")),
        P(("dp", "ctx"), "tp"),
        P(("dp", "ctx"), "tp"),
        P(("dp", "ctx"), "tp"),
        P(),
        P(),
        P("tp", ("dp", "ctx")),
        P(("dp", "ctx")),
        P(("dp", "ctx"), "tp"),
        P(("dp", "ctx"), "tp"),
        P("tp", ("dp", "ctx")),
        P(None, ("dp", "ctx", "tp"), None),
    )
    out_specs = (
        P(None, ("dp", "ctx", "tp"), None),
        P(None, ("dp", "ctx", "tp"), None),
        P(("dp", "ctx")),
        P(("dp", "ctx"), "tp"),
        P(("dp", "ctx"), "tp"),
        P(("dp", "ctx"), "tp"),
        P(),
        P(),
        P("tp", ("dp", "ctx")),
        P(("dp", "ctx")),
        P(("dp", "ctx"), "tp"),
        P(("dp", "ctx"), "tp"),
        P("tp", ("dp", "ctx")),
    )
    return jax.shard_map(
        per_device, mesh=mesh, in_specs=in_specs, out_specs=out_specs, check_vma=False
    )
```

```python
import functools
import math

import jax
import jax.numpy as jnp
from jax import lax
from jax.experimental import pallas as pl
from jax.experimental.pallas import tpu as pltpu
from jax.sharding import PartitionSpec as P

D = 2048
HD = 64


NORM_EPS = 1e-05
ROPE_BASE = 1000000.0
MASKED = -1e30


def matmul(left_mat, right_mat):
    return jnp.dot(left_mat, right_mat, preferred_element_type=jnp.float32)


def matmul_tn(left_mat, right_mat):
    return lax.dot_general(
        left_mat, right_mat, (((0,), (0,)), ((), ())), preferred_element_type=jnp.float32
    )


def matmul_nt(left_mat, right_mat):
    return lax.dot_general(
        left_mat, right_mat, (((1,), (1,)), ((), ())), preferred_element_type=jnp.float32
    )


def norm_forward(values, gain_vec):
    scale_rows = lax.rsqrt(jnp.mean(values * values, axis=-1, keepdims=True) + NORM_EPS)
    unit_rows = values * scale_rows
    return (unit_rows * gain_vec, unit_rows, scale_rows)


def norm_backward(grad_rows, unit_rows, scale_rows, gain_vec):
    scaled = grad_rows * gain_vec
    return scale_rows * (scaled - unit_rows * jnp.mean(scaled * unit_rows, axis=-1, keepdims=True))


def ring_hop(values):
    count = lax.axis_size("tp")
    return lax.ppermute(values, "tp", [(i, (i + 1) % count) for i in range(count)])


def ctx_swap(values, mask):
    count = lax.axis_size("ctx")
    return lax.ppermute(values, "ctx", [(i, i ^ mask) for i in range(count)])


def ctx_masks():
    masks = [0]
    bit = lax.axis_size("ctx") // 2
    while bit:
        masks = masks + [mask ^ bit for mask in masks]
        bit //= 2
    return masks


def ctx_gather(own):
    blocks = [own]
    bit = lax.axis_size("ctx") // 2
    while bit:
        blocks = blocks + [ctx_swap(block, bit) for block in blocks]
        bit //= 2
    return blocks


def gather_weight(shard):
    return lax.all_gather(shard, ("dp", "ctx"), axis=0, tiled=True)


def scatter_grad(grad):
    return lax.psum_scatter(
        grad.astype(jnp.bfloat16), ("dp", "ctx"), scatter_dimension=0, tiled=True
    ).astype(jnp.float32)


def all_sum(values, axes):
    for axis in axes:
        count = lax.axis_size(axis)
        bit = 1
        while bit < count:
            values = values + lax.ppermute(values, axis, [(i, i ^ bit) for i in range(count)])
            bit *= 2
    return values


def together(*values):
    return lax.optimization_barrier(values)


def lane_iota(shape):
    return lax.broadcasted_iota(jnp.int32, shape, 1)


def head_means(values):
    width = values.shape[1]
    row = lax.broadcasted_iota(jnp.int32, (width, width), 0) // HD
    col = lax.broadcasted_iota(jnp.int32, (width, width), 1) // HD
    pick = jnp.where(row == col, 1.0 / HD, 0.0).astype(jnp.float32)
    return jnp.dot(
        values, pick, precision=lax.Precision.HIGHEST, preferred_element_type=jnp.float32
    )


def half_swap(values):
    width, half = values.shape[1], HD // 2
    first = lax.rem(lane_iota(values.shape), HD) < half
    return jnp.where(
        first, pltpu.roll(values, width - half, 1), pltpu.roll(values, half, 1)
    )


def other_head(values):
    return pltpu.roll(values, HD, 1)


def twice(values, head):
    wide = values.astype(jnp.float32)
    low = lane_iota(wide.shape) < HD
    other = other_head(wide)
    both = jnp.where(low, wide, other) if head == 0 else jnp.where(low, other, wide)
    return both.astype(values.dtype)


def apart(values):
    wide = values.astype(jnp.float32)
    low = lane_iota(wide.shape) < HD
    zero = jnp.zeros_like(wide)
    return jnp.concatenate(
        [jnp.where(low, wide, zero), jnp.where(low, zero, wide)], axis=0
    ).astype(values.dtype)


def heads_kernel(raw_ref, cos_ref, sin_ref, q_gain_ref, k_gain_ref, q_ref, kv_ref):
    pair = 2 * HD
    q_cols = q_ref.shape[1]
    k_cols = kv_ref.shape[1] // 2
    cos, sin = cos_ref[...], sin_ref[...]
    for first in range(0, q_cols + k_cols, pair):
        values = raw_ref[:, first : first + pair]
        gain = q_gain_ref[...] if first < q_cols else k_gain_ref[...]
        normed = values * lax.rsqrt(head_means(values * values) + NORM_EPS) * gain
        turned = (normed * cos + half_swap(normed) * sin).astype(jnp.bfloat16)
        if first < q_cols:
            q_ref[:, first : first + pair] = turned
        else:
            kv_ref[:, first - q_cols : first - q_cols + pair] = turned
    kv_ref[:, k_cols:] = raw_ref[:, q_cols + k_cols :].astype(jnp.bfloat16)


def make_heads(raw, cos_wide, sin_wide, q_gain, k_gain, q_cols, k_cols):
    rows = raw.shape[0]
    return pl.pallas_call(
        heads_kernel,
        out_shape=(
            jax.ShapeDtypeStruct((rows, q_cols), jnp.bfloat16),
            jax.ShapeDtypeStruct((rows, 2 * k_cols), jnp.bfloat16),
        ),
        cost_estimate=pl.CostEstimate(
            flops=rows * raw.shape[1] * 400, bytes_accessed=rows * raw.shape[1] * 7, transcendentals=0
        ),
        name="make_heads",
    )(raw, cos_wide, sin_wide, q_gain, k_gain)


def turn_back(grad, values, gain, cos, sin):
    turned = grad * cos - half_swap(grad) * sin
    scale = lax.rsqrt(head_means(values * values) + NORM_EPS)
    unit = values * scale
    scaled = turned * gain
    return scale * (scaled - unit * head_means(scaled * unit)), turned * unit


def fill_bias(starts_ref, low_ref, high_ref, bias_ref, piece):
    low, high = low_ref[0], high_ref[0]
    for i in range(bias_ref.shape[0] // piece):
        place = starts_ref[i] + lax.broadcasted_iota(jnp.int32, (piece, low.shape[1]), 0)
        linked = (place >= low) & (place <= high)
        bias_ref[i * piece : (i + 1) * piece, :] = jnp.where(linked, 0.0, MASKED)


def attend_kernel(places, blocks, block_keys, skip, *refs):
    starts_ref, low_ref, high_ref = refs[:3]
    q_refs = refs[3 : 3 + places]
    kv_refs = refs[3 + places : 3 + places + blocks]
    refs = refs[3 + places + blocks + skip :]
    out_refs = refs[:places]
    total_ref, bias_ref, key_ref, value_ref = refs[places:]
    pair = 2 * HD
    piece, q_cols = q_refs[0].shape
    rows = places * piece
    k_cols = kv_refs[0].shape[2] // 2
    k_heads = k_cols // HD
    group = q_cols // k_cols
    scale = math.log2(math.e) / math.sqrt(HD)
    fill_bias(starts_ref, low_ref, high_ref, bias_ref, piece)
    for block in range(blocks):
        for head in range(k_heads):
            cols = slice(head // 2 * pair, head // 2 * pair + pair)
            vcols = slice(k_cols + head // 2 * pair, k_cols + head // 2 * pair + pair)
            where = slice(block * block_keys, (block + 1) * block_keys)
            keys = kv_refs[block][:, :, cols].reshape(block_keys, pair)
            key_ref[head, where, :] = twice(keys, head % 2)
            if head % 2 == 0:
                values = kv_refs[block][:, :, vcols].reshape(block_keys, pair)
                value_ref[head // 2, :, where] = values.astype(jnp.float32).T.astype(jnp.bfloat16)
    for first in range(0, q_cols, pair):
        head = first // HD // group
        queries = apart(jnp.concatenate([q_ref[:, first : first + pair] for q_ref in q_refs], axis=0))

        def step(block, carry):
            mixed, total = carry
            where = pl.ds(pl.multiple_of(block * block_keys, block_keys), block_keys)
            scores = matmul_nt(key_ref[head, where, :], queries)
            bias = bias_ref[where, :]
            weight = jnp.exp2(scores * scale + jnp.concatenate([bias, bias], axis=1))
            total = total + jnp.sum(weight, axis=0, keepdims=True)
            values = value_ref[head // 2, head % 2 * HD : (head % 2 + 1) * HD, where]
            return mixed + matmul(values, weight.astype(jnp.bfloat16)), total

        mixed, total = lax.fori_loop(
            0,
            blocks,
            step,
            (jnp.zeros((HD, 2 * rows), jnp.float32), jnp.zeros((1, 2 * rows), jnp.float32)),
        )
        mixed = mixed / total
        out = jnp.concatenate([mixed[:, :rows], mixed[:, rows:]], axis=0).T.astype(jnp.bfloat16)
        for place in range(places):
            out_refs[place][:, first : first + pair] = out[place * piece : (place + 1) * piece]
        total_ref[0, first // pair, :] = jnp.log2(total)[0]


def attend(starts, low, high, q_chunks, kv_blocks, batch, part, parts, before):
    places, blocks = len(q_chunks), len(kv_blocks)
    count = batch // parts
    base = part * count
    rows, q_cols = q_chunks[0].shape
    piece = rows // batch
    kv_cols = kv_blocks[0].shape[2]
    k_cols = kv_cols // 2
    keys = blocks * places * piece
    q_rows = places * piece
    pairs = q_cols // (2 * HD)
    q_spec = pl.BlockSpec((piece, q_cols), lambda b: (base + b, 0))
    kv_spec = pl.BlockSpec((places, piece, kv_cols), lambda b: (0, base + b, 0))
    line_spec = pl.BlockSpec((1, 1, q_rows), lambda b: (base + b, 0, 0))
    work = count * q_cols // HD * q_rows * keys
    results = pl.pallas_call(
        functools.partial(attend_kernel, places, blocks, places * piece, len(before)),
        grid=(count,),
        out_shape=tuple(
            [jax.ShapeDtypeStruct((rows, q_cols), jnp.bfloat16)] * places
            + [jax.ShapeDtypeStruct((batch, pairs, 2 * q_rows), jnp.float32)]
        ),
        in_specs=[
            pl.BlockSpec(memory_space=pltpu.SMEM),
            line_spec,
            pl.BlockSpec((1, 1, q_rows), lambda b: (0, 0, 0)),
        ]
        + [q_spec] * places
        + [kv_spec] * blocks
        + [pl.BlockSpec(memory_space=pl.ANY)] * len(before),
        out_specs=tuple(
            [q_spec] * places + [pl.BlockSpec((1, pairs, 2 * q_rows), lambda b: (base + b, 0, 0))]
        ),
        input_output_aliases={3 + places + blocks + i: i for i in range(len(before))},
        scratch_shapes=[
            pltpu.VMEM((keys, q_rows), jnp.float32),
            pltpu.VMEM((k_cols // HD, keys, 2 * HD), jnp.bfloat16),
            pltpu.VMEM((k_cols // HD // 2, 2 * HD, keys), jnp.bfloat16),
        ],
        cost_estimate=pl.CostEstimate(
            flops=work * 4 * HD * 4, bytes_accessed=count * q_rows * q_cols * 8, transcendentals=work
        ),
        name="attend",
    )(starts, low, high, *q_chunks, *kv_blocks, *before)
    return list(results)


def attend_back_kernel(places, blocks, block_keys, skip, *refs):
    starts_ref, low_ref, high_ref, total_ref, cos_ref, sin_ref, gain_ref = refs[:7]
    refs = refs[7:]
    q_refs, refs = refs[:places], refs[places:]
    raw_refs, refs = refs[:places], refs[places:]
    grad_refs, refs = refs[:places], refs[places:]
    kv_refs, refs = refs[:blocks], refs[blocks + skip :]
    dq_refs, refs = refs[:places], refs[places:]
    dkv_refs, refs = refs[:blocks], refs[blocks:]
    gain_sum_ref, bias_ref, key_ref, turned_ref, value_ref, prob_ref, dprob_ref, dkey_ref, dvalue_ref = refs
    pair = 2 * HD
    piece, q_cols = q_refs[0].shape
    rows = places * piece
    k_cols = kv_refs[0].shape[2] // 2
    k_heads = k_cols // HD
    group = q_cols // k_cols
    inv_root = 1.0 / math.sqrt(HD)
    scale = math.log2(math.e) * inv_root
    fill_bias(starts_ref, low_ref, high_ref, bias_ref, piece)

    @pl.when(pl.program_id(0) == 0)
    def _():
        gain_sum_ref[...] = jnp.zeros_like(gain_sum_ref)

    for block in range(blocks):
        for head in range(k_heads):
            cols = slice(head // 2 * pair, head // 2 * pair + pair)
            vcols = slice(k_cols + head // 2 * pair, k_cols + head // 2 * pair + pair)
            where = slice(block * block_keys, (block + 1) * block_keys)
            keys = kv_refs[block][:, :, cols].reshape(block_keys, pair)
            values = kv_refs[block][:, :, vcols].reshape(block_keys, pair)
            key_ref[head, where, :] = twice(keys, head % 2)
            value_ref[head, where, :] = twice(values, head % 2)
            if head % 2 == 0:
                turned_ref[head // 2, :, where] = keys.astype(jnp.float32).T.astype(jnp.bfloat16)
    for first in range(0, q_cols, pair):
        head = first // HD // group
        fresh = first % (group * HD) == 0
        queries = apart(jnp.concatenate([q_ref[:, first : first + pair] for q_ref in q_refs], axis=0))
        grads = apart(jnp.concatenate([g_ref[:, first : first + pair] for g_ref in grad_refs], axis=0))
        total = total_ref[0, first // pair : first // pair + 1, :]

        def look(block, delta):
            where = pl.ds(pl.multiple_of(block * block_keys, block_keys), block_keys)
            scores = matmul_nt(key_ref[head, where, :], queries)
            bias = bias_ref[where, :]
            prob = jnp.exp2(scores * scale + jnp.concatenate([bias, bias], axis=1) - total)
            dprob = matmul_nt(value_ref[head, where, :], grads)
            prob_ref[where, :] = prob
            dprob_ref[where, :] = dprob
            return delta + jnp.sum(prob * dprob, axis=0, keepdims=True)

        delta = lax.fori_loop(0, blocks, look, jnp.zeros((1, 2 * rows), jnp.float32))

        def step(block, dquery):
            where = pl.ds(pl.multiple_of(block * block_keys, block_keys), block_keys)
            prob = prob_ref[where, :]
            dscore = (prob * (dprob_ref[where, :] - delta)).astype(jnp.bfloat16)
            dvalue = matmul(prob.astype(jnp.bfloat16), grads)
            dkey = matmul(dscore, queries)
            if fresh:
                dvalue_ref[head, where, :] = dvalue
                dkey_ref[head, where, :] = dkey
            else:
                dvalue_ref[head, where, :] += dvalue
                dkey_ref[head, where, :] += dkey
            keys = turned_ref[head // 2, head % 2 * HD : (head % 2 + 1) * HD, where]
            return dquery + matmul(keys, dscore)

        dquery = lax.fori_loop(0, blocks, step, jnp.zeros((HD, 2 * rows), jnp.float32)) * inv_root
        dquery = jnp.concatenate([dquery[:, :rows], dquery[:, rows:]], axis=0).T
        raw = jnp.concatenate([raw_ref[:, first : first + pair] for raw_ref in raw_refs], axis=0)
        dq, addend = turn_back(
            dquery, raw, gain_ref[...], cos_ref[...].reshape(rows, pair), sin_ref[...].reshape(rows, pair)
        )
        gain_sum_ref[...] += jnp.sum(addend.reshape(-1, 8, pair), axis=0)
        for place in range(places):
            dq_refs[place][:, first : first + pair] = dq[place * piece : (place + 1) * piece].astype(
                jnp.bfloat16
            )
    low = lane_iota((block_keys, pair)) < HD
    for block in range(blocks):
        where = slice(block * block_keys, (block + 1) * block_keys)
        for first in range(0, k_heads, 2):
            for shift, ref, factor in ((0, dkey_ref, inv_root), (k_cols, dvalue_ref, 1.0)):
                one, two = ref[first, where, :], ref[first + 1, where, :]
                sums = jnp.where(low, one + other_head(one), two + other_head(two)) * factor
                cols = slice(shift + first // 2 * pair, shift + first // 2 * pair + pair)
                dkv_refs[block][:, :, cols] = sums.reshape(places, piece, pair).astype(
                    dkv_refs[block].dtype
                )


def attend_back(
    starts,
    low,
    high,
    totals,
    cos_wide,
    sin_wide,
    q_gain,
    q_chunks,
    raw_chunks,
    grad_chunks,
    kv_blocks,
    kinds,
    batch,
    part,
    parts,
    before,
):
    places, blocks = len(q_chunks), len(kv_blocks)
    count = batch // parts
    base = part * count
    rows, q_cols = q_chunks[0].shape
    piece = rows // batch
    kv_cols = kv_blocks[0].shape[2]
    k_cols = kv_cols // 2
    keys = blocks * places * piece
    q_rows = places * piece
    pairs = q_cols // (2 * HD)
    k_heads = k_cols // HD
    q_spec = pl.BlockSpec((piece, q_cols), lambda b: (base + b, 0))
    kv_spec = pl.BlockSpec((places, piece, kv_cols), lambda b: (0, base + b, 0))
    line_spec = pl.BlockSpec((1, 1, q_rows), lambda b: (base + b, 0, 0))
    turn_spec = pl.BlockSpec((places, piece, 2 * HD), lambda b: (0, base + b, 0))
    work = count * q_cols // HD * q_rows * keys
    results = pl.pallas_call(
        functools.partial(attend_back_kernel, places, blocks, places * piece, len(before)),
        grid=(count,),
        out_shape=tuple(
            [jax.ShapeDtypeStruct((rows, q_cols), jnp.bfloat16)] * places
            + [jax.ShapeDtypeStruct((places, rows, kv_cols), kind) for kind in kinds]
            + [jax.ShapeDtypeStruct((8, 2 * HD), jnp.float32)]
        ),
        in_specs=[
            pl.BlockSpec(memory_space=pltpu.SMEM),
            line_spec,
            pl.BlockSpec((1, 1, q_rows), lambda b: (0, 0, 0)),
            pl.BlockSpec((1, pairs, 2 * q_rows), lambda b: (base + b, 0, 0)),
            turn_spec,
            turn_spec,
            pl.BlockSpec((1, 2 * HD), lambda b: (0, 0)),
        ]
        + [q_spec] * (3 * places)
        + [kv_spec] * blocks
        + [pl.BlockSpec(memory_space=pl.ANY)] * len(before),
        out_specs=tuple(
            [q_spec] * places + [kv_spec] * blocks + [pl.BlockSpec((8, 2 * HD), lambda b: (0, 0))]
        ),
        input_output_aliases={7 + 3 * places + blocks + i: i for i in range(len(before))},
        scratch_shapes=[
            pltpu.VMEM((keys, q_rows), jnp.float32),
            pltpu.VMEM((k_heads, keys, 2 * HD), jnp.bfloat16),
            pltpu.VMEM((k_heads // 2, 2 * HD, keys), jnp.bfloat16),
            pltpu.VMEM((k_heads, keys, 2 * HD), jnp.bfloat16),
            pltpu.VMEM((keys, 2 * q_rows), jnp.float32),
            pltpu.VMEM((keys, 2 * q_rows), jnp.float32),
            pltpu.VMEM((k_heads, keys, 2 * HD), jnp.float32),
            pltpu.VMEM((k_heads, keys, 2 * HD), jnp.float32),
        ],
        cost_estimate=pl.CostEstimate(
            flops=work * 10 * HD * 4, bytes_accessed=count * q_rows * q_cols * 16, transcendentals=work
        ),
        name="attend_back",
    )(
        starts,
        low,
        high,
        totals,
        cos_wide,
        sin_wide,
        q_gain,
        *q_chunks,
        *raw_chunks,
        *grad_chunks,
        *kv_blocks,
        *before,
    )
    return list(results[:-1]), results[-1]


def keys_back_kernel(own_ref, came_ref, raw_ref, cos_ref, sin_ref, gain_ref, out_ref, gain_sum_ref):
    k_cols = own_ref.shape[2] // 2
    pair = 2 * HD
    addends = jnp.zeros((8, pair), jnp.float32)
    for first in range(0, k_cols, pair):
        cols = slice(first, first + pair)
        grad = own_ref[0, :, cols] + came_ref[0, :, cols].astype(jnp.float32)
        dk, addend = turn_back(grad, raw_ref[:, cols], gain_ref[...], cos_ref[0], sin_ref[0])
        out_ref[:, cols] = dk.astype(jnp.bfloat16)
        addends = addends + jnp.sum(addend.reshape(-1, 8, pair), axis=0)
    rest = slice(k_cols, 2 * k_cols)
    out_ref[:, rest] = (own_ref[0, :, rest] + came_ref[0, :, rest].astype(jnp.float32)).astype(
        jnp.bfloat16
    )
    gain_sum_ref[...] = addends


def keys_back(place, own, came, raw, cos_wide, sin_wide, k_gain, q_cols):
    _, rows, kv_cols = own.shape
    kv_spec = pl.BlockSpec((1, rows, kv_cols), lambda i: (place, 0, 0))
    turn_spec = pl.BlockSpec((1, rows, 2 * HD), lambda i: (place, 0, 0))
    k_cols = kv_cols // 2
    return pl.pallas_call(
        keys_back_kernel,
        grid=(1,),
        out_shape=(
            jax.ShapeDtypeStruct((rows, kv_cols), jnp.bfloat16),
            jax.ShapeDtypeStruct((8, 2 * HD), jnp.float32),
        ),
        in_specs=[
            kv_spec,
            kv_spec,
            pl.BlockSpec((rows, k_cols), lambda i: (0, q_cols // k_cols)),
            turn_spec,
            turn_spec,
            pl.BlockSpec((1, 2 * HD), lambda i: (0, 0)),
        ],
        out_specs=(
            pl.BlockSpec((rows, kv_cols), lambda i: (0, 0)),
            pl.BlockSpec((8, 2 * HD), lambda i: (0, 0)),
        ),
        cost_estimate=pl.CostEstimate(
            flops=rows * kv_cols * 400, bytes_accessed=rows * kv_cols * 10, transcendentals=0
        ),
        name="keys_back",
    )(own, came, raw, cos_wide, sin_wide, k_gain)


def per_device(
    block_in,
    segments,
    positions,
    attention_gain,
    query_weight,
    key_weight,
    value_weight,
    query_gain,
    key_gain,
    output_weight,
    hidden_gain,
    gate_weight,
    up_weight,
    down_weight,
    cotangent,
):
    tp_count = lax.axis_size("tp")
    tp_index = lax.axis_index("tp")
    ctx_index = lax.axis_index("ctx")
    batch, own_rows, width = block_in.shape
    rows = batch * own_rows
    ctx_rows = own_rows * tp_count
    places = range(tp_count)
    order = [*range(1, tp_count), 0]
    masks = ctx_masks()
    q_cols = query_weight.shape[1]
    k_cols = key_weight.shape[1]
    qkv_cols = q_cols + 2 * k_cols
    hidden_cols = gate_weight.shape[1]
    q_gain = jnp.tile(query_gain.astype(jnp.float32), 2)[None]
    k_gain = jnp.tile(key_gain.astype(jnp.float32), 2)[None]

    gains = lax.all_gather(
        jnp.stack([attention_gain, hidden_gain]), ("dp", "ctx"), axis=1, tiled=True
    ).astype(jnp.float32)
    gain_attention, gain_hidden = gains[0], gains[1]
    qkv_weight = jnp.concatenate([query_weight, key_weight, value_weight], axis=1)
    full_first = gather_weight(jnp.concatenate([qkv_weight, output_weight.T], axis=1))
    full_second = gather_weight(jnp.concatenate([gate_weight, up_weight, down_weight.T], axis=1))
    full_qkv, full_out_t = full_first[:, :qkv_cols], full_first[:, qkv_cols:]
    full_gate = full_second[:, :hidden_cols]
    full_up = full_second[:, hidden_cols : 2 * hidden_cols]
    full_down_t = full_second[:, 2 * hidden_cols :]

    def chunk_start(place):
        owner = lax.rem(tp_index - place + tp_count, tp_count)
        return owner * own_rows

    def own_part(table, start):
        return lax.dynamic_slice_in_dim(table, start, own_rows, 1)

    iota = jnp.arange(own_rows, dtype=jnp.int32)
    row_starts = [ctx_index * ctx_rows + chunk_start(place) for place in places]
    low = jnp.concatenate([own_part(segments, start) for start in row_starts], axis=1)[:, None]
    high = jnp.concatenate([start + iota for start in row_starts])[None, None]
    starts = jnp.stack(
        [
            jnp.bitwise_xor(ctx_index, mask) * ctx_rows + chunk_start(place)
            for mask in masks
            for place in places
        ]
    ).astype(jnp.int32)
    position = jnp.stack([own_part(positions, start).reshape(rows) for start in row_starts])
    half = HD // 2
    frequency = ROPE_BASE ** (-2.0 * jnp.arange(half, dtype=jnp.float32) / HD)
    sign = jnp.where(jnp.arange(2 * HD) % HD < half, -1.0, 1.0).astype(jnp.float32)
    angles = position.astype(jnp.float32)[..., None] * jnp.tile(frequency, 4)
    cos_wide, sin_wide = jnp.cos(angles), jnp.sin(angles) * sign

    def project(place):
        values = matmul(normed_rows[place], full_qkv)
        query_rot, kv = make_heads(
            values, cos_wide[place], sin_wide[place], q_gain, k_gain, q_cols, k_cols
        )
        return values, query_rot, kv

    tokens = block_in.reshape(rows, width).astype(jnp.float32)
    normed, unit_attention, scale_attention = norm_forward(tokens, gain_attention)
    normed_rows, heads = [normed.astype(jnp.bfloat16)], []
    for place in range(1, tp_count):
        came = ring_hop(normed_rows[-1])
        if place > 1:
            heads.append(project(place - 2))
            came, heads[-1] = together(came, heads[-1])
        normed_rows.append(came)

    grad_own, normed_rows[-1] = together(cotangent.reshape(rows, width), normed_rows[-1])
    came = ring_hop(grad_own)
    heads.append(project(tp_count - 2))
    heads.append(project(tp_count - 1))
    raw, queries, key_value = ([h[i] for h in heads] for i in range(3))
    blocks = ctx_gather(jnp.stack(key_value))
    came, blocks = together(came, blocks)
    grad_rows = [grad_own, came]
    attended = []
    parts = tp_count - 2
    for part in range(parts):
        came = ring_hop(grad_rows[-1])
        attended = attend(starts, low, high, queries, blocks, batch, part, parts, attended)
        came, attended = together(came, attended)
        grad_rows.append(came)
    attended_rows, totals = attended[:tp_count], attended[tp_count]

    def ring_sum(term, extra):
        total = term(order[0]).astype(jnp.bfloat16)
        done = []
        for step, place in enumerate(order[1:]):
            came = ring_hop(total)
            came, addend, work = together(came, term(place), extra(step, done))
            done.append(work)
            total = came.astype(jnp.float32) + addend
            if place:
                total = total.astype(jnp.bfloat16)
        return total, done

    grad_acts = {}

    def mixed_extra(step, done):
        last = step == tp_count - 2
        mine = order[step : step + 2] if last else order[step : step + 1]
        return [matmul(grad_rows[place], full_down_t) for place in mine]

    mixed_in, done = ring_sum(lambda place: matmul_nt(attended_rows[place], full_out_t), mixed_extra)
    for place, value in zip(order, [value for work in done for value in work]):
        grad_acts[place] = value
    hidden = tokens + mixed_in
    hidden_normed, unit_hidden, scale_hidden = norm_forward(hidden, gain_hidden)

    def feed(place):
        gate_proj = matmul(hidden_rows[place], full_gate)
        up_proj = matmul(hidden_rows[place], full_up)
        sigmoid_gate = jax.nn.sigmoid(gate_proj)
        silu_gate = gate_proj * sigmoid_gate
        grad_act = grad_acts[place]
        grad_gate = grad_act * up_proj * sigmoid_gate * (1.0 + gate_proj * (1.0 - sigmoid_gate))
        return (
            (silu_gate * up_proj).astype(jnp.bfloat16),
            grad_gate.astype(jnp.bfloat16),
            (grad_act * silu_gate).astype(jnp.bfloat16),
        )

    hidden_rows, fed = [hidden_normed.astype(jnp.bfloat16)], []
    for place in range(1, tp_count):
        came = ring_hop(hidden_rows[-1])
        fed.append(feed(place - 1))
        came, fed[-1] = together(came, fed[-1])
        hidden_rows.append(came)

    def hidden_term(place):
        return matmul_nt(fed[place][1], full_gate) + matmul_nt(fed[place][2], full_up)

    products = {}

    def hidden_sum():
        total = hidden_term(1).astype(jnp.bfloat16)
        came = ring_hop(total)
        last = feed(tp_count - 1)
        came, addend, last = together(came, hidden_term(2), last)
        fed.append(last)
        total = (came.astype(jnp.float32) + addend).astype(jnp.bfloat16)
        for place in order[2:]:
            came = ring_hop(total)
            if place:
                work = matmul_tn(
                    jnp.concatenate(grad_rows), jnp.concatenate([f[0] for f in fed])
                ).astype(jnp.bfloat16)
            else:
                pair = jnp.concatenate([jnp.concatenate([f[1], f[2]], axis=1) for f in fed])
                work = matmul_tn(jnp.concatenate(hidden_rows), pair).astype(jnp.bfloat16)
            came, addend, work = together(came, hidden_term(place), work)
            products[place] = work
            total = came.astype(jnp.float32) + addend
            if place:
                total = total.astype(jnp.bfloat16)
        return total

    grad_hidden_normed = hidden_sum()
    down_shard = lax.psum_scatter(products[3], ("dp", "ctx"), scatter_dimension=0, tiled=True)
    pair_shard = lax.psum_scatter(products[0], ("dp", "ctx"), scatter_dimension=0, tiled=True)

    grad_hidden = grad_own.astype(jnp.float32) + norm_backward(
        grad_hidden_normed, unit_hidden, scale_hidden, gain_hidden
    )
    branch_rows, grad_att = [grad_hidden.astype(jnp.bfloat16)], []
    for place in range(1, tp_count):
        came = ring_hop(branch_rows[-1])
        grad_att.append(matmul(branch_rows[-1], full_out_t).astype(jnp.bfloat16))
        came, grad_att[-1] = together(came, grad_att[-1])
        branch_rows.append(came)
    grad_att.append(matmul(branch_rows[-1], full_out_t).astype(jnp.bfloat16))
    down_shard, grad_att[-1] = together(down_shard, grad_att[-1])

    kinds = [jnp.float32] * (len(masks) // 2) + [jnp.bfloat16] * (len(masks) - len(masks) // 2)
    query_gain_sum = jnp.zeros((8, 2 * HD), jnp.float32)

    def feed_extra(step, done):
        nonlocal query_gain_sum
        if step < 2:
            back, addend = attend_back(
                starts,
                low,
                high,
                totals,
                cos_wide,
                sin_wide,
                q_gain,
                queries,
                raw,
                grad_att,
                blocks,
                kinds,
                batch,
                step,
                2,
                done[-1] if done else [],
            )
            query_gain_sum = query_gain_sum + addend
            return back
        nonlocal pair_shard
        pair_shard, done[-1] = together(pair_shard, done[-1])
        grad_blocks = done[-1][tp_count:]
        bit = 1
        while len(grad_blocks) > 2:
            half_count = len(grad_blocks) // 2
            grad_blocks = [
                grad_blocks[i]
                + ctx_swap(grad_blocks[half_count + i].astype(jnp.bfloat16), bit).astype(jnp.float32)
                for i in range(half_count)
            ]
            bit *= 2
        came = ctx_swap(grad_blocks[1].astype(jnp.bfloat16), bit)
        return [
            keys_back(place, grad_blocks[0], came, raw[place], cos_wide, sin_wide, k_gain, q_cols)
            for place in places
        ]

    activation_1, grad_att[0] = together(fed[1][0], grad_att[0])
    activation = [f[0] for f in fed]
    activation[1] = activation_1
    feed_out, done = ring_sum(lambda place: matmul_nt(activation[place], full_down_t), feed_extra)
    block_out = (hidden + feed_out).astype(jnp.bfloat16).reshape(block_in.shape)
    grad_query = done[1][:tp_count]
    grad_kv = [pair[0] for pair in done[2]]
    key_gain_sum = sum(pair[1] for pair in done[2])
    grad_qkv = [jnp.concatenate([grad_query[i], grad_kv[i]], axis=1) for i in places]

    def last_extra(step, done):
        if step:
            return []
        return [
            jnp.concatenate(
                [
                    matmul_tn(jnp.concatenate(normed_rows), jnp.concatenate(grad_qkv)),
                    matmul_tn(jnp.concatenate(branch_rows), jnp.concatenate(attended_rows)),
                ],
                axis=1,
            ).astype(jnp.bfloat16)
        ]

    grad_normed, done = ring_sum(lambda place: matmul_nt(grad_qkv[place], full_qkv), last_extra)
    last_shard = scatter_grad(done[0][0])
    input_grad = grad_hidden + norm_backward(
        grad_normed, unit_attention, scale_attention, gain_attention
    )
    down_grad = down_shard.astype(jnp.float32).T
    gate_grad = pair_shard[:, :hidden_cols].astype(jnp.float32)
    up_grad = pair_shard[:, hidden_cols:].astype(jnp.float32)
    qkv_grad = last_shard[:, :qkv_cols]
    output_grad = last_shard[:, qkv_cols:].T

    head_sums = jnp.stack([query_gain_sum, key_gain_sum]).sum(axis=1).reshape(2, 2, HD).sum(axis=1)
    head_sums = all_sum(head_sums, ("tp", "ctx", "dp"))
    attention_sum = jnp.sum(qkv_grad * qkv_weight.astype(jnp.float32), axis=1)
    hidden_sums = jnp.sum(
        gate_grad * gate_weight.astype(jnp.float32) + up_grad * up_weight.astype(jnp.float32), axis=1
    )
    attention_gain_grad = all_sum(attention_sum, ("tp",)) / attention_gain.astype(jnp.float32)
    hidden_gain_grad = all_sum(hidden_sums, ("tp",)) / hidden_gain.astype(jnp.float32)
    return (
        block_out,
        input_grad.reshape(block_in.shape),
        attention_gain_grad,
        qkv_grad[:, :q_cols],
        qkv_grad[:, q_cols : q_cols + k_cols],
        qkv_grad[:, q_cols + k_cols :],
        head_sums[0],
        head_sums[1],
        output_grad,
        hidden_gain_grad,
        gate_grad,
        up_grad,
        down_grad,
    )


def solution(mesh):
    in_specs = (
        P(None, ("dp", "ctx", "tp"), None),
        P(None, "dp"),
        P(None, "dp"),
        P(("dp", "ctx")),
        P(("dp", "ctx"), "tp"),
        P(("dp", "ctx"), "tp"),
        P(("dp", "ctx"), "tp"),
        P(),
        P(),
        P("tp", ("dp", "ctx")),
        P(("dp", "ctx")),
        P(("dp", "ctx"), "tp"),
        P(("dp", "ctx"), "tp"),
        P("tp", ("dp", "ctx")),
        P(None, ("dp", "ctx", "tp"), None),
    )
    out_specs = (
        P(None, ("dp", "ctx", "tp"), None),
        P(None, ("dp", "ctx", "tp"), None),
        P(("dp", "ctx")),
        P(("dp", "ctx"), "tp"),
        P(("dp", "ctx"), "tp"),
        P(("dp", "ctx"), "tp"),
        P(),
        P(),
        P("tp", ("dp", "ctx")),
        P(("dp", "ctx")),
        P(("dp", "ctx"), "tp"),
        P(("dp", "ctx"), "tp"),
        P("tp", ("dp", "ctx")),
    )
    return jax.shard_map(
        per_device, mesh=mesh, in_specs=in_specs, out_specs=out_specs, check_vma=False
    )
```

```python
import functools
import math

import jax
import jax.numpy as jnp
from jax import lax
from jax.experimental import pallas as pl
from jax.experimental.pallas import tpu as pltpu
from jax.sharding import Mesh
from jax.sharding import PartitionSpec as P

D = 2048
HD = 64


NORM_EPS = 1e-05
ROPE_BASE = 1000000.0
MASKED = -1e30
CTX = ("ctx_pair", "ctx_place")


def matmul(left_mat, right_mat):
    return jnp.dot(left_mat, right_mat, preferred_element_type=jnp.float32)


def matmul_tn(left_mat, right_mat):
    return lax.dot_general(
        left_mat, right_mat, (((0,), (0,)), ((), ())), preferred_element_type=jnp.float32
    )


def matmul_nt(left_mat, right_mat):
    return lax.dot_general(
        left_mat, right_mat, (((1,), (1,)), ((), ())), preferred_element_type=jnp.float32
    )


def ring_hop(values):
    count = lax.axis_size("tp")
    return lax.ppermute(values, "tp", [(i, (i + 1) % count) for i in range(count)])


def ctx_swap(values, mask):
    count = lax.axis_size(CTX)
    return lax.ppermute(values, CTX, [(i, i ^ mask) for i in range(count)])


def ctx_masks():
    masks = [0]
    bit = lax.axis_size(CTX) // 2
    while bit:
        masks = masks + [mask ^ bit for mask in masks]
        bit //= 2
    return masks


def ctx_gather(own):
    blocks = [own]
    bit = lax.axis_size(CTX) // 2
    while bit:
        blocks = blocks + [ctx_swap(block, bit) for block in blocks]
        bit //= 2
    return blocks


def gather_weight(shard):
    return lax.all_gather(shard, ("dp", *CTX), axis=0, tiled=True)


def all_sum(values, axes):
    for axis in axes:
        count = lax.axis_size(axis)
        bit = 1
        while bit < count:
            values = values + lax.ppermute(values, axis, [(i, i ^ bit) for i in range(count)])
            bit *= 2
    return values


def shift(values, places):
    count = lax.axis_size("tp")
    return lax.ppermute(values, "tp", [(i, (i + places) % count) for i in range(count)])


def together(*values):
    return lax.optimization_barrier(values)


def lane_iota(shape):
    return lax.broadcasted_iota(jnp.int32, shape, 1)


def head_means(values):
    width = values.shape[1]
    row = lax.broadcasted_iota(jnp.int32, (width, width), 0) // HD
    col = lax.broadcasted_iota(jnp.int32, (width, width), 1) // HD
    pick = jnp.where(row == col, 1.0 / HD, 0.0).astype(jnp.float32)
    return jnp.dot(
        values, pick, precision=lax.Precision.HIGHEST, preferred_element_type=jnp.float32
    )


def half_swap(values):
    width, half = values.shape[1], HD // 2
    first = lax.rem(lane_iota(values.shape), HD) < half
    return jnp.where(
        first, pltpu.roll(values, width - half, 1), pltpu.roll(values, half, 1)
    )


def other_head(values):
    return pltpu.roll(values, HD, 1)


def twice(values, head):
    wide = values.astype(jnp.float32)
    low = lane_iota(wide.shape) < HD
    other = other_head(wide)
    both = jnp.where(low, wide, other) if head == 0 else jnp.where(low, other, wide)
    return both.astype(values.dtype)


def apart(values):
    wide = values.astype(jnp.float32)
    low = lane_iota(wide.shape) < HD
    zero = jnp.zeros_like(wide)
    return jnp.concatenate(
        [jnp.where(low, wide, zero), jnp.where(low, zero, wide)], axis=0
    ).astype(values.dtype)


def heads_kernel(raw_ref, cos_ref, sin_ref, q_gain_ref, k_gain_ref, q_ref, kv_ref):
    pair = 2 * HD
    q_cols = q_ref.shape[1]
    k_cols = kv_ref.shape[1] // 2
    cos, sin = cos_ref[...], sin_ref[...]
    for first in range(0, q_cols + k_cols, pair):
        values = raw_ref[:, first : first + pair]
        gain = q_gain_ref[...] if first < q_cols else k_gain_ref[...]
        normed = values * lax.rsqrt(head_means(values * values) + NORM_EPS) * gain
        turned = (normed * cos + half_swap(normed) * sin).astype(jnp.bfloat16)
        if first < q_cols:
            q_ref[:, first : first + pair] = turned
        else:
            kv_ref[:, first - q_cols : first - q_cols + pair] = turned
    kv_ref[:, k_cols:] = raw_ref[:, q_cols + k_cols :].astype(jnp.bfloat16)


def make_heads(raw, cos_wide, sin_wide, q_gain, k_gain, q_cols, k_cols):
    rows = raw.shape[0]
    return pl.pallas_call(
        heads_kernel,
        out_shape=(
            jax.ShapeDtypeStruct((rows, q_cols), jnp.bfloat16),
            jax.ShapeDtypeStruct((rows, 2 * k_cols), jnp.bfloat16),
        ),
        cost_estimate=pl.CostEstimate(
            flops=rows * raw.shape[1] * 400, bytes_accessed=rows * raw.shape[1] * 7, transcendentals=0
        ),
        name="make_heads",
    )(raw, cos_wide, sin_wide, q_gain, k_gain)


def turn_back(grad, values, gain, cos, sin):
    turned = grad * cos - half_swap(grad) * sin
    scale = lax.rsqrt(head_means(values * values) + NORM_EPS)
    unit = values * scale
    scaled = turned * gain
    return scale * (scaled - unit * head_means(scaled * unit)), turned * unit


def fill_bias(starts_ref, low_ref, high_ref, bias_ref, piece):
    low, high = low_ref[0], high_ref[0]
    for i in range(bias_ref.shape[0] // piece):
        place = starts_ref[i] + lax.broadcasted_iota(jnp.int32, (piece, low.shape[1]), 0)
        linked = (place >= low) & (place <= high)
        bias_ref[i * piece : (i + 1) * piece, :] = jnp.where(linked, 0.0, MASKED)


def attend_kernel(places, blocks, block_keys, skip, *refs):
    starts_ref, low_ref, high_ref = refs[:3]
    q_refs = refs[3 : 3 + places]
    kv_refs = refs[3 + places : 3 + places + blocks * places]
    refs = refs[3 + places + blocks * places + skip :]
    out_refs = refs[:places]
    total_ref, bias_ref, key_ref, value_ref = refs[places:]
    pair = 2 * HD
    piece, q_cols = q_refs[0].shape
    rows = places * piece
    k_cols = kv_refs[0].shape[1] // 2
    k_heads = k_cols // HD
    group = q_cols // k_cols
    scale = math.log2(math.e) / math.sqrt(HD)
    fill_bias(starts_ref, low_ref, high_ref, bias_ref, piece)
    for block in range(blocks):
        mine = kv_refs[block * places : (block + 1) * places]
        for head in range(k_heads):
            cols = slice(head // 2 * pair, head // 2 * pair + pair)
            vcols = slice(k_cols + head // 2 * pair, k_cols + head // 2 * pair + pair)
            where = slice(block * block_keys, (block + 1) * block_keys)
            keys = jnp.concatenate([ref[:, cols] for ref in mine], axis=0)
            key_ref[head, where, :] = twice(keys, head % 2)
            if head % 2 == 0:
                values = jnp.concatenate([ref[:, vcols] for ref in mine], axis=0)
                value_ref[head // 2, :, where] = values.astype(jnp.float32).T.astype(jnp.bfloat16)
    for first in range(0, q_cols, pair):
        head = first // HD // group
        queries = apart(jnp.concatenate([q_ref[:, first : first + pair] for q_ref in q_refs], axis=0))

        def step(block, carry):
            mixed, total = carry
            where = pl.ds(pl.multiple_of(block * block_keys, block_keys), block_keys)
            scores = matmul_nt(key_ref[head, where, :], queries)
            bias = bias_ref[where, :]
            weight = jnp.exp2(scores * scale + jnp.concatenate([bias, bias], axis=1))
            total = total + jnp.sum(weight, axis=0, keepdims=True)
            values = value_ref[head // 2, head % 2 * HD : (head % 2 + 1) * HD, where]
            return mixed + matmul(values, weight.astype(jnp.bfloat16)), total

        mixed, total = lax.fori_loop(
            0,
            blocks,
            step,
            (jnp.zeros((HD, 2 * rows), jnp.float32), jnp.zeros((1, 2 * rows), jnp.float32)),
        )
        mixed = mixed / total
        out = jnp.concatenate([mixed[:, :rows], mixed[:, rows:]], axis=0).T.astype(jnp.bfloat16)
        for place in range(places):
            out_refs[place][:, first : first + pair] = out[place * piece : (place + 1) * piece]
        total_ref[0, first // pair, :] = jnp.log2(total)[0]


def attend(starts, low, high, q_chunks, kv_blocks, batch, part, parts, before):
    places, blocks = len(q_chunks), len(kv_blocks)
    kv_flat = [kv for block in kv_blocks for kv in block]
    count = batch // parts
    base = part * count
    rows, q_cols = q_chunks[0].shape
    piece = rows // batch
    kv_cols = kv_flat[0].shape[1]
    k_cols = kv_cols // 2
    keys = blocks * places * piece
    q_rows = places * piece
    pairs = q_cols // (2 * HD)
    q_spec = pl.BlockSpec((piece, q_cols), lambda b: (base + b, 0))
    kv_spec = pl.BlockSpec((piece, kv_cols), lambda b: (base + b, 0))
    line_spec = pl.BlockSpec((1, 1, q_rows), lambda b: (base + b, 0, 0))
    work = count * q_cols // HD * q_rows * keys
    results = pl.pallas_call(
        functools.partial(attend_kernel, places, blocks, places * piece, len(before)),
        grid=(count,),
        out_shape=tuple(
            [jax.ShapeDtypeStruct((rows, q_cols), jnp.bfloat16)] * places
            + [jax.ShapeDtypeStruct((batch, pairs, 2 * q_rows), jnp.float32)]
        ),
        in_specs=[
            pl.BlockSpec(memory_space=pltpu.SMEM),
            line_spec,
            pl.BlockSpec((1, 1, q_rows), lambda b: (0, 0, 0)),
        ]
        + [q_spec] * places
        + [kv_spec] * len(kv_flat)
        + [pl.BlockSpec(memory_space=pl.ANY)] * len(before),
        out_specs=tuple(
            [q_spec] * places + [pl.BlockSpec((1, pairs, 2 * q_rows), lambda b: (base + b, 0, 0))]
        ),
        input_output_aliases={3 + places + len(kv_flat) + i: i for i in range(len(before))},
        scratch_shapes=[
            pltpu.VMEM((keys, q_rows), jnp.float32),
            pltpu.VMEM((k_cols // HD, keys, 2 * HD), jnp.bfloat16),
            pltpu.VMEM((k_cols // HD // 2, 2 * HD, keys), jnp.bfloat16),
        ],
        cost_estimate=pl.CostEstimate(
            flops=work * 4 * HD * 4, bytes_accessed=count * q_rows * q_cols * 8, transcendentals=work
        ),
        name="attend",
    )(starts, low, high, *q_chunks, *kv_flat, *before)
    return list(results)


def attend_back_kernel(places, blocks, block_keys, *refs):
    starts_ref, low_ref, high_ref, total_ref, cos_ref, sin_ref, gain_ref = refs[:7]
    refs = refs[7:]
    q_refs, refs = refs[:places], refs[places:]
    raw_refs, refs = refs[:places], refs[places:]
    grad_refs, refs = refs[:places], refs[places:]
    kv_refs, refs = refs[: blocks * places], refs[blocks * places :]
    dq_ref, refs = refs[0], refs[1:]
    dkv_refs, refs = refs[:blocks], refs[blocks:]
    gain_sum_ref, bias_ref, key_ref, turned_ref, value_ref, prob_ref, dprob_ref, dkey_ref, dvalue_ref = refs
    pair = 2 * HD
    piece, q_cols = q_refs[0].shape
    rows = places * piece
    k_cols = kv_refs[0].shape[1] // 2
    k_heads = k_cols // HD
    group = q_cols // k_cols
    inv_root = 1.0 / math.sqrt(HD)
    scale = math.log2(math.e) * inv_root
    fill_bias(starts_ref, low_ref, high_ref, bias_ref, piece)

    @pl.when(pl.program_id(0) == 0)
    def _():
        gain_sum_ref[...] = jnp.zeros_like(gain_sum_ref)

    for block in range(blocks):
        mine = kv_refs[block * places : (block + 1) * places]
        for head in range(k_heads):
            cols = slice(head // 2 * pair, head // 2 * pair + pair)
            vcols = slice(k_cols + head // 2 * pair, k_cols + head // 2 * pair + pair)
            where = slice(block * block_keys, (block + 1) * block_keys)
            keys = jnp.concatenate([ref[:, cols] for ref in mine], axis=0)
            values = jnp.concatenate([ref[:, vcols] for ref in mine], axis=0)
            key_ref[head, where, :] = twice(keys, head % 2)
            value_ref[head, where, :] = twice(values, head % 2)
            if head % 2 == 0:
                turned_ref[head // 2, :, where] = keys.astype(jnp.float32).T.astype(jnp.bfloat16)
    for first in range(0, q_cols, pair):
        head = first // HD // group
        fresh = first % (group * HD) == 0
        queries = apart(jnp.concatenate([q_ref[:, first : first + pair] for q_ref in q_refs], axis=0))
        grads = apart(jnp.concatenate([g_ref[:, first : first + pair] for g_ref in grad_refs], axis=0))
        total = total_ref[0, first // pair : first // pair + 1, :]

        def look(block, delta):
            where = pl.ds(pl.multiple_of(block * block_keys, block_keys), block_keys)
            scores = matmul_nt(key_ref[head, where, :], queries)
            bias = bias_ref[where, :]
            prob = jnp.exp2(scores * scale + jnp.concatenate([bias, bias], axis=1) - total)
            dprob = matmul_nt(value_ref[head, where, :], grads)
            prob_ref[where, :] = prob
            dprob_ref[where, :] = dprob
            return delta + jnp.sum(prob * dprob, axis=0, keepdims=True)

        delta = lax.fori_loop(0, blocks, look, jnp.zeros((1, 2 * rows), jnp.float32))

        def step(block, dquery):
            where = pl.ds(pl.multiple_of(block * block_keys, block_keys), block_keys)
            prob = prob_ref[where, :]
            dscore = (prob * (dprob_ref[where, :] - delta)).astype(jnp.bfloat16)
            dvalue = matmul(prob.astype(jnp.bfloat16), grads)
            dkey = matmul(dscore, queries)
            if fresh:
                dvalue_ref[head, where, :] = dvalue
                dkey_ref[head, where, :] = dkey
            else:
                dvalue_ref[head, where, :] += dvalue
                dkey_ref[head, where, :] += dkey
            keys = turned_ref[head // 2, head % 2 * HD : (head % 2 + 1) * HD, where]
            return dquery + matmul(keys, dscore)

        dquery = lax.fori_loop(0, blocks, step, jnp.zeros((HD, 2 * rows), jnp.float32)) * inv_root
        dquery = jnp.concatenate([dquery[:, :rows], dquery[:, rows:]], axis=0).T
        raw = jnp.concatenate([raw_ref[:, first : first + pair] for raw_ref in raw_refs], axis=0)
        dq, addend = turn_back(
            dquery, raw, gain_ref[...], cos_ref[...].reshape(rows, pair), sin_ref[...].reshape(rows, pair)
        )
        gain_sum_ref[...] += jnp.sum(addend.reshape(-1, 8, pair), axis=0)
        dq_ref[:, :, first : first + pair] = dq.reshape(places, piece, pair).astype(jnp.bfloat16)
    low = lane_iota((block_keys, pair)) < HD
    for block in range(blocks):
        where = slice(block * block_keys, (block + 1) * block_keys)
        for first in range(0, k_heads, 2):
            for shift, ref, factor in ((0, dkey_ref, inv_root), (k_cols, dvalue_ref, 1.0)):
                one, two = ref[first, where, :], ref[first + 1, where, :]
                sums = jnp.where(low, one + other_head(one), two + other_head(two)) * factor
                cols = slice(shift + first // 2 * pair, shift + first // 2 * pair + pair)
                dkv_refs[block][:, :, cols] = sums.reshape(places, piece, pair).astype(
                    dkv_refs[block].dtype
                )


def attend_back(
    starts,
    low,
    high,
    totals,
    cos_wide,
    sin_wide,
    q_gain,
    q_chunks,
    raw_chunks,
    grad_chunks,
    kv_blocks,
    kinds,
    batch,
    part,
    parts,
):
    places, blocks = len(q_chunks), len(kv_blocks)
    kv_flat = [kv for block in kv_blocks for kv in block]
    count = batch // parts
    base = part * count
    rows, q_cols = q_chunks[0].shape
    piece = rows // batch
    kv_cols = kv_flat[0].shape[1]
    k_cols = kv_cols // 2
    keys = blocks * places * piece
    q_rows = places * piece
    pairs = q_cols // (2 * HD)
    k_heads = k_cols // HD
    q_spec = pl.BlockSpec((piece, q_cols), lambda b: (base + b, 0))
    kv_spec = pl.BlockSpec((piece, kv_cols), lambda b: (base + b, 0))
    line_spec = pl.BlockSpec((1, 1, q_rows), lambda b: (base + b, 0, 0))
    turn_spec = pl.BlockSpec((places, piece, 2 * HD), lambda b: (0, base + b, 0))
    work = count * q_cols // HD * q_rows * keys
    results = pl.pallas_call(
        functools.partial(attend_back_kernel, places, blocks, places * piece),
        grid=(count,),
        out_shape=tuple(
            [jax.ShapeDtypeStruct((places, rows // parts, q_cols), jnp.bfloat16)]
            + [jax.ShapeDtypeStruct((places, rows // parts, kv_cols), kind) for kind in kinds]
            + [jax.ShapeDtypeStruct((8, 2 * HD), jnp.float32)]
        ),
        in_specs=[
            pl.BlockSpec(memory_space=pltpu.SMEM),
            line_spec,
            pl.BlockSpec((1, 1, q_rows), lambda b: (0, 0, 0)),
            pl.BlockSpec((1, pairs, 2 * q_rows), lambda b: (base + b, 0, 0)),
            turn_spec,
            turn_spec,
            pl.BlockSpec((1, 2 * HD), lambda b: (0, 0)),
        ]
        + [q_spec] * (3 * places)
        + [kv_spec] * len(kv_flat),
        out_specs=tuple(
            [pl.BlockSpec((places, piece, q_cols), lambda b: (0, b, 0))]
            + [pl.BlockSpec((places, piece, kv_cols), lambda b: (0, b, 0))] * blocks
            + [pl.BlockSpec((8, 2 * HD), lambda b: (0, 0))]
        ),
        scratch_shapes=[
            pltpu.VMEM((keys, q_rows), jnp.float32),
            pltpu.VMEM((k_heads, keys, 2 * HD), jnp.bfloat16),
            pltpu.VMEM((k_heads // 2, 2 * HD, keys), jnp.bfloat16),
            pltpu.VMEM((k_heads, keys, 2 * HD), jnp.bfloat16),
            pltpu.VMEM((keys, 2 * q_rows), jnp.float32),
            pltpu.VMEM((keys, 2 * q_rows), jnp.float32),
            pltpu.VMEM((k_heads, keys, 2 * HD), jnp.float32),
            pltpu.VMEM((k_heads, keys, 2 * HD), jnp.float32),
        ],
        cost_estimate=pl.CostEstimate(
            flops=work * 10 * HD * 4, bytes_accessed=count * q_rows * q_cols * 16, transcendentals=work
        ),
        name="attend_back",
    )(
        starts,
        low,
        high,
        totals,
        cos_wide,
        sin_wide,
        q_gain,
        *q_chunks,
        *raw_chunks,
        *grad_chunks,
        *kv_flat,
    )
    return results[0], list(results[1:-1]), results[-1]


def heads_back_kernel(places, parts, q_cols, *refs):
    dq_refs, refs = refs[:parts], refs[parts:]
    own_refs, refs = refs[:parts], refs[parts:]
    came_refs, refs = refs[:parts], refs[parts:]
    raw_refs, refs = refs[:places], refs[places:]
    cos_ref, sin_ref, gain_ref, out_ref, gain_sum_ref = refs
    rows = raw_refs[0].shape[0]
    part_rows = rows // parts
    k_cols = own_refs[0].shape[2] // 2
    pair = 2 * HD
    addends = jnp.zeros((8, pair), jnp.float32)
    for place in range(places):
        for part in range(parts):
            mine = slice(part * part_rows, (part + 1) * part_rows)
            out = slice(place * rows + part * part_rows, place * rows + (part + 1) * part_rows)
            out_ref[out, :q_cols] = dq_refs[part][place]
            grads = own_refs[part][place] + came_refs[part][place].astype(jnp.float32)
            for first in range(0, k_cols, pair):
                cols = slice(first, first + pair)
                dk, addend = turn_back(
                    grads[:, cols],
                    raw_refs[place][mine, cols],
                    gain_ref[...],
                    cos_ref[place, mine],
                    sin_ref[place, mine],
                )
                out_ref[out, q_cols + first : q_cols + first + pair] = dk.astype(jnp.bfloat16)
                addends = addends + jnp.sum(addend.reshape(-1, 8, pair), axis=0)
            out_ref[out, q_cols + k_cols :] = grads[:, k_cols:].astype(jnp.bfloat16)
    gain_sum_ref[...] = addends


def heads_back(dq_parts, own_parts, came_parts, raw_chunks, cos_wide, sin_wide, k_gain):
    parts, places = len(dq_parts), len(raw_chunks)
    rows = raw_chunks[0].shape[0]
    q_cols, kv_cols = dq_parts[0].shape[2], own_parts[0].shape[2]
    k_cols = kv_cols // 2

    def whole(array):
        return pl.BlockSpec(array.shape, lambda i: (0,) * array.ndim)

    inputs = [*dq_parts, *own_parts, *came_parts]
    turns = [cos_wide, sin_wide, k_gain]
    return pl.pallas_call(
        functools.partial(heads_back_kernel, places, parts, q_cols),
        grid=(1,),
        out_shape=(
            jax.ShapeDtypeStruct((places * rows, q_cols + kv_cols), jnp.bfloat16),
            jax.ShapeDtypeStruct((8, 2 * HD), jnp.float32),
        ),
        in_specs=[whole(array) for array in inputs]
        + [pl.BlockSpec((rows, k_cols), lambda i: (0, q_cols // k_cols))] * places
        + [whole(array) for array in turns],
        out_specs=(
            pl.BlockSpec((places * rows, q_cols + kv_cols), lambda i: (0, 0)),
            pl.BlockSpec((8, 2 * HD), lambda i: (0, 0)),
        ),
        cost_estimate=pl.CostEstimate(
            flops=places * rows * kv_cols * 400, bytes_accessed=places * rows * 4096, transcendentals=0
        ),
        name="heads_back",
    )(*inputs, *raw_chunks, *turns)


def feed_kernel(count, *refs):
    hidden_refs, grad_refs = refs[:count], refs[count : 2 * count]
    gate_ref, up_ref, down_ref, act_ref, dgate_ref, dup_ref, hidden, grads = refs[2 * count :]

    @pl.when(pl.program_id(0) == 0)
    def _():
        rows = hidden_refs[0].shape[0]
        for i in range(count):
            hidden[i * rows : (i + 1) * rows, :] = hidden_refs[i][...]
            grads[i * rows : (i + 1) * rows, :] = grad_refs[i][...]

    gate = matmul(hidden[...], gate_ref[...])
    up = matmul(hidden[...], up_ref[...])
    grad = matmul(grads[...], down_ref[...])
    sigmoid = 1.0 / (1.0 + jnp.exp(-gate))
    silu = gate * sigmoid
    act_ref[...] = (silu * up).astype(jnp.bfloat16)
    dgate_ref[...] = (grad * up * sigmoid * (1.0 + gate * (1.0 - sigmoid))).astype(jnp.bfloat16)
    dup_ref[...] = (grad * silu).astype(jnp.bfloat16)


def feed_rows(hidden_rows, grad_rows, gate, up, down_t, cols):
    count = len(hidden_rows)
    rows, width = hidden_rows[0].shape
    total = count * rows
    tile = min(cols, 512 if count == 1 else 256)
    steps = cols // tile
    row_spec = pl.BlockSpec((rows, width), lambda j: (0, 0))
    out_spec = pl.BlockSpec((total, tile), lambda j: (0, j))

    def weight_spec(weight):
        return pl.BlockSpec((width, tile), lambda j: (0, weight[1] * steps + j))

    return pl.pallas_call(
        functools.partial(feed_kernel, count),
        grid=(steps,),
        out_shape=tuple([jax.ShapeDtypeStruct((total, cols), jnp.bfloat16)] * 3),
        in_specs=[row_spec] * (2 * count)
        + [
            weight_spec(gate),
            weight_spec(up),
            weight_spec(down_t),
        ],
        out_specs=tuple([out_spec] * 3),
        scratch_shapes=[pltpu.VMEM((total, width), jnp.bfloat16)] * 2,
        cost_estimate=pl.CostEstimate(
            flops=6 * total * width * cols,
            bytes_accessed=6 * width * cols + 4 * total * width + 6 * total * cols,
            transcendentals=total * cols,
        ),
        name="feed_rows",
    )(*hidden_rows, *grad_rows, gate[0], up[0], down_t[0])


def fill_rows(parts, whole):
    row = 0
    for line in parts:
        col = 0
        for ref in line:
            rows, cols = ref.shape
            whole[row : row + rows, col : col + cols] = ref[...]
            col += cols
        row += rows


def rows_nt_kernel(layouts, *refs):
    count = len(layouts)
    parts = []
    for lines, cols in layouts:
        parts.append([refs[i * cols : (i + 1) * cols] for i in range(lines)])
        refs = refs[lines * cols :]
    weight_refs, out_refs, wholes = refs[:count], refs[count:-count], refs[-count:]

    @pl.when(pl.program_id(0) == 0)
    def _():
        for part, whole in zip(parts, wholes):
            fill_rows(part, whole)

    result = matmul_nt(wholes[0][...], weight_refs[0][...])
    for weight_ref, whole in zip(weight_refs[1:], wholes[1:]):
        result = result + matmul_nt(whole[...], weight_ref[...])
    rows = out_refs[0].shape[0]
    for i, out_ref in enumerate(out_refs):
        out_ref[...] = result[i * rows : (i + 1) * rows].astype(out_ref.dtype)


def rows_nt(addends, kind, outs=1, tile=512):
    layouts, parts, depths = [], [], []
    for lines, _ in addends:
        layouts.append((len(lines), len(lines[0])))
        parts.extend(part for line in lines for part in line)
        depths.append(sum(part.shape[1] for part in lines[0]))
    rows = sum(line[0].shape[0] for line in addends[0][0])
    weights = [weight for _, weight in addends]
    width = weights[0][0].shape[0]

    def weight_spec(weight, depth):
        return pl.BlockSpec((tile, depth), lambda j: (j, weight[1]))

    results = pl.pallas_call(
        functools.partial(rows_nt_kernel, layouts),
        grid=(width // tile,),
        out_shape=tuple([jax.ShapeDtypeStruct((rows // outs, width), kind)] * outs),
        in_specs=[pl.BlockSpec(part.shape, lambda j: (0, 0)) for part in parts]
        + [weight_spec(weight, depth) for weight, depth in zip(weights, depths)],
        out_specs=tuple([pl.BlockSpec((rows // outs, tile), lambda j: (0, j))] * outs),
        scratch_shapes=[pltpu.VMEM((rows, depth), jnp.bfloat16) for depth in depths],
        cost_estimate=pl.CostEstimate(
            flops=2 * rows * sum(depths) * width,
            bytes_accessed=2 * sum(depths) * (rows + width) + 2 * rows * width,
            transcendentals=0,
        ),
        name="rows_nt",
    )(*parts, *[weight[0] for weight in weights])
    return list(results)


def add_kernel(one_ref, two_ref, out_ref):
    out_ref[...] = (one_ref[...].astype(jnp.float32) + two_ref[...].astype(jnp.float32)).astype(
        out_ref.dtype
    )


def add_rows(one, two, tile=1024):
    rows, cols = one.shape
    spec = pl.BlockSpec((rows, tile), lambda j: (0, j))
    return pl.pallas_call(
        add_kernel,
        grid=(cols // tile,),
        out_shape=jax.ShapeDtypeStruct(one.shape, one.dtype),
        in_specs=[spec, spec],
        out_specs=spec,
        cost_estimate=pl.CostEstimate(flops=rows * cols, bytes_accessed=6 * rows * cols, transcendentals=0),
        name="add_rows",
    )(one, two)


def split_kernel(rows_ref, weight_ref, *out_refs):
    result = matmul(rows_ref[...], weight_ref[...]).astype(jnp.bfloat16)
    for i, out_ref in enumerate(out_refs):

        @pl.when(pl.program_id(0) == i)
        def _():
            out_ref[...] = result


def split_columns(rows, weight, first, count, cols):
    total, depth = rows.shape
    return pl.pallas_call(
        split_kernel,
        grid=(count,),
        out_shape=tuple([jax.ShapeDtypeStruct((total, cols), jnp.bfloat16)] * count),
        in_specs=[
            pl.BlockSpec((total, depth), lambda j: (0, 0)),
            pl.BlockSpec((depth, cols), lambda j: (0, first + j)),
        ],
        out_specs=tuple([pl.BlockSpec((total, cols), lambda j: (0, 0))] * count),
        cost_estimate=pl.CostEstimate(
            flops=2 * total * depth * cols * count,
            bytes_accessed=2 * (total * depth + depth * cols * count + total * cols * count),
            transcendentals=0,
        ),
        name="split_columns",
    )(rows, weight)


def product_kernel(left_count, right_counts, blocks, first_ref, *refs):
    left_refs, refs = refs[:left_count], refs[left_count:]
    rights = []
    for count in right_counts:
        rights.append(refs[:count])
        refs = refs[count:]
    out_ref, left, right = refs
    steps = pl.num_programs(0) // len(rights)

    @pl.when(pl.program_id(0) == 0)
    def _():
        if blocks:
            cols = left.shape[1] // blocks
            row = 0
            for ref in left_refs:
                rows = ref.shape[0]
                for i in range(blocks):
                    start = pl.multiple_of((2 * i + first_ref[0]) * cols, cols)
                    left[row : row + rows, i * cols : (i + 1) * cols] = ref[:, pl.ds(start, cols)]
                row += rows
        else:
            fill_rows([[ref] for ref in left_refs], left)

    for i, refs in enumerate(rights):

        @pl.when(pl.program_id(0) // steps == i)
        def _():
            fill_rows([[ref] for ref in refs], right)

    out_ref[...] = matmul_tn(left[...], right[...]).astype(jnp.bfloat16)


def product(left, rights, tile=512, first=None, blocks=0):
    width, cols = left[0].shape[1], rights[0][0].shape[1]
    depth = sum(part.shape[0] for part in left)
    tile = min(tile, cols)
    steps = cols // tile
    out_rows = width // 2 if blocks else width
    first = jnp.zeros((1,), jnp.int32) if first is None else first

    def right_spec(part, index):
        return pl.BlockSpec(
            (part.shape[0], tile), lambda j: (0, jnp.clip(j - index * steps, 0, steps - 1))
        )

    return pl.pallas_call(
        functools.partial(product_kernel, len(left), [len(parts) for parts in rights], blocks),
        grid=(steps * len(rights),),
        out_shape=jax.ShapeDtypeStruct((out_rows, cols * len(rights)), jnp.bfloat16),
        in_specs=[pl.BlockSpec(memory_space=pltpu.SMEM)]
        + [pl.BlockSpec(part.shape, lambda j: (0, 0)) for part in left]
        + [right_spec(part, index) for index, parts in enumerate(rights) for part in parts],
        out_specs=pl.BlockSpec((out_rows, tile), lambda j: (0, j)),
        scratch_shapes=[
            pltpu.VMEM((depth, out_rows), jnp.bfloat16),
            pltpu.VMEM((depth, tile), jnp.bfloat16),
        ],
        cost_estimate=pl.CostEstimate(
            flops=2 * depth * out_rows * cols * len(rights),
            bytes_accessed=2 * (depth * width + (depth + out_rows) * cols * len(rights)),
            transcendentals=0,
        ),
        name="product",
    )(first, *left, *[part for parts in rights for part in parts])


def unit_of(values):
    scale = lax.rsqrt(jnp.mean(values * values, axis=-1, keepdims=True) + NORM_EPS)
    return values * scale, scale


def norm_kernel(rows_ref, more_ref, sum_ref, unit_ref):
    values = rows_ref[...].astype(jnp.float32) + more_ref[...]
    sum_ref[...] = values
    unit_ref[...] = unit_of(values)[0].astype(jnp.bfloat16)


def add_and_norm(rows, more, tile=64):
    count, width = rows.shape
    spec = pl.BlockSpec((tile, width), lambda i: (i, 0))
    return pl.pallas_call(
        norm_kernel,
        grid=(count // tile,),
        out_shape=(
            jax.ShapeDtypeStruct(rows.shape, jnp.float32),
            jax.ShapeDtypeStruct(rows.shape, jnp.bfloat16),
        ),
        in_specs=[spec, spec],
        out_specs=(spec, spec),
        cost_estimate=pl.CostEstimate(
            flops=5 * count * width, bytes_accessed=12 * count * width, transcendentals=0
        ),
        name="add_and_norm",
    )(rows, more)


def norm_back_kernel(one_ref, two_ref, rows_ref, base_ref, *out_refs):
    scaled = one_ref[...].astype(jnp.float32) + two_ref[...].astype(jnp.float32)
    unit, scale = unit_of(rows_ref[...].astype(jnp.float32))
    result = base_ref[...].astype(jnp.float32) + scale * (
        scaled - unit * jnp.mean(scaled * unit, axis=-1, keepdims=True)
    )
    for out_ref in out_refs:
        out_ref[...] = result.astype(out_ref.dtype)


def norm_back(one, two, rows, base, kinds, tile=64):
    count, width = rows.shape
    spec = pl.BlockSpec((tile, width), lambda i: (i, 0))
    return pl.pallas_call(
        norm_back_kernel,
        grid=(count // tile,),
        out_shape=tuple(jax.ShapeDtypeStruct(rows.shape, kind) for kind in kinds),
        in_specs=[spec] * 4,
        out_specs=tuple([spec] * len(kinds)),
        cost_estimate=pl.CostEstimate(
            flops=10 * count * width, bytes_accessed=14 * count * width, transcendentals=0
        ),
        name="norm_back",
    )(one, two, rows, base)


def per_device(
    block_in,
    segments,
    positions,
    attention_gain,
    query_weight,
    key_weight,
    value_weight,
    query_gain,
    key_gain,
    output_weight,
    hidden_gain,
    gate_weight,
    up_weight,
    down_weight,
    cotangent,
):
    tp_count = lax.axis_size("tp")
    tp_index = lax.axis_index("tp")
    ctx_index = lax.axis_index(CTX)
    batch, own_rows, width = block_in.shape
    rows = batch * own_rows
    ctx_rows = own_rows * tp_count
    places = range(tp_count)
    order = [*range(1, tp_count), 0]
    masks = ctx_masks()
    q_cols = query_weight.shape[1]
    k_cols = key_weight.shape[1]
    qkv_cols = q_cols + 2 * k_cols
    hidden_cols = gate_weight.shape[1]
    q_gain = jnp.tile(query_gain.astype(jnp.float32), 2)[None]
    k_gain = jnp.tile(key_gain.astype(jnp.float32), 2)[None]

    block = width // (lax.axis_size("dp") * lax.axis_size(CTX))
    paired = block % 128 == 0
    pair_first = lax.rem(ctx_index, 2).astype(jnp.int32)[None]

    def meet(arrays):
        return [*arrays, *[ctx_swap(array, 1) for array in arrays]] if paired else list(arrays)

    def grad_product(left, rights, tile=512):
        return product(left, rights, tile, pair_first, width // block // 2 if paired else 0)

    def scatter_sum(addend):
        axes = ("dp", CTX[0]) if paired else ("dp", *CTX)
        return lax.psum_scatter(addend, axes, scatter_dimension=0, tiled=True)

    back_places = [(tp_count - place) % tp_count for place in places]
    attention_rows = attention_gain.astype(jnp.float32)[:, None]
    hidden_gain_rows = hidden_gain.astype(jnp.float32)[:, None]
    qkv_weight = jnp.concatenate([query_weight, key_weight, value_weight], axis=1).astype(jnp.float32)
    first_weight = jnp.concatenate(
        [
            (gate_weight.astype(jnp.float32) * hidden_gain_rows).astype(jnp.bfloat16),
            (qkv_weight * attention_rows).astype(jnp.bfloat16),
        ],
        axis=1,
    )
    full_first = gather_weight(first_weight)
    full_qkv = full_first[:, hidden_cols:]

    def chunk_start(place):
        owner = lax.rem(tp_index - place + tp_count, tp_count)
        return owner * own_rows

    def own_part(table, start):
        return lax.dynamic_slice_in_dim(table, start, own_rows, 1)

    iota = jnp.arange(own_rows, dtype=jnp.int32)
    row_starts = [ctx_index * ctx_rows + chunk_start(place) for place in places]
    low = jnp.concatenate([own_part(segments, start) for start in row_starts], axis=1)[:, None]
    high = jnp.concatenate([start + iota for start in row_starts])[None, None]
    starts = jnp.stack(
        [
            jnp.bitwise_xor(ctx_index, mask) * ctx_rows + chunk_start(place)
            for mask in masks
            for place in places
        ]
    ).astype(jnp.int32)
    position = jnp.stack([own_part(positions, start).reshape(rows) for start in row_starts])
    half = HD // 2
    frequency = ROPE_BASE ** (-2.0 * jnp.arange(half, dtype=jnp.float32) / HD)
    sign = jnp.where(jnp.arange(2 * HD) % HD < half, -1.0, 1.0).astype(jnp.float32)
    angles = position.astype(jnp.float32)[..., None] * jnp.tile(frequency, 4)
    cos_wide, sin_wide = jnp.cos(angles), jnp.sin(angles) * sign

    def project(place):
        values = matmul(normed_rows[place], full_qkv)
        query_rot, kv = make_heads(
            values, cos_wide[place], sin_wide[place], q_gain, k_gain, q_cols, k_cols
        )
        return values, query_rot, kv

    def project_and_send(place):
        values, query_rot, kv = project(place)
        blocks = ctx_gather(kv)
        return values, query_rot, blocks

    tokens = block_in.reshape(rows, width)
    normed_rows, heads = [unit_of(tokens.astype(jnp.float32))[0].astype(jnp.bfloat16)], []
    for place in range(1, tp_count):
        came = ring_hop(normed_rows[-1])
        ready = range(tp_count - 1) if place == tp_count - 1 else []
        work = [project_and_send(mine) for mine in ready]
        came, work = together(came, work)
        if place == 1:
            came, out_own = together(came, output_weight.T)
            out_pieces = [out_own] + [shift(out_own, -other) for other in range(1, tp_count)]
        if place == 2:
            came, out_pieces = together(came, out_pieces)
            second_weight = jnp.concatenate(
                [*out_pieces, (up_weight.astype(jnp.float32) * hidden_gain_rows).astype(jnp.bfloat16)],
                axis=1,
            )
            full_second = gather_weight(second_weight)
        heads.extend(work)
        normed_rows.append(came)
    last_weight, normed_rows[-1] = together(down_weight.T, normed_rows[-1])
    full_down_t = gather_weight(last_weight)
    full_out, full_gate, full_up, full_down = (full_second, 0), (full_first, 0), (full_second, 1), (full_down_t, 0)

    grad_own, normed_rows[-1] = together(cotangent.reshape(rows, width), normed_rows[-1])
    came = ring_hop(grad_own)
    work = [project_and_send(mine) for mine in range(len(heads), tp_count)]
    came, work = together(came, work)
    heads.extend(work)
    raw, queries, gathered = ([h[i] for h in heads] for i in range(3))
    blocks = [[gathered[place][i] for place in places] for i in range(len(masks))]
    grad_rows = [grad_own, came]
    attended = []
    parts = 2
    late_qkv = full_qkv
    came = ring_hop(grad_rows[-1])
    for part in range(parts):
        attended = attend(starts, low, high, queries, blocks, batch, part, parts, attended)
        if part == 0:
            late_qkv, attended = together(late_qkv, attended)
    came, attended = together(came, attended)
    grad_rows.append(came)
    attended_rows, totals = attended[:tp_count], attended[tp_count]
    mine = [attended_rows[0]] + [shift(attended_rows[place], -place) for place in range(1, tp_count)]
    grad_rows[-1], mine = together(grad_rows[-1], mine)
    for _ in range(len(grad_rows), tp_count):
        grad_rows.append(ring_hop(grad_rows[-1]))
    met_grads = meet(grad_rows)
    (mixed_in,) = rows_nt([([mine], full_out)], jnp.float32)
    met_mine = [meet([piece]) for piece in mine]
    hidden, unit_hidden = add_and_norm(tokens, mixed_in)

    def feed(group):
        return feed_rows(
            [hidden_rows[place] for place in group],
            [grad_rows[place] for place in group],
            full_gate,
            full_up,
            full_down,
            hidden_cols,
        )

    def hidden_terms(fed):
        return rows_nt([([[fed[1]]], full_gate), ([[fed[2]]], full_up)], jnp.bfloat16, 2)

    first, second = list(places)[: tp_count // 2], list(places)[tp_count // 2 :]
    hidden_rows = [unit_hidden]
    fed_first, terms_first = None, None
    for place in range(1, tp_count):
        came = ring_hop(hidden_rows[-1])
        if place == len(first):
            fed_first = feed(first)
            came, fed_first, met_grads, met_mine = together(came, fed_first, met_grads, met_mine)
        if place == len(first) + 1:
            met_first = [meet([fed]) for fed in fed_first]
            terms_first = hidden_terms(fed_first)
            came, terms_first, met_first = together(came, terms_first, met_first)
        hidden_rows.append(came)

    came = ring_hop(terms_first[1])
    met_hidden = meet(hidden_rows)
    fed_second = feed(second)
    came, fed_second, met_hidden = together(came, fed_second, met_hidden)
    met_fed = [old + meet([fed]) for old, fed in zip(met_first, fed_second)]
    if paired:
        met_fed = [[fed[0], fed[2], fed[1], fed[3]] for fed in met_fed]
    terms_second = hidden_terms(fed_second)
    came = ring_hop(add_rows(came, terms_second[0]))
    down_product = grad_product(met_grads, [met_fed[0]])
    came, down_product = together(came, down_product)
    came = ring_hop(add_rows(came, terms_second[1]))
    down_shard = scatter_sum(down_product)
    gate_product = grad_product(met_hidden, [met_fed[1]])
    up_product = grad_product(met_hidden, [met_fed[2]])
    came, gate_product, up_product = together(came, gate_product, up_product)
    gate_shard = scatter_sum(gate_product)

    grad_hidden, branch = norm_back(
        came, terms_first[0], hidden, grad_own, (jnp.float32, jnp.bfloat16)
    )
    pieces = split_columns(branch, full_second, 0, tp_count, q_cols)
    grad_att = [pieces[0]] + [shift(pieces[place], place) for place in range(1, tp_count)]
    met_branch = meet([branch])
    feed_terms = rows_nt(
        [([[fed_first[0]], [fed_second[0]]], full_down)], jnp.bfloat16, tp_count
    )
    out_product = grad_product(met_branch, met_mine)
    grad_att, out_product, feed_terms = together(grad_att, out_product, feed_terms)
    out_shard = scatter_sum(out_product)

    kinds = [jnp.float32] * (len(masks) // 2) + [jnp.bfloat16] * (len(masks) - len(masks) // 2)
    query_gain_sum = jnp.zeros((8, 2 * HD), jnp.float32)
    dq_parts, own_parts, came_parts = [], [], []
    total = feed_terms[1]
    for step, place in enumerate(order[1:]):
        came = ring_hop(total)
        if step < 2:
            dq, back, addend = attend_back(
                starts,
                low,
                high,
                totals,
                cos_wide,
                sin_wide,
                q_gain,
                queries,
                raw,
                grad_att,
                blocks,
                kinds,
                batch,
                step,
                2,
            )
            came, dq, back, addend, grad_att, own_parts, came_parts = together(
                came, dq, back, addend, grad_att, own_parts, came_parts
            )
            if step == 0:
                came, down_shard = together(came, down_shard)
            query_gain_sum = query_gain_sum + addend
            dq_parts.append(dq)
            bit = 1
            while len(back) > 2:
                half_count = len(back) // 2
                back = [
                    back[i] + ctx_swap(back[half_count + i].astype(jnp.bfloat16), bit).astype(jnp.float32)
                    for i in range(half_count)
                ]
                bit *= 2
            own_parts.append(back[0])
            came_parts.append(ctx_swap(back[1].astype(jnp.bfloat16), bit))
        else:
            grad_qkv, key_gain_sum = heads_back(
                dq_parts, own_parts, came_parts, raw, cos_wide, sin_wide, k_gain
            )
            came, grad_qkv, gate_shard, out_shard = together(came, grad_qkv, gate_shard, out_shard)
        if place:
            total = add_rows(came, feed_terms[place])
    feed_out = came.astype(jnp.float32) + feed_terms[0].astype(jnp.float32)
    block_out = (hidden + feed_out).astype(jnp.bfloat16).reshape(block_in.shape)

    row_terms = rows_nt([([[grad_qkv]], (late_qkv, 0))], jnp.bfloat16, tp_count)
    up_shard = scatter_sum(up_product)
    head_sums = jnp.stack([query_gain_sum, key_gain_sum]).sum(axis=1).reshape(2, 2, HD).sum(axis=1)
    total = row_terms[1]
    out_total = out_shard[:, back_places[1] * q_cols : (back_places[1] + 1) * q_cols]
    for step, place in enumerate(order[1:]):
        came = ring_hop(total)
        start = back_places[place] * q_cols
        out_total = ring_hop(out_total).astype(jnp.float32) + out_shard[
            :, start : start + q_cols
        ].astype(jnp.float32)
        if place:
            out_total = out_total.astype(jnp.bfloat16)
        if step == 0:
            head_sums = all_sum(head_sums, (CTX, "dp"))
            qkv_product = product(normed_rows, [[grad_qkv]], grad_qkv.shape[1])
            came, qkv_product, head_sums, out_total = together(
                came, qkv_product, head_sums, out_total
            )
            qkv_shard = lax.psum_scatter(qkv_product, ("dp", *CTX), scatter_dimension=0, tiled=True)
        if step == 1:
            came, up_shard, out_total = together(came, up_shard, out_total)
        if place:
            total = add_rows(came, row_terms[place])
    qkv_sums = qkv_shard.astype(jnp.float32)
    gate_sums, up_sums = gate_shard.astype(jnp.float32), up_shard.astype(jnp.float32)
    attention_sum = jnp.sum(qkv_sums * qkv_weight, axis=1)
    hidden_sums = jnp.sum(
        gate_sums * gate_weight.astype(jnp.float32) + up_sums * up_weight.astype(jnp.float32), axis=1
    )
    small_sums = jnp.concatenate([jnp.stack([attention_sum, hidden_sums]), head_sums], axis=1)
    small_sums = all_sum(small_sums, ("tp",))
    attention_gain_grad, hidden_gain_grad = small_sums[0, :block], small_sums[1, :block]
    head_sums = small_sums[:, block:]
    (input_grad,) = norm_back(came, row_terms[0], tokens, grad_hidden, (jnp.float32,))
    output_grad = out_total.T
    down_grad = down_shard.astype(jnp.float32).T
    gate_grad, up_grad = gate_sums * hidden_gain_rows, up_sums * hidden_gain_rows
    qkv_grad = qkv_sums * attention_rows
    return (
        block_out,
        input_grad.reshape(block_in.shape),
        attention_gain_grad,
        qkv_grad[:, :q_cols],
        qkv_grad[:, q_cols : q_cols + k_cols],
        qkv_grad[:, q_cols + k_cols :],
        head_sums[0],
        head_sums[1],
        output_grad,
        hidden_gain_grad,
        gate_grad,
        up_grad,
        down_grad,
    )


def solution(mesh):
    in_specs = (
        P(None, ("dp", *CTX, "tp"), None),
        P(None, "dp"),
        P(None, "dp"),
        P(("dp", *CTX)),
        P(("dp", *CTX), "tp"),
        P(("dp", *CTX), "tp"),
        P(("dp", *CTX), "tp"),
        P(),
        P(),
        P("tp", ("dp", *CTX)),
        P(("dp", *CTX)),
        P(("dp", *CTX), "tp"),
        P(("dp", *CTX), "tp"),
        P("tp", ("dp", *CTX)),
        P(None, ("dp", *CTX, "tp"), None),
    )
    out_specs = (
        P(None, ("dp", *CTX, "tp"), None),
        P(None, ("dp", *CTX, "tp"), None),
        P(("dp", *CTX)),
        P(("dp", *CTX), "tp"),
        P(("dp", *CTX), "tp"),
        P(("dp", *CTX), "tp"),
        P(),
        P(),
        P("tp", ("dp", *CTX)),
        P(("dp", *CTX)),
        P(("dp", *CTX), "tp"),
        P(("dp", *CTX), "tp"),
        P("tp", ("dp", *CTX)),
    )
    shape = (mesh.shape["dp"], mesh.shape["ctx"] // 2, 2, mesh.shape["tp"])
    split = Mesh(mesh.devices.reshape(shape), ("dp", *CTX, "tp"))
    return jax.shard_map(
        per_device, mesh=split, in_specs=in_specs, out_specs=out_specs, check_vma=False
    )
```

```python
import functools
import math

import jax
import jax.numpy as jnp
from jax import lax
from jax.experimental import pallas as pl
from jax.experimental.pallas import tpu as pltpu
from jax.sharding import Mesh
from jax.sharding import PartitionSpec as P

D = 2048
HD = 64


NORM_EPS = 1e-05
ROPE_BASE = 1000000.0
MASKED = -1e30
CTX = ("ctx_pair", "ctx_place")


def matmul(left_mat, right_mat):
    return jnp.dot(left_mat, right_mat, preferred_element_type=jnp.float32)


def matmul_tn(left_mat, right_mat):
    return lax.dot_general(
        left_mat, right_mat, (((0,), (0,)), ((), ())), preferred_element_type=jnp.float32
    )


def matmul_nt(left_mat, right_mat):
    return lax.dot_general(
        left_mat, right_mat, (((1,), (1,)), ((), ())), preferred_element_type=jnp.float32
    )


def ring_hop(values):
    count = lax.axis_size("tp")
    return lax.ppermute(values, "tp", [(i, (i + 1) % count) for i in range(count)])


def ctx_swap(values, mask):
    count = lax.axis_size(CTX)
    return lax.ppermute(values, CTX, [(i, i ^ mask) for i in range(count)])


def ctx_masks():
    masks = [0]
    bit = lax.axis_size(CTX) // 2
    while bit:
        masks = masks + [mask ^ bit for mask in masks]
        bit //= 2
    return masks


def ctx_gather(own):
    blocks = [own]
    bit = lax.axis_size(CTX) // 2
    while bit:
        blocks = blocks + [ctx_swap(block, bit) for block in blocks]
        bit //= 2
    return blocks


def gather_weight(shard):
    return lax.all_gather(shard, ("dp", *CTX), axis=0, tiled=True)


def all_sum(values, axes):
    for axis in axes:
        count = lax.axis_size(axis)
        bit = 1
        while bit < count:
            values = values + lax.ppermute(values, axis, [(i, i ^ bit) for i in range(count)])
            bit *= 2
    return values


def shift(values, places):
    count = lax.axis_size("tp")
    return lax.ppermute(values, "tp", [(i, (i + places) % count) for i in range(count)])


def together(*values):
    return lax.optimization_barrier(values)


def lane_iota(shape):
    return lax.broadcasted_iota(jnp.int32, shape, 1)


def head_means(values):
    width = values.shape[1]
    row = lax.broadcasted_iota(jnp.int32, (width, width), 0) // HD
    col = lax.broadcasted_iota(jnp.int32, (width, width), 1) // HD
    pick = jnp.where(row == col, 1.0 / HD, 0.0).astype(jnp.float32)
    return jnp.dot(
        values, pick, precision=lax.Precision.HIGHEST, preferred_element_type=jnp.float32
    )


def half_swap(values):
    width, half = values.shape[1], HD // 2
    first = lax.rem(lane_iota(values.shape), HD) < half
    return jnp.where(
        first, pltpu.roll(values, width - half, 1), pltpu.roll(values, half, 1)
    )


def other_head(values):
    return pltpu.roll(values, HD, 1)


def twice(values, head):
    wide = values.astype(jnp.float32)
    low = lane_iota(wide.shape) < HD
    other = other_head(wide)
    both = jnp.where(low, wide, other) if head == 0 else jnp.where(low, other, wide)
    return both.astype(values.dtype)


def apart(values):
    wide = values.astype(jnp.float32)
    low = lane_iota(wide.shape) < HD
    zero = jnp.zeros_like(wide)
    return jnp.concatenate(
        [jnp.where(low, wide, zero), jnp.where(low, zero, wide)], axis=0
    ).astype(values.dtype)


def heads_kernel(raw_ref, cos_ref, sin_ref, q_gain_ref, k_gain_ref, q_ref, kv_ref):
    pair = 2 * HD
    q_cols = q_ref.shape[1]
    k_cols = kv_ref.shape[1] // 2
    cos, sin = cos_ref[...], sin_ref[...]
    for first in range(0, q_cols + k_cols, pair):
        values = raw_ref[:, first : first + pair]
        gain = q_gain_ref[...] if first < q_cols else k_gain_ref[...]
        normed = values * lax.rsqrt(head_means(values * values) + NORM_EPS) * gain
        turned = (normed * cos + half_swap(normed) * sin).astype(jnp.bfloat16)
        if first < q_cols:
            q_ref[:, first : first + pair] = turned
        else:
            kv_ref[:, first - q_cols : first - q_cols + pair] = turned
    kv_ref[:, k_cols:] = raw_ref[:, q_cols + k_cols :].astype(jnp.bfloat16)


def make_heads(raw, cos_wide, sin_wide, q_gain, k_gain, q_cols, k_cols):
    rows = raw.shape[0]
    return pl.pallas_call(
        heads_kernel,
        out_shape=(
            jax.ShapeDtypeStruct((rows, q_cols), jnp.bfloat16),
            jax.ShapeDtypeStruct((rows, 2 * k_cols), jnp.bfloat16),
        ),
        cost_estimate=pl.CostEstimate(
            flops=rows * raw.shape[1] * 400, bytes_accessed=rows * raw.shape[1] * 7, transcendentals=0
        ),
        name="make_heads",
    )(raw, cos_wide, sin_wide, q_gain, k_gain)


def turn_back(grad, values, gain, cos, sin):
    turned = grad * cos - half_swap(grad) * sin
    scale = lax.rsqrt(head_means(values * values) + NORM_EPS)
    unit = values * scale
    scaled = turned * gain
    return scale * (scaled - unit * head_means(scaled * unit)), turned * unit


def fill_bias(starts_ref, low_ref, high_ref, bias_ref, piece):
    low, high = low_ref[0], high_ref[0]
    for i in range(bias_ref.shape[0] // piece):
        place = starts_ref[i] + lax.broadcasted_iota(jnp.int32, (piece, low.shape[1]), 0)
        linked = (place >= low) & (place <= high)
        bias = jnp.where(linked, 0.0, MASKED)
        bias_ref[i * piece : (i + 1) * piece, : low.shape[1]] = bias
        bias_ref[i * piece : (i + 1) * piece, low.shape[1] :] = bias


def attend_kernel(places, blocks, block_keys, skip, *refs):
    starts_ref, low_ref, high_ref = refs[:3]
    q_refs = refs[3 : 3 + places]
    kv_refs = refs[3 + places : 3 + places + blocks * places]
    refs = refs[3 + places + blocks * places + skip :]
    out_refs = refs[:places]
    total_ref, bias_ref, key_ref, value_ref = refs[places:]
    pair = 2 * HD
    piece, q_cols = q_refs[0].shape
    rows = places * piece
    k_cols = kv_refs[0].shape[1] // 2
    k_heads = k_cols // HD
    group = q_cols // k_cols
    scale = math.log2(math.e) / math.sqrt(HD)
    fill_bias(starts_ref, low_ref, high_ref, bias_ref, piece)
    for block in range(blocks):
        mine = kv_refs[block * places : (block + 1) * places]
        for head in range(k_heads):
            cols = slice(head // 2 * pair, head // 2 * pair + pair)
            vcols = slice(k_cols + head // 2 * pair, k_cols + head // 2 * pair + pair)
            where = slice(block * block_keys, (block + 1) * block_keys)
            keys = jnp.concatenate([ref[:, cols] for ref in mine], axis=0)
            key_ref[head, where, :] = twice(keys, head % 2)
            if head % 2 == 0:
                values = jnp.concatenate([ref[:, vcols] for ref in mine], axis=0)
                value_ref[head // 2, :, where] = values.astype(jnp.float32).T.astype(jnp.bfloat16)
    for first in range(0, q_cols, pair):
        head = first // HD // group
        queries = apart(jnp.concatenate([q_ref[:, first : first + pair] for q_ref in q_refs], axis=0))

        mixed = jnp.zeros((HD, 2 * rows), jnp.float32)
        total = jnp.zeros((1, 2 * rows), jnp.float32)
        for block in range(blocks):
            where = slice(block * block_keys, (block + 1) * block_keys)
            scores = matmul_nt(key_ref[head, where, :], queries)
            weight = jnp.exp2(scores * scale + bias_ref[where, :])
            total = total + jnp.sum(weight, axis=0, keepdims=True)
            values = value_ref[head // 2, head % 2 * HD : (head % 2 + 1) * HD, where]
            mixed = mixed + matmul(values, weight.astype(jnp.bfloat16))
        mixed = mixed / total
        out = jnp.concatenate([mixed[:, :rows], mixed[:, rows:]], axis=0).T.astype(jnp.bfloat16)
        for place in range(places):
            out_refs[place][:, first : first + pair] = out[place * piece : (place + 1) * piece]
        total_ref[0, first // pair, :] = jnp.log2(total)[0]


def attend(starts, low, high, q_chunks, kv_blocks, batch, part, parts, before):
    places, blocks = len(q_chunks), len(kv_blocks)
    kv_flat = [kv for block in kv_blocks for kv in block]
    count = batch // parts
    base = part * count
    rows, q_cols = q_chunks[0].shape
    piece = rows // batch
    kv_cols = kv_flat[0].shape[1]
    k_cols = kv_cols // 2
    keys = blocks * places * piece
    q_rows = places * piece
    pairs = q_cols // (2 * HD)
    q_spec = pl.BlockSpec((piece, q_cols), lambda b: (base + b, 0))
    kv_spec = pl.BlockSpec((piece, kv_cols), lambda b: (base + b, 0))
    line_spec = pl.BlockSpec((1, 1, q_rows), lambda b: (base + b, 0, 0))
    work = count * q_cols // HD * q_rows * keys
    results = pl.pallas_call(
        functools.partial(attend_kernel, places, blocks, places * piece, len(before)),
        grid=(count,),
        out_shape=tuple(
            [jax.ShapeDtypeStruct((rows, q_cols), jnp.bfloat16)] * places
            + [jax.ShapeDtypeStruct((batch, pairs, 2 * q_rows), jnp.float32)]
        ),
        in_specs=[
            pl.BlockSpec(memory_space=pltpu.SMEM),
            line_spec,
            pl.BlockSpec((1, 1, q_rows), lambda b: (0, 0, 0)),
        ]
        + [q_spec] * places
        + [kv_spec] * len(kv_flat)
        + [pl.BlockSpec(memory_space=pl.ANY)] * len(before),
        out_specs=tuple(
            [q_spec] * places + [pl.BlockSpec((1, pairs, 2 * q_rows), lambda b: (base + b, 0, 0))]
        ),
        input_output_aliases={3 + places + len(kv_flat) + i: i for i in range(len(before))},
        scratch_shapes=[
            pltpu.VMEM((keys, 2 * q_rows), jnp.float32),
            pltpu.VMEM((k_cols // HD, keys, 2 * HD), jnp.bfloat16),
            pltpu.VMEM((k_cols // HD // 2, 2 * HD, keys), jnp.bfloat16),
        ],
        cost_estimate=pl.CostEstimate(
            flops=work * 4 * HD * 4, bytes_accessed=count * q_rows * q_cols * 8, transcendentals=work
        ),
        name="attend",
    )(starts, low, high, *q_chunks, *kv_flat, *before)
    return list(results)


def attend_back_kernel(places, blocks, block_keys, *refs):
    starts_ref, low_ref, high_ref, total_ref, cos_ref, sin_ref, gain_ref = refs[:7]
    refs = refs[7:]
    q_refs, refs = refs[:places], refs[places:]
    raw_refs, refs = refs[:places], refs[places:]
    grad_refs, refs = refs[:places], refs[places:]
    mixed_refs, refs = refs[:places], refs[places:]
    kv_refs, refs = refs[: blocks * places], refs[blocks * places :]
    dq_ref, refs = refs[0], refs[1:]
    dkv_refs, refs = refs[:blocks], refs[blocks:]
    gain_sum_ref, bias_ref, key_ref, turned_ref, value_ref, dkey_ref, dvalue_ref = refs
    pair = 2 * HD
    piece, q_cols = q_refs[0].shape
    rows = places * piece
    k_cols = kv_refs[0].shape[1] // 2
    k_heads = k_cols // HD
    group = q_cols // k_cols
    inv_root = 1.0 / math.sqrt(HD)
    scale = math.log2(math.e) * inv_root
    fill_bias(starts_ref, low_ref, high_ref, bias_ref, piece)

    @pl.when(pl.program_id(0) == 0)
    def _():
        gain_sum_ref[...] = jnp.zeros_like(gain_sum_ref)

    for block in range(blocks):
        mine = kv_refs[block * places : (block + 1) * places]
        for head in range(k_heads):
            cols = slice(head // 2 * pair, head // 2 * pair + pair)
            vcols = slice(k_cols + head // 2 * pair, k_cols + head // 2 * pair + pair)
            where = slice(block * block_keys, (block + 1) * block_keys)
            keys = jnp.concatenate([ref[:, cols] for ref in mine], axis=0)
            values = jnp.concatenate([ref[:, vcols] for ref in mine], axis=0)
            key_ref[head, where, :] = twice(keys, head % 2)
            value_ref[head, where, :] = twice(values, head % 2)
            if head % 2 == 0:
                turned_ref[head // 2, :, where] = keys.astype(jnp.float32).T.astype(jnp.bfloat16)
    for first in range(0, q_cols, pair):
        head = first // HD // group
        fresh = first % (group * HD) == 0
        queries = apart(jnp.concatenate([q_ref[:, first : first + pair] for q_ref in q_refs], axis=0))
        grads = apart(jnp.concatenate([g_ref[:, first : first + pair] for g_ref in grad_refs], axis=0))
        total = total_ref[0, first // pair : first // pair + 1, :]

        mixed = apart(jnp.concatenate([m_ref[:, first : first + pair] for m_ref in mixed_refs], axis=0))
        delta = jnp.sum((grads.astype(jnp.float32) * mixed.astype(jnp.float32)).T, axis=0, keepdims=True)
        dquery = jnp.zeros((HD, 2 * rows), jnp.float32)
        for block in range(blocks):
            where = slice(block * block_keys, (block + 1) * block_keys)
            scores = matmul_nt(key_ref[head, where, :], queries)
            dprob = matmul_nt(value_ref[head, where, :], grads)
            prob = jnp.exp2(scores * scale + bias_ref[where, :] - total)
            dscore = (prob * (dprob - delta)).astype(jnp.bfloat16)
            dvalue = matmul(prob.astype(jnp.bfloat16), grads)
            dkey = matmul(dscore, queries)
            if fresh:
                dvalue_ref[head, where, :] = dvalue
                dkey_ref[head, where, :] = dkey
            else:
                dvalue_ref[head, where, :] += dvalue
                dkey_ref[head, where, :] += dkey
            keys = turned_ref[head // 2, head % 2 * HD : (head % 2 + 1) * HD, where]
            dquery = dquery + matmul(keys, dscore)
        dquery = dquery * inv_root
        dquery = jnp.concatenate([dquery[:, :rows], dquery[:, rows:]], axis=0).T
        raw = jnp.concatenate([raw_ref[:, first : first + pair] for raw_ref in raw_refs], axis=0)
        dq, addend = turn_back(
            dquery, raw, gain_ref[...], cos_ref[...].reshape(rows, pair), sin_ref[...].reshape(rows, pair)
        )
        gain_sum_ref[...] += jnp.sum(addend.reshape(-1, 8, pair), axis=0)
        dq_ref[:, :, first : first + pair] = dq.reshape(places, piece, pair).astype(jnp.bfloat16)
    low = lane_iota((block_keys, pair)) < HD
    for block in range(blocks):
        where = slice(block * block_keys, (block + 1) * block_keys)
        for first in range(0, k_heads, 2):
            for shift, ref, factor in ((0, dkey_ref, inv_root), (k_cols, dvalue_ref, 1.0)):
                one, two = ref[first, where, :], ref[first + 1, where, :]
                sums = jnp.where(low, one + other_head(one), two + other_head(two)) * factor
                cols = slice(shift + first // 2 * pair, shift + first // 2 * pair + pair)
                dkv_refs[block][:, :, cols] = sums.reshape(places, piece, pair).astype(
                    dkv_refs[block].dtype
                )


def attend_back(
    starts,
    low,
    high,
    totals,
    cos_wide,
    sin_wide,
    q_gain,
    q_chunks,
    raw_chunks,
    grad_chunks,
    mixed_chunks,
    kv_blocks,
    kinds,
    batch,
    part,
    parts,
):
    places, blocks = len(q_chunks), len(kv_blocks)
    kv_flat = [kv for block in kv_blocks for kv in block]
    count = batch // parts
    base = part * count
    rows, q_cols = q_chunks[0].shape
    piece = rows // batch
    kv_cols = kv_flat[0].shape[1]
    k_cols = kv_cols // 2
    keys = blocks * places * piece
    q_rows = places * piece
    pairs = q_cols // (2 * HD)
    k_heads = k_cols // HD
    q_spec = pl.BlockSpec((piece, q_cols), lambda b: (base + b, 0))
    kv_spec = pl.BlockSpec((piece, kv_cols), lambda b: (base + b, 0))
    line_spec = pl.BlockSpec((1, 1, q_rows), lambda b: (base + b, 0, 0))
    turn_spec = pl.BlockSpec((places, piece, 2 * HD), lambda b: (0, base + b, 0))
    work = count * q_cols // HD * q_rows * keys
    results = pl.pallas_call(
        functools.partial(attend_back_kernel, places, blocks, places * piece),
        grid=(count,),
        out_shape=tuple(
            [jax.ShapeDtypeStruct((places, rows // parts, q_cols), jnp.bfloat16)]
            + [jax.ShapeDtypeStruct((places, rows // parts, kv_cols), kind) for kind in kinds]
            + [jax.ShapeDtypeStruct((8, 2 * HD), jnp.float32)]
        ),
        in_specs=[
            pl.BlockSpec(memory_space=pltpu.SMEM),
            line_spec,
            pl.BlockSpec((1, 1, q_rows), lambda b: (0, 0, 0)),
            pl.BlockSpec((1, pairs, 2 * q_rows), lambda b: (base + b, 0, 0)),
            turn_spec,
            turn_spec,
            pl.BlockSpec((1, 2 * HD), lambda b: (0, 0)),
        ]
        + [q_spec] * (4 * places)
        + [kv_spec] * len(kv_flat),
        out_specs=tuple(
            [pl.BlockSpec((places, piece, q_cols), lambda b: (0, b, 0))]
            + [pl.BlockSpec((places, piece, kv_cols), lambda b: (0, b, 0))] * blocks
            + [pl.BlockSpec((8, 2 * HD), lambda b: (0, 0))]
        ),
        scratch_shapes=[
            pltpu.VMEM((keys, 2 * q_rows), jnp.float32),
            pltpu.VMEM((k_heads, keys, 2 * HD), jnp.bfloat16),
            pltpu.VMEM((k_heads // 2, 2 * HD, keys), jnp.bfloat16),
            pltpu.VMEM((k_heads, keys, 2 * HD), jnp.bfloat16),
            pltpu.VMEM((k_heads, keys, 2 * HD), jnp.float32),
            pltpu.VMEM((k_heads, keys, 2 * HD), jnp.float32),
        ],
        cost_estimate=pl.CostEstimate(
            flops=work * 10 * HD * 4, bytes_accessed=count * q_rows * q_cols * 16, transcendentals=work
        ),
        name="attend_back",
    )(
        starts,
        low,
        high,
        totals,
        cos_wide,
        sin_wide,
        q_gain,
        *q_chunks,
        *raw_chunks,
        *grad_chunks,
        *mixed_chunks,
        *kv_flat,
    )
    return results[0], list(results[1:-1]), results[-1]


def heads_back_kernel(places, parts, q_cols, *refs):
    dq_refs, refs = refs[:parts], refs[parts:]
    own_refs, refs = refs[:parts], refs[parts:]
    came_refs, refs = refs[:parts], refs[parts:]
    raw_refs, refs = refs[:places], refs[places:]
    cos_ref, sin_ref, gain_ref, out_ref, gain_sum_ref = refs
    rows = raw_refs[0].shape[0]
    part_rows = rows // parts
    k_cols = own_refs[0].shape[2] // 2
    pair = 2 * HD
    addends = jnp.zeros((8, pair), jnp.float32)
    for place in range(places):
        for part in range(parts):
            mine = slice(part * part_rows, (part + 1) * part_rows)
            out = slice(place * rows + part * part_rows, place * rows + (part + 1) * part_rows)
            out_ref[out, :q_cols] = dq_refs[part][place]
            grads = own_refs[part][place] + came_refs[part][place].astype(jnp.float32)
            for first in range(0, k_cols, pair):
                cols = slice(first, first + pair)
                dk, addend = turn_back(
                    grads[:, cols],
                    raw_refs[place][mine, cols],
                    gain_ref[...],
                    cos_ref[place, mine],
                    sin_ref[place, mine],
                )
                out_ref[out, q_cols + first : q_cols + first + pair] = dk.astype(jnp.bfloat16)
                addends = addends + jnp.sum(addend.reshape(-1, 8, pair), axis=0)
            out_ref[out, q_cols + k_cols :] = grads[:, k_cols:].astype(jnp.bfloat16)
    gain_sum_ref[...] = addends


def heads_back(dq_parts, own_parts, came_parts, raw_chunks, cos_wide, sin_wide, k_gain):
    parts, places = len(dq_parts), len(raw_chunks)
    rows = raw_chunks[0].shape[0]
    q_cols, kv_cols = dq_parts[0].shape[2], own_parts[0].shape[2]
    k_cols = kv_cols // 2

    def whole(array):
        return pl.BlockSpec(array.shape, lambda i: (0,) * array.ndim)

    inputs = [*dq_parts, *own_parts, *came_parts]
    turns = [cos_wide, sin_wide, k_gain]
    return pl.pallas_call(
        functools.partial(heads_back_kernel, places, parts, q_cols),
        grid=(1,),
        out_shape=(
            jax.ShapeDtypeStruct((places * rows, q_cols + kv_cols), jnp.bfloat16),
            jax.ShapeDtypeStruct((8, 2 * HD), jnp.float32),
        ),
        in_specs=[whole(array) for array in inputs]
        + [pl.BlockSpec((rows, k_cols), lambda i: (0, q_cols // k_cols))] * places
        + [whole(array) for array in turns],
        out_specs=(
            pl.BlockSpec((places * rows, q_cols + kv_cols), lambda i: (0, 0)),
            pl.BlockSpec((8, 2 * HD), lambda i: (0, 0)),
        ),
        cost_estimate=pl.CostEstimate(
            flops=places * rows * kv_cols * 400, bytes_accessed=places * rows * 4096, transcendentals=0
        ),
        name="heads_back",
    )(*inputs, *raw_chunks, *turns)


def feed_kernel(count, *refs):
    hidden_refs, grad_refs = refs[:count], refs[count : 2 * count]
    gate_ref, up_ref, down_ref, act_ref, dgate_ref, dup_ref, hidden, grads = refs[2 * count :]

    @pl.when(pl.program_id(0) == 0)
    def _():
        rows = hidden_refs[0].shape[0]
        for i in range(count):
            hidden[i * rows : (i + 1) * rows, :] = hidden_refs[i][...]
            grads[i * rows : (i + 1) * rows, :] = grad_refs[i][...]

    gate = matmul(hidden[...], gate_ref[...])
    up = matmul(hidden[...], up_ref[...])
    grad = matmul(grads[...], down_ref[...])
    sigmoid = 1.0 / (1.0 + jnp.exp(-gate))
    silu = gate * sigmoid
    act_ref[...] = (silu * up).astype(jnp.bfloat16)
    dgate_ref[...] = (grad * up * sigmoid * (1.0 + gate * (1.0 - sigmoid))).astype(jnp.bfloat16)
    dup_ref[...] = (grad * silu).astype(jnp.bfloat16)


def feed_rows(hidden_rows, grad_rows, gate, up, down_t, cols):
    count = len(hidden_rows)
    rows, width = hidden_rows[0].shape
    total = count * rows
    tile = min(cols, 512 if count == 1 else 256)
    steps = cols // tile
    row_spec = pl.BlockSpec((rows, width), lambda j: (0, 0))
    out_spec = pl.BlockSpec((total, tile), lambda j: (0, j))

    def weight_spec(weight):
        return pl.BlockSpec((width, tile), lambda j: (0, weight[1] * steps + j))

    return pl.pallas_call(
        functools.partial(feed_kernel, count),
        grid=(steps,),
        out_shape=tuple([jax.ShapeDtypeStruct((total, cols), jnp.bfloat16)] * 3),
        in_specs=[row_spec] * (2 * count)
        + [
            weight_spec(gate),
            weight_spec(up),
            weight_spec(down_t),
        ],
        out_specs=tuple([out_spec] * 3),
        scratch_shapes=[pltpu.VMEM((total, width), jnp.bfloat16)] * 2,
        cost_estimate=pl.CostEstimate(
            flops=6 * total * width * cols,
            bytes_accessed=6 * width * cols + 4 * total * width + 6 * total * cols,
            transcendentals=total * cols,
        ),
        name="feed_rows",
    )(*hidden_rows, *grad_rows, gate[0], up[0], down_t[0])


def fill_rows(parts, whole):
    row = 0
    for line in parts:
        col = 0
        for ref in line:
            rows, cols = ref.shape
            whole[row : row + rows, col : col + cols] = ref[...]
            col += cols
        row += rows


def rows_nt_kernel(layouts, *refs):
    count = len(layouts)
    parts = []
    for lines, cols in layouts:
        parts.append([refs[i * cols : (i + 1) * cols] for i in range(lines)])
        refs = refs[lines * cols :]
    weight_refs, out_refs, wholes = refs[:count], refs[count:-count], refs[-count:]

    @pl.when(pl.program_id(0) == 0)
    def _():
        for part, whole in zip(parts, wholes):
            fill_rows(part, whole)

    result = matmul_nt(wholes[0][...], weight_refs[0][...])
    for weight_ref, whole in zip(weight_refs[1:], wholes[1:]):
        result = result + matmul_nt(whole[...], weight_ref[...])
    rows = out_refs[0].shape[0]
    for i, out_ref in enumerate(out_refs):
        out_ref[...] = result[i * rows : (i + 1) * rows].astype(out_ref.dtype)


def rows_nt(addends, kind, outs, rows_each, tile=512):
    layouts, parts, depths = [], [], []
    for lines, _ in addends:
        layouts.append((len(lines), len(lines[0])))
        parts.extend(part for line in lines for part in line)
        depths.append(sum(part[0].shape[1] for part in lines[0]))
    rows = rows_each * len(addends[0][0])
    weights = [weight for _, weight in addends]
    width = weights[0][0].shape[0]

    def part_spec(part):
        return pl.BlockSpec((rows_each, part[0].shape[1]), lambda j: (part[1], 0))

    def weight_spec(weight, depth):
        return pl.BlockSpec((tile, depth), lambda j: (j, weight[1]))

    results = pl.pallas_call(
        functools.partial(rows_nt_kernel, layouts),
        grid=(width // tile,),
        out_shape=tuple([jax.ShapeDtypeStruct((rows // outs, width), kind)] * outs),
        in_specs=[part_spec(part) for part in parts]
        + [weight_spec(weight, depth) for weight, depth in zip(weights, depths)],
        out_specs=tuple([pl.BlockSpec((rows // outs, tile), lambda j: (0, j))] * outs),
        scratch_shapes=[pltpu.VMEM((rows, depth), jnp.bfloat16) for depth in depths],
        cost_estimate=pl.CostEstimate(
            flops=2 * rows * sum(depths) * width,
            bytes_accessed=2 * sum(depths) * (rows + width) + 2 * rows * width,
            transcendentals=0,
        ),
        name="rows_nt",
    )(*[part[0] for part in parts], *[weight[0] for weight in weights])
    return list(results)


def add_kernel(one_ref, two_ref, out_ref):
    out_ref[...] = (one_ref[...].astype(jnp.float32) + two_ref[...].astype(jnp.float32)).astype(
        out_ref.dtype
    )


def add_rows(one, two, tile=1024):
    rows, cols = one.shape
    spec = pl.BlockSpec((rows, tile), lambda j: (0, j))
    return pl.pallas_call(
        add_kernel,
        grid=(cols // tile,),
        out_shape=jax.ShapeDtypeStruct(one.shape, one.dtype),
        in_specs=[spec, spec],
        out_specs=spec,
        cost_estimate=pl.CostEstimate(flops=rows * cols, bytes_accessed=6 * rows * cols, transcendentals=0),
        name="add_rows",
    )(one, two)


def split_kernel(rows_ref, weight_ref, *out_refs):
    result = matmul(rows_ref[...], weight_ref[...]).astype(jnp.bfloat16)
    for i, out_ref in enumerate(out_refs):

        @pl.when(pl.program_id(0) == i)
        def _():
            out_ref[...] = result


def split_columns(rows, weight, first, count, cols):
    total, depth = rows.shape
    return pl.pallas_call(
        split_kernel,
        grid=(count,),
        out_shape=tuple([jax.ShapeDtypeStruct((total, cols), jnp.bfloat16)] * count),
        in_specs=[
            pl.BlockSpec((total, depth), lambda j: (0, 0)),
            pl.BlockSpec((depth, cols), lambda j: (0, first + j)),
        ],
        out_specs=tuple([pl.BlockSpec((total, cols), lambda j: (0, 0))] * count),
        cost_estimate=pl.CostEstimate(
            flops=2 * total * depth * cols * count,
            bytes_accessed=2 * (total * depth + depth * cols * count + total * cols * count),
            transcendentals=0,
        ),
        name="split_columns",
    )(rows, weight)


def product_kernel(left_count, right_counts, blocks, first_ref, *refs):
    left_refs, refs = refs[:left_count], refs[left_count:]
    rights = []
    for count in right_counts:
        rights.append(refs[:count])
        refs = refs[count:]
    out_ref, left, right = refs
    steps = pl.num_programs(0) // len(rights)

    @pl.when(pl.program_id(0) == 0)
    def _():
        if blocks:
            cols = left.shape[1] // blocks
            row = 0
            for ref in left_refs:
                rows = ref.shape[0]
                for i in range(blocks):
                    start = pl.multiple_of((2 * i + first_ref[0]) * cols, cols)
                    left[row : row + rows, i * cols : (i + 1) * cols] = ref[:, pl.ds(start, cols)]
                row += rows
        else:
            fill_rows([[ref] for ref in left_refs], left)

    for i, refs in enumerate(rights):

        @pl.when(pl.program_id(0) // steps == i)
        def _():
            fill_rows([[ref] for ref in refs], right)

    out_ref[...] = matmul_tn(left[...], right[...]).astype(jnp.bfloat16)


def product(left, rights, tile=512, first=None, blocks=0):
    width, cols = left[0].shape[1], rights[0][0].shape[1]
    depth = sum(part.shape[0] for part in left)
    tile = min(tile, cols)
    steps = cols // tile
    out_rows = width // 2 if blocks else width
    first = jnp.zeros((1,), jnp.int32) if first is None else first

    def right_spec(part, index):
        return pl.BlockSpec(
            (part.shape[0], tile), lambda j: (0, jnp.clip(j - index * steps, 0, steps - 1))
        )

    return pl.pallas_call(
        functools.partial(product_kernel, len(left), [len(parts) for parts in rights], blocks),
        grid=(steps * len(rights),),
        out_shape=jax.ShapeDtypeStruct((out_rows, cols * len(rights)), jnp.bfloat16),
        in_specs=[pl.BlockSpec(memory_space=pltpu.SMEM)]
        + [pl.BlockSpec(part.shape, lambda j: (0, 0)) for part in left]
        + [right_spec(part, index) for index, parts in enumerate(rights) for part in parts],
        out_specs=pl.BlockSpec((out_rows, tile), lambda j: (0, j)),
        scratch_shapes=[
            pltpu.VMEM((depth, out_rows), jnp.bfloat16),
            pltpu.VMEM((depth, tile), jnp.bfloat16),
        ],
        cost_estimate=pl.CostEstimate(
            flops=2 * depth * out_rows * cols * len(rights),
            bytes_accessed=2 * (depth * width + (depth + out_rows) * cols * len(rights)),
            transcendentals=0,
        ),
        name="product",
    )(first, *left, *[part for parts in rights for part in parts])


def unit_of(values):
    scale = lax.rsqrt(jnp.mean(values * values, axis=-1, keepdims=True) + NORM_EPS)
    return values * scale, scale


def norm_kernel(rows_ref, more_ref, sum_ref, unit_ref):
    values = rows_ref[...].astype(jnp.float32) + more_ref[...]
    sum_ref[...] = values
    unit_ref[...] = unit_of(values)[0].astype(jnp.bfloat16)


def add_and_norm(rows, more, tile=64):
    count, width = rows.shape
    spec = pl.BlockSpec((tile, width), lambda i: (i, 0))
    return pl.pallas_call(
        norm_kernel,
        grid=(count // tile,),
        out_shape=(
            jax.ShapeDtypeStruct(rows.shape, jnp.float32),
            jax.ShapeDtypeStruct(rows.shape, jnp.bfloat16),
        ),
        in_specs=[spec, spec],
        out_specs=(spec, spec),
        cost_estimate=pl.CostEstimate(
            flops=5 * count * width, bytes_accessed=12 * count * width, transcendentals=0
        ),
        name="add_and_norm",
    )(rows, more)


def norm_back_kernel(one_ref, two_ref, rows_ref, base_ref, *out_refs):
    scaled = one_ref[...].astype(jnp.float32) + two_ref[...].astype(jnp.float32)
    unit, scale = unit_of(rows_ref[...].astype(jnp.float32))
    result = base_ref[...].astype(jnp.float32) + scale * (
        scaled - unit * jnp.mean(scaled * unit, axis=-1, keepdims=True)
    )
    for out_ref in out_refs:
        out_ref[...] = result.astype(out_ref.dtype)


def norm_back(one, two, rows, base, kinds, tile=64):
    count, width = rows.shape
    spec = pl.BlockSpec((tile, width), lambda i: (i, 0))
    return pl.pallas_call(
        norm_back_kernel,
        grid=(count // tile,),
        out_shape=tuple(jax.ShapeDtypeStruct(rows.shape, kind) for kind in kinds),
        in_specs=[spec] * 4,
        out_specs=tuple([spec] * len(kinds)),
        cost_estimate=pl.CostEstimate(
            flops=10 * count * width, bytes_accessed=14 * count * width, transcendentals=0
        ),
        name="norm_back",
    )(one, two, rows, base)


def per_device(
    block_in,
    segments,
    positions,
    attention_gain,
    query_weight,
    key_weight,
    value_weight,
    query_gain,
    key_gain,
    output_weight,
    hidden_gain,
    gate_weight,
    up_weight,
    down_weight,
    cotangent,
):
    tp_count = lax.axis_size("tp")
    tp_index = lax.axis_index("tp")
    ctx_index = lax.axis_index(CTX)
    batch, own_rows, width = block_in.shape
    rows = batch * own_rows
    ctx_rows = own_rows * tp_count
    places = range(tp_count)
    order = [*range(1, tp_count), 0]
    masks = ctx_masks()
    q_cols = query_weight.shape[1]
    k_cols = key_weight.shape[1]
    qkv_cols = q_cols + 2 * k_cols
    hidden_cols = gate_weight.shape[1]
    q_gain = jnp.tile(query_gain.astype(jnp.float32), 2)[None]
    k_gain = jnp.tile(key_gain.astype(jnp.float32), 2)[None]

    block = width // (lax.axis_size("dp") * lax.axis_size(CTX))
    paired = block % 128 == 0
    pair_first = lax.rem(ctx_index, 2).astype(jnp.int32)[None]

    def meet(arrays):
        return [*arrays, *[ctx_swap(array, 1) for array in arrays]] if paired else list(arrays)

    def grad_product(left, rights, tile=512):
        return product(left, rights, tile, pair_first, width // block // 2 if paired else 0)

    def scatter_sum(addend):
        axes = ("dp", CTX[0]) if paired else ("dp", *CTX)
        return lax.psum_scatter(addend, axes, scatter_dimension=0, tiled=True)

    back_places = [(tp_count - place) % tp_count for place in places]
    attention_rows = attention_gain.astype(jnp.float32)[:, None]
    hidden_gain_rows = hidden_gain.astype(jnp.float32)[:, None]
    qkv_weight = jnp.concatenate([query_weight, key_weight, value_weight], axis=1).astype(jnp.float32)
    first_weight = jnp.concatenate(
        [
            (gate_weight.astype(jnp.float32) * hidden_gain_rows).astype(jnp.bfloat16),
            (qkv_weight * attention_rows).astype(jnp.bfloat16),
        ],
        axis=1,
    )
    full_first = gather_weight(first_weight)
    full_qkv = full_first[:, hidden_cols:]

    def chunk_start(place):
        owner = lax.rem(tp_index - place + tp_count, tp_count)
        return owner * own_rows

    def own_part(table, start):
        return lax.dynamic_slice_in_dim(table, start, own_rows, 1)

    iota = jnp.arange(own_rows, dtype=jnp.int32)
    row_starts = [ctx_index * ctx_rows + chunk_start(place) for place in places]
    low = jnp.concatenate([own_part(segments, start) for start in row_starts], axis=1)[:, None]
    high = jnp.concatenate([start + iota for start in row_starts])[None, None]
    starts = jnp.stack(
        [
            jnp.bitwise_xor(ctx_index, mask) * ctx_rows + chunk_start(place)
            for mask in masks
            for place in places
        ]
    ).astype(jnp.int32)
    position = jnp.stack([own_part(positions, start).reshape(rows) for start in row_starts])
    half = HD // 2
    frequency = ROPE_BASE ** (-2.0 * jnp.arange(half, dtype=jnp.float32) / HD)
    sign = jnp.where(jnp.arange(2 * HD) % HD < half, -1.0, 1.0).astype(jnp.float32)
    angles = position.astype(jnp.float32)[..., None] * jnp.tile(frequency, 4)
    cos_wide, sin_wide = jnp.cos(angles), jnp.sin(angles) * sign

    def project(place):
        values = matmul(normed_rows[place], full_qkv)
        query_rot, kv = make_heads(
            values, cos_wide[place], sin_wide[place], q_gain, k_gain, q_cols, k_cols
        )
        return values, query_rot, kv

    def project_and_send(place):
        values, query_rot, kv = project(place)
        blocks = ctx_gather(kv)
        return values, query_rot, blocks

    tokens = block_in.reshape(rows, width)
    normed = unit_of(tokens.astype(jnp.float32))[0].astype(jnp.bfloat16)
    normed, out_own = together(normed, output_weight.T)
    normed_rows, heads = [normed], []
    out_pieces = [out_own]
    for _ in range(1, tp_count):
        out_pieces.append(shift(out_pieces[-1], -1))
    for place in range(1, tp_count):
        came = ring_hop(normed_rows[-1])
        ready = range(tp_count - 2) if place == tp_count - 1 else []
        work = [project_and_send(mine) for mine in ready]
        came, work = together(came, work)
        if place == 1:
            came, out_pieces = together(came, out_pieces)
            second_weight = jnp.concatenate(
                [*out_pieces, (up_weight.astype(jnp.float32) * hidden_gain_rows).astype(jnp.bfloat16)],
                axis=1,
            )
            full_second = gather_weight(second_weight)
        heads.extend(work)
        normed_rows.append(came)
    last_weight, normed_rows[-1] = together(down_weight.T, normed_rows[-1])
    full_down_t = gather_weight(last_weight)
    full_out, full_gate, full_up, full_down = (full_second, 0), (full_first, 0), (full_second, 1), (full_down_t, 0)

    grad_own, normed_rows[-1] = together(cotangent.reshape(rows, width), normed_rows[-1])
    came = ring_hop(grad_own)
    work = [project_and_send(mine) for mine in range(len(heads), tp_count)]
    came, work = together(came, work)
    heads.extend(work)
    raw, queries, gathered = ([h[i] for h in heads] for i in range(3))
    blocks = [[gathered[place][i] for place in places] for i in range(len(masks))]
    grad_rows = [grad_own, came]
    attended = []
    parts = 2
    late_qkv = full_qkv
    came = ring_hop(grad_rows[-1])
    for part in range(parts):
        attended = attend(starts, low, high, queries, blocks, batch, part, parts, attended)
        if part == 0:
            late_qkv, attended = together(late_qkv, attended)
    came, attended = together(came, attended)
    grad_rows.append(came)
    attended_rows, totals = attended[:tp_count], attended[tp_count]
    mine = [attended_rows[0]] + [shift(attended_rows[place], -place) for place in range(1, tp_count)]
    grad_rows[-1], mine = together(grad_rows[-1], mine)
    for _ in range(len(grad_rows), tp_count):
        grad_rows.append(ring_hop(grad_rows[-1]))
    met_grads = meet(grad_rows)
    (mixed_in,) = rows_nt([([[(piece, 0) for piece in mine]], full_out)], jnp.float32, 1, rows)
    met_mine = [meet([piece]) for piece in mine]
    hidden, unit_hidden = add_and_norm(tokens, mixed_in)

    def feed(group):
        return feed_rows(
            [hidden_rows[place] for place in group],
            [grad_rows[place] for place in group],
            full_gate,
            full_up,
            full_down,
            hidden_cols,
        )

    def hidden_terms(fed):
        halves = range(tp_count // 2)
        gates, ups = ([[(fed[part], half)] for half in halves] for part in (1, 2))
        return rows_nt([(gates, full_gate), (ups, full_up)], jnp.bfloat16, len(halves), rows)

    first, second = list(places)[: tp_count // 2], list(places)[tp_count // 2 :]
    hidden_rows = [unit_hidden]
    fed_first, terms_first = None, None
    for place in range(1, tp_count):
        came = ring_hop(hidden_rows[-1])
        if place == len(first):
            fed_first = feed(first)
            came, fed_first, met_grads, met_mine = together(came, fed_first, met_grads, met_mine)
        if place == len(first) + 1:
            met_first = [meet([fed]) for fed in fed_first]
            terms_first = hidden_terms(fed_first)
            came, terms_first, met_first = together(came, terms_first, met_first)
        hidden_rows.append(came)

    came = ring_hop(terms_first[1])
    met_hidden = meet(hidden_rows)
    fed_second = feed(second)
    feed_terms = rows_nt([([[(fed_first[0], 1)]], full_down)], jnp.bfloat16, 1, rows)
    came, fed_second, met_hidden, feed_terms = together(came, fed_second, met_hidden, feed_terms)
    feed_came = ring_hop(feed_terms[0])
    met_fed = [old + meet([fed]) for old, fed in zip(met_first, fed_second)]
    if paired:
        met_fed = [[fed[0], fed[2], fed[1], fed[3]] for fed in met_fed]
    terms_second, feed_came = together(hidden_terms(fed_second), feed_came)
    came = ring_hop(add_rows(came, terms_second[0]))
    down_product = grad_product(met_grads, [met_fed[0]])
    came, down_product = together(came, down_product)
    came = ring_hop(add_rows(came, terms_second[1]))
    down_shard = scatter_sum(down_product)
    gate_product = grad_product(met_hidden, [met_fed[1]])
    lines = [[(fed_second[0], 0)], [(fed_second[0], 1)], [(fed_first[0], 0)]]
    feed_rest = rows_nt([(lines, full_down)], jnp.bfloat16, len(lines), rows)
    came, gate_product, feed_rest = together(came, gate_product, feed_rest)
    feed_terms = dict(zip(order, feed_terms + feed_rest))
    gate_shard = scatter_sum(gate_product)

    grad_hidden, branch = norm_back(
        came, terms_first[0], hidden, grad_own, (jnp.float32, jnp.bfloat16)
    )
    pieces = split_columns(branch, full_second, 0, tp_count, q_cols)
    grad_att = [pieces[0]] + [shift(pieces[place], place) for place in range(1, tp_count)]
    met_branch = meet([branch])
    up_product = grad_product(met_hidden, [met_fed[2]])
    out_product = grad_product(met_branch, met_mine)
    grad_att, out_product, up_product = together(grad_att, out_product, up_product)
    out_shard = scatter_sum(out_product)

    kinds = [jnp.float32] * (len(masks) // 2) + [jnp.bfloat16] * (len(masks) - len(masks) // 2)
    query_gain_sum = jnp.zeros((8, 2 * HD), jnp.float32)
    dq_parts, own_parts, came_parts = [], [], []
    came = feed_came
    for step, place in enumerate(order[1:]):
        if place:
            came = ring_hop(add_rows(came, feed_terms[place]))
        if step < 2:
            dq, back, addend = attend_back(
                starts,
                low,
                high,
                totals,
                cos_wide,
                sin_wide,
                q_gain,
                queries,
                raw,
                grad_att,
                attended_rows,
                blocks,
                kinds,
                batch,
                step,
                2,
            )
            if step == 0:
                came, dq, back, addend, grad_att, down_shard = together(
                    came, dq, back, addend, grad_att, down_shard
                )
            else:
                dq, back, addend, own_parts, came_parts = together(
                    dq, back, addend, own_parts, came_parts
                )
            query_gain_sum = query_gain_sum + addend
            dq_parts.append(dq)
            bit = 1
            while len(back) > 2:
                half_count = len(back) // 2
                back = [
                    back[i] + ctx_swap(back[half_count + i].astype(jnp.bfloat16), bit).astype(jnp.float32)
                    for i in range(half_count)
                ]
                bit *= 2
            own_parts.append(back[0])
            came_parts.append(ctx_swap(back[1].astype(jnp.bfloat16), bit))
        else:
            grad_qkv, key_gain_sum = heads_back(
                dq_parts, own_parts, came_parts, raw, cos_wide, sin_wide, k_gain
            )
            came, grad_qkv, gate_shard = together(came, grad_qkv, gate_shard)
    feed_out = came.astype(jnp.float32) + feed_terms[0].astype(jnp.float32)
    block_out = (hidden + feed_out).astype(jnp.bfloat16).reshape(block_in.shape)

    def out_hop(total, place):
        start = back_places[place] * q_cols
        total = ring_hop(total).astype(jnp.float32) + out_shard[:, start : start + q_cols].astype(
            jnp.float32
        )
        return total.astype(jnp.bfloat16) if place else total

    row_terms = rows_nt(
        [([[(grad_qkv, place)] for place in places], (late_qkv, 0))], jnp.bfloat16, tp_count, rows
    )
    up_shard = scatter_sum(up_product)
    head_sums = jnp.stack([query_gain_sum, key_gain_sum]).sum(axis=1).reshape(2, 2, HD).sum(axis=1)
    total = row_terms[1]
    for step, place in enumerate(order[1:]):
        came = ring_hop(total)
        if step == 0:
            head_sums = all_sum(head_sums, (CTX, "dp"))
            qkv_product = product(normed_rows, [[grad_qkv]], grad_qkv.shape[1])
            came, head_sums, out_shard, qkv_product = together(came, head_sums, out_shard, qkv_product)
            qkv_shard = lax.psum_scatter(qkv_product, ("dp", *CTX), scatter_dimension=0, tiled=True)
            out_total = out_shard[:, back_places[1] * q_cols : (back_places[1] + 1) * q_cols]
        else:
            out_total = out_hop(out_total, order[step])
            came, out_total = together(came, out_total)
        if step == 1:
            came, up_shard = together(came, up_shard)
        if place:
            total = add_rows(came, row_terms[place])
    out_total = out_hop(out_total, 0)
    qkv_sums = qkv_shard.astype(jnp.float32)
    gate_sums, up_sums = gate_shard.astype(jnp.float32), up_shard.astype(jnp.float32)
    attention_sum = jnp.sum(qkv_sums * qkv_weight, axis=1)
    hidden_sums = jnp.sum(
        gate_sums * gate_weight.astype(jnp.float32) + up_sums * up_weight.astype(jnp.float32), axis=1
    )
    small_sums = jnp.concatenate([jnp.stack([attention_sum, hidden_sums]), head_sums], axis=1)
    small_sums = all_sum(small_sums, ("tp",))
    attention_gain_grad, hidden_gain_grad = small_sums[0, :block], small_sums[1, :block]
    head_sums = small_sums[:, block:]
    (input_grad,) = norm_back(came, row_terms[0], tokens, grad_hidden, (jnp.float32,))
    output_grad = out_total.T
    down_grad = down_shard.astype(jnp.float32).T
    gate_grad, up_grad = gate_sums * hidden_gain_rows, up_sums * hidden_gain_rows
    qkv_grad = qkv_sums * attention_rows
    return (
        block_out,
        input_grad.reshape(block_in.shape),
        attention_gain_grad,
        qkv_grad[:, :q_cols],
        qkv_grad[:, q_cols : q_cols + k_cols],
        qkv_grad[:, q_cols + k_cols :],
        head_sums[0],
        head_sums[1],
        output_grad,
        hidden_gain_grad,
        gate_grad,
        up_grad,
        down_grad,
    )


def solution(mesh):
    in_specs = (
        P(None, ("dp", *CTX, "tp"), None),
        P(None, "dp"),
        P(None, "dp"),
        P(("dp", *CTX)),
        P(("dp", *CTX), "tp"),
        P(("dp", *CTX), "tp"),
        P(("dp", *CTX), "tp"),
        P(),
        P(),
        P("tp", ("dp", *CTX)),
        P(("dp", *CTX)),
        P(("dp", *CTX), "tp"),
        P(("dp", *CTX), "tp"),
        P("tp", ("dp", *CTX)),
        P(None, ("dp", *CTX, "tp"), None),
    )
    out_specs = (
        P(None, ("dp", *CTX, "tp"), None),
        P(None, ("dp", *CTX, "tp"), None),
        P(("dp", *CTX)),
        P(("dp", *CTX), "tp"),
        P(("dp", *CTX), "tp"),
        P(("dp", *CTX), "tp"),
        P(),
        P(),
        P("tp", ("dp", *CTX)),
        P(("dp", *CTX)),
        P(("dp", *CTX), "tp"),
        P(("dp", *CTX), "tp"),
        P("tp", ("dp", *CTX)),
    )
    shape = (mesh.shape["dp"], mesh.shape["ctx"] // 2, 2, mesh.shape["tp"])
    split = Mesh(mesh.devices.reshape(shape), ("dp", *CTX, "tp"))
    return jax.shard_map(
        per_device, mesh=split, in_specs=in_specs, out_specs=out_specs, check_vma=False
    )
```

```python
import functools
import math

import jax
import jax.numpy as jnp
from jax import lax
from jax.experimental import pallas as pl
from jax.experimental.pallas import tpu as pltpu
from jax.sharding import Mesh
from jax.sharding import PartitionSpec as P

D = 2048
HD = 64


NORM_EPS = 1e-05
ROPE_BASE = 1000000.0
MASKED = -1e30
CTX = ("ctx_pair", "ctx_place")


def matmul(left_mat, right_mat):
    return jnp.dot(left_mat, right_mat, preferred_element_type=jnp.float32)


def matmul_tn(left_mat, right_mat):
    return lax.dot_general(
        left_mat, right_mat, (((0,), (0,)), ((), ())), preferred_element_type=jnp.float32
    )


def matmul_nt(left_mat, right_mat):
    return lax.dot_general(
        left_mat, right_mat, (((1,), (1,)), ((), ())), preferred_element_type=jnp.float32
    )


def ring_hop(values):
    count = lax.axis_size("tp")
    return lax.ppermute(values, "tp", [(i, (i + 1) % count) for i in range(count)])


def ctx_swap(values, mask):
    count = lax.axis_size(CTX)
    return lax.ppermute(values, CTX, [(i, i ^ mask) for i in range(count)])


def ctx_masks():
    masks = [0]
    bit = lax.axis_size(CTX) // 2
    while bit:
        masks = masks + [mask ^ bit for mask in masks]
        bit //= 2
    return masks


def ctx_gather(own):
    blocks = [own]
    bit = lax.axis_size(CTX) // 2
    while bit:
        blocks = blocks + [ctx_swap(block, bit) for block in blocks]
        bit //= 2
    return blocks


def gather_weight(shard):
    return lax.all_gather(shard, ("dp", *CTX), axis=0, tiled=True)


def all_sum(values, axes):
    for axis in axes:
        count = lax.axis_size(axis)
        bit = 1
        while bit < count:
            values = values + lax.ppermute(values, axis, [(i, i ^ bit) for i in range(count)])
            bit *= 2
    return values


def shift(values, places):
    count = lax.axis_size("tp")
    return lax.ppermute(values, "tp", [(i, (i + places) % count) for i in range(count)])


def together(*values):
    return lax.optimization_barrier(values)


def lane_iota(shape):
    return lax.broadcasted_iota(jnp.int32, shape, 1)


def head_means(values):
    width = values.shape[1]
    row = lax.broadcasted_iota(jnp.int32, (width, width), 0) // HD
    col = lax.broadcasted_iota(jnp.int32, (width, width), 1) // HD
    pick = jnp.where(row == col, 1.0 / HD, 0.0).astype(jnp.float32)
    return jnp.dot(
        values, pick, precision=lax.Precision.HIGHEST, preferred_element_type=jnp.float32
    )


def half_swap(values):
    width, half = values.shape[1], HD // 2
    first = lax.rem(lane_iota(values.shape), HD) < half
    return jnp.where(
        first, pltpu.roll(values, width - half, 1), pltpu.roll(values, half, 1)
    )


def other_head(values):
    return pltpu.roll(values, HD, 1)


def twice(values, head):
    wide = values.astype(jnp.float32)
    low = lane_iota(wide.shape) < HD
    other = other_head(wide)
    both = jnp.where(low, wide, other) if head == 0 else jnp.where(low, other, wide)
    return both.astype(values.dtype)


def apart(values):
    wide = values.astype(jnp.float32)
    low = lane_iota(wide.shape) < HD
    zero = jnp.zeros_like(wide)
    return jnp.concatenate(
        [jnp.where(low, wide, zero), jnp.where(low, zero, wide)], axis=0
    ).astype(values.dtype)


def heads_kernel(raw_ref, cos_ref, sin_ref, q_gain_ref, k_gain_ref, q_ref, kv_ref):
    pair = 2 * HD
    q_cols = q_ref.shape[1]
    k_cols = kv_ref.shape[1] // 2
    cos, sin = cos_ref[...], sin_ref[...]
    for first in range(0, q_cols + k_cols, pair):
        values = raw_ref[:, first : first + pair]
        gain = q_gain_ref[...] if first < q_cols else k_gain_ref[...]
        normed = values * lax.rsqrt(head_means(values * values) + NORM_EPS) * gain
        turned = (normed * cos + half_swap(normed) * sin).astype(jnp.bfloat16)
        if first < q_cols:
            q_ref[:, first : first + pair] = turned
        else:
            kv_ref[:, first - q_cols : first - q_cols + pair] = turned
    kv_ref[:, k_cols:] = raw_ref[:, q_cols + k_cols :].astype(jnp.bfloat16)


def make_heads(raw, cos_wide, sin_wide, q_gain, k_gain, q_cols, k_cols):
    rows = raw.shape[0]
    return pl.pallas_call(
        heads_kernel,
        out_shape=(
            jax.ShapeDtypeStruct((rows, q_cols), jnp.bfloat16),
            jax.ShapeDtypeStruct((rows, 2 * k_cols), jnp.bfloat16),
        ),
        cost_estimate=pl.CostEstimate(
            flops=rows * raw.shape[1] * 400, bytes_accessed=rows * raw.shape[1] * 7, transcendentals=0
        ),
        name="make_heads",
    )(raw, cos_wide, sin_wide, q_gain, k_gain)


def turn_back(grad, values, gain, cos, sin):
    turned = grad * cos - half_swap(grad) * sin
    scale = lax.rsqrt(head_means(values * values) + NORM_EPS)
    unit = values * scale
    scaled = turned * gain
    return scale * (scaled - unit * head_means(scaled * unit)), turned * unit


def fill_bias(starts_ref, low_ref, high_ref, bias_ref, piece):
    low, high = low_ref[0], high_ref[0]
    for i in range(bias_ref.shape[0] // piece):
        place = starts_ref[i] + lax.broadcasted_iota(jnp.int32, (piece, low.shape[1]), 0)
        linked = (place >= low) & (place <= high)
        bias = jnp.where(linked, 0.0, MASKED)
        bias_ref[i * piece : (i + 1) * piece, : low.shape[1]] = bias
        bias_ref[i * piece : (i + 1) * piece, low.shape[1] :] = bias


def attend_kernel(places, blocks, block_keys, *refs):
    starts_ref, low_ref, high_ref = refs[:3]
    q_refs = refs[3 : 3 + places]
    kv_refs = refs[3 + places : 3 + places + blocks * places]
    refs = refs[3 + places + blocks * places :]
    out_refs = refs[:places]
    total_ref, bias_ref, key_ref, value_ref = refs[places:]
    pair = 2 * HD
    piece, q_cols = q_refs[0].shape
    rows = places * piece
    k_cols = kv_refs[0].shape[1] // 2
    k_heads = k_cols // HD
    group = q_cols // k_cols
    scale = math.log2(math.e) / math.sqrt(HD)
    fill_bias(starts_ref, low_ref, high_ref, bias_ref, piece)
    for block in range(blocks):
        mine = kv_refs[block * places : (block + 1) * places]
        for head in range(k_heads):
            cols = slice(head // 2 * pair, head // 2 * pair + pair)
            vcols = slice(k_cols + head // 2 * pair, k_cols + head // 2 * pair + pair)
            where = slice(block * block_keys, (block + 1) * block_keys)
            keys = jnp.concatenate([ref[:, cols] for ref in mine], axis=0)
            key_ref[head, where, :] = twice(keys, head % 2)
            if head % 2 == 0:
                values = jnp.concatenate([ref[:, vcols] for ref in mine], axis=0)
                value_ref[head // 2, :, where] = values.astype(jnp.float32).T.astype(jnp.bfloat16)
    for first in range(0, q_cols, pair):
        head = first // HD // group
        queries = apart(jnp.concatenate([q_ref[:, first : first + pair] for q_ref in q_refs], axis=0))

        mixed = jnp.zeros((HD, 2 * rows), jnp.float32)
        total = jnp.zeros((1, 2 * rows), jnp.float32)
        for block in range(blocks):
            where = slice(block * block_keys, (block + 1) * block_keys)
            scores = matmul_nt(key_ref[head, where, :], queries)
            weight = jnp.exp2(scores * scale + bias_ref[where, :])
            total = total + jnp.sum(weight, axis=0, keepdims=True)
            values = value_ref[head // 2, head % 2 * HD : (head % 2 + 1) * HD, where]
            mixed = mixed + matmul(values, weight.astype(jnp.bfloat16))
        mixed = mixed / total
        out = jnp.concatenate([mixed[:, :rows], mixed[:, rows:]], axis=0).T.astype(jnp.bfloat16)
        for place in range(places):
            out_refs[place][:, first : first + pair] = out[place * piece : (place + 1) * piece]
        total_ref[0, first // pair, :] = jnp.log2(total)[0]


def attend(starts, low, high, q_chunks, kv_blocks, batch):
    places, blocks = len(q_chunks), len(kv_blocks)
    kv_flat = [kv for block in kv_blocks for kv in block]
    rows, q_cols = q_chunks[0].shape
    piece = rows // batch
    kv_cols = kv_flat[0].shape[1]
    k_cols = kv_cols // 2
    keys = blocks * places * piece
    q_rows = places * piece
    pairs = q_cols // (2 * HD)
    q_spec = pl.BlockSpec((piece, q_cols), lambda b: (b, 0))
    kv_spec = pl.BlockSpec((piece, kv_cols), lambda b: (b, 0))
    line_spec = pl.BlockSpec((1, 1, q_rows), lambda b: (b, 0, 0))
    work = batch * q_cols // HD * q_rows * keys
    results = pl.pallas_call(
        functools.partial(attend_kernel, places, blocks, places * piece),
        grid=(batch,),
        out_shape=tuple(
            [jax.ShapeDtypeStruct((rows, q_cols), jnp.bfloat16)] * places
            + [jax.ShapeDtypeStruct((batch, pairs, 2 * q_rows), jnp.float32)]
        ),
        in_specs=[
            pl.BlockSpec(memory_space=pltpu.SMEM),
            line_spec,
            pl.BlockSpec((1, 1, q_rows), lambda b: (0, 0, 0)),
        ]
        + [q_spec] * places
        + [kv_spec] * len(kv_flat),
        out_specs=tuple(
            [q_spec] * places + [pl.BlockSpec((1, pairs, 2 * q_rows), lambda b: (b, 0, 0))]
        ),
        scratch_shapes=[
            pltpu.VMEM((keys, 2 * q_rows), jnp.float32),
            pltpu.VMEM((k_cols // HD, keys, 2 * HD), jnp.bfloat16),
            pltpu.VMEM((k_cols // HD // 2, 2 * HD, keys), jnp.bfloat16),
        ],
        cost_estimate=pl.CostEstimate(
            flops=work * 4 * HD * 4, bytes_accessed=batch * q_rows * q_cols * 8, transcendentals=work
        ),
        name="attend",
    )(starts, low, high, *q_chunks, *kv_flat)
    return list(results)


def attend_back_kernel(places, blocks, block_keys, *refs):
    starts_ref, low_ref, high_ref, total_ref, cos_ref, sin_ref, gain_ref = refs[:7]
    refs = refs[7:]
    q_refs, refs = refs[:places], refs[places:]
    raw_refs, refs = refs[:places], refs[places:]
    grad_refs, refs = refs[:places], refs[places:]
    mixed_refs, refs = refs[:places], refs[places:]
    kv_refs, refs = refs[: blocks * places], refs[blocks * places :]
    dq_ref, refs = refs[0], refs[1:]
    dkv_refs, refs = refs[:blocks], refs[blocks:]
    gain_sum_ref, bias_ref, key_ref, turned_ref, value_ref, dkey_ref, dvalue_ref = refs
    pair = 2 * HD
    piece, q_cols = q_refs[0].shape
    rows = places * piece
    k_cols = kv_refs[0].shape[1] // 2
    k_heads = k_cols // HD
    group = q_cols // k_cols
    inv_root = 1.0 / math.sqrt(HD)
    scale = math.log2(math.e) * inv_root
    fill_bias(starts_ref, low_ref, high_ref, bias_ref, piece)

    @pl.when(pl.program_id(0) == 0)
    def _():
        gain_sum_ref[...] = jnp.zeros_like(gain_sum_ref)

    for block in range(blocks):
        mine = kv_refs[block * places : (block + 1) * places]
        for head in range(k_heads):
            cols = slice(head // 2 * pair, head // 2 * pair + pair)
            vcols = slice(k_cols + head // 2 * pair, k_cols + head // 2 * pair + pair)
            where = slice(block * block_keys, (block + 1) * block_keys)
            keys = jnp.concatenate([ref[:, cols] for ref in mine], axis=0)
            values = jnp.concatenate([ref[:, vcols] for ref in mine], axis=0)
            key_ref[head, where, :] = twice(keys, head % 2)
            value_ref[head, where, :] = twice(values, head % 2)
            if head % 2 == 0:
                turned_ref[head // 2, :, where] = keys.astype(jnp.float32).T.astype(jnp.bfloat16)
    for first in range(0, q_cols, pair):
        head = first // HD // group
        fresh = first % (group * HD) == 0
        queries = apart(jnp.concatenate([q_ref[:, first : first + pair] for q_ref in q_refs], axis=0))
        grads = apart(jnp.concatenate([g_ref[:, first : first + pair] for g_ref in grad_refs], axis=0))
        total = total_ref[0, first // pair : first // pair + 1, :]

        mixed = apart(jnp.concatenate([m_ref[:, first : first + pair] for m_ref in mixed_refs], axis=0))
        delta = jnp.sum((grads.astype(jnp.float32) * mixed.astype(jnp.float32)).T, axis=0, keepdims=True)
        dquery = jnp.zeros((HD, 2 * rows), jnp.float32)
        for block in range(blocks):
            where = slice(block * block_keys, (block + 1) * block_keys)
            scores = matmul_nt(key_ref[head, where, :], queries)
            dprob = matmul_nt(value_ref[head, where, :], grads)
            prob = jnp.exp2(scores * scale + bias_ref[where, :] - total)
            dscore = (prob * (dprob - delta)).astype(jnp.bfloat16)
            dvalue = matmul(prob.astype(jnp.bfloat16), grads)
            dkey = matmul(dscore, queries)
            if fresh:
                dvalue_ref[head, where, :] = dvalue
                dkey_ref[head, where, :] = dkey
            else:
                dvalue_ref[head, where, :] += dvalue
                dkey_ref[head, where, :] += dkey
            keys = turned_ref[head // 2, head % 2 * HD : (head % 2 + 1) * HD, where]
            dquery = dquery + matmul(keys, dscore)
        dquery = dquery * inv_root
        dquery = jnp.concatenate([dquery[:, :rows], dquery[:, rows:]], axis=0).T
        raw = jnp.concatenate([raw_ref[:, first : first + pair] for raw_ref in raw_refs], axis=0)
        dq, addend = turn_back(
            dquery, raw, gain_ref[...], cos_ref[...].reshape(rows, pair), sin_ref[...].reshape(rows, pair)
        )
        gain_sum_ref[...] += jnp.sum(addend.reshape(-1, 8, pair), axis=0)
        dq_ref[:, :, first : first + pair] = dq.reshape(places, piece, pair).astype(jnp.bfloat16)
    low = lane_iota((block_keys, pair)) < HD
    for block in range(blocks):
        where = slice(block * block_keys, (block + 1) * block_keys)
        for first in range(0, k_heads, 2):
            for shift, ref, factor in ((0, dkey_ref, inv_root), (k_cols, dvalue_ref, 1.0)):
                one, two = ref[first, where, :], ref[first + 1, where, :]
                sums = jnp.where(low, one + other_head(one), two + other_head(two)) * factor
                cols = slice(shift + first // 2 * pair, shift + first // 2 * pair + pair)
                dkv_refs[block][:, :, cols] = sums.reshape(places, piece, pair).astype(
                    dkv_refs[block].dtype
                )


def attend_back(
    starts,
    low,
    high,
    totals,
    cos_wide,
    sin_wide,
    q_gain,
    q_chunks,
    raw_chunks,
    grad_chunks,
    mixed_chunks,
    kv_blocks,
    kinds,
    batch,
    base,
    count,
):
    places, blocks = len(q_chunks), len(kv_blocks)
    kv_flat = [kv for block in kv_blocks for kv in block]
    rows, q_cols = q_chunks[0].shape
    piece = rows // batch
    kv_cols = kv_flat[0].shape[1]
    k_cols = kv_cols // 2
    keys = blocks * places * piece
    q_rows = places * piece
    pairs = q_cols // (2 * HD)
    k_heads = k_cols // HD
    q_spec = pl.BlockSpec((piece, q_cols), lambda b: (base + b, 0))
    kv_spec = pl.BlockSpec((piece, kv_cols), lambda b: (base + b, 0))
    line_spec = pl.BlockSpec((1, 1, q_rows), lambda b: (base + b, 0, 0))
    turn_spec = pl.BlockSpec((places, piece, 2 * HD), lambda b: (0, base + b, 0))
    work = count * q_cols // HD * q_rows * keys
    results = pl.pallas_call(
        functools.partial(attend_back_kernel, places, blocks, places * piece),
        grid=(count,),
        out_shape=tuple(
            [jax.ShapeDtypeStruct((places, count * piece, q_cols), jnp.bfloat16)]
            + [jax.ShapeDtypeStruct((places, count * piece, kv_cols), kind) for kind in kinds]
            + [jax.ShapeDtypeStruct((8, 2 * HD), jnp.float32)]
        ),
        in_specs=[
            pl.BlockSpec(memory_space=pltpu.SMEM),
            line_spec,
            pl.BlockSpec((1, 1, q_rows), lambda b: (0, 0, 0)),
            pl.BlockSpec((1, pairs, 2 * q_rows), lambda b: (base + b, 0, 0)),
            turn_spec,
            turn_spec,
            pl.BlockSpec((1, 2 * HD), lambda b: (0, 0)),
        ]
        + [q_spec] * (4 * places)
        + [kv_spec] * len(kv_flat),
        out_specs=tuple(
            [pl.BlockSpec((places, piece, q_cols), lambda b: (0, b, 0))]
            + [pl.BlockSpec((places, piece, kv_cols), lambda b: (0, b, 0))] * blocks
            + [pl.BlockSpec((8, 2 * HD), lambda b: (0, 0))]
        ),
        scratch_shapes=[
            pltpu.VMEM((keys, 2 * q_rows), jnp.float32),
            pltpu.VMEM((k_heads, keys, 2 * HD), jnp.bfloat16),
            pltpu.VMEM((k_heads // 2, 2 * HD, keys), jnp.bfloat16),
            pltpu.VMEM((k_heads, keys, 2 * HD), jnp.bfloat16),
            pltpu.VMEM((k_heads, keys, 2 * HD), jnp.float32),
            pltpu.VMEM((k_heads, keys, 2 * HD), jnp.float32),
        ],
        cost_estimate=pl.CostEstimate(
            flops=work * 10 * HD * 4, bytes_accessed=count * q_rows * q_cols * 16, transcendentals=work
        ),
        name="attend_back",
    )(
        starts,
        low,
        high,
        totals,
        cos_wide,
        sin_wide,
        q_gain,
        *q_chunks,
        *raw_chunks,
        *grad_chunks,
        *mixed_chunks,
        *kv_flat,
    )
    return results[0], list(results[1:-1]), results[-1]


def heads_back_kernel(places, came_counts, q_cols, *refs):
    parts = len(came_counts)
    dq_refs, refs = refs[:parts], refs[parts:]
    own_refs, refs = refs[:parts], refs[parts:]
    came_refs = []
    for count in came_counts:
        came_refs.append(refs[:count])
        refs = refs[count:]
    raw_refs, refs = refs[:places], refs[places:]
    cos_ref, sin_ref, gain_ref, out_ref, gain_sum_ref = refs
    rows = raw_refs[0].shape[0]
    k_cols = own_refs[0].shape[2] // 2
    pair = 2 * HD
    addends = jnp.zeros((8, pair), jnp.float32)
    for place in range(places):
        start = 0
        for part in range(parts):
            stop = start + own_refs[part].shape[1]
            mine = slice(start, stop)
            out = slice(place * rows + start, place * rows + stop)
            start = stop
            out_ref[out, :q_cols] = dq_refs[part][place]
            grads = own_refs[part][place]
            for came_ref in came_refs[part]:
                grads = grads + came_ref[place].astype(jnp.float32)
            for first in range(0, k_cols, pair):
                cols = slice(first, first + pair)
                dk, addend = turn_back(
                    grads[:, cols],
                    raw_refs[place][mine, cols],
                    gain_ref[...],
                    cos_ref[place, mine],
                    sin_ref[place, mine],
                )
                out_ref[out, q_cols + first : q_cols + first + pair] = dk.astype(jnp.bfloat16)
                addends = addends + jnp.sum(addend.reshape(-1, 8, pair), axis=0)
            out_ref[out, q_cols + k_cols :] = grads[:, k_cols:].astype(jnp.bfloat16)
    gain_sum_ref[...] = addends


def heads_back(dq_parts, own_parts, came_parts, raw_chunks, cos_wide, sin_wide, k_gain):
    parts, places = len(dq_parts), len(raw_chunks)
    rows = raw_chunks[0].shape[0]
    q_cols, kv_cols = dq_parts[0].shape[2], own_parts[0].shape[2]
    k_cols = kv_cols // 2

    def whole(array):
        return pl.BlockSpec(array.shape, lambda i: (0,) * array.ndim)

    inputs = [*dq_parts, *own_parts, *[came for part in came_parts for came in part]]
    turns = [cos_wide, sin_wide, k_gain]
    return pl.pallas_call(
        functools.partial(heads_back_kernel, places, [len(part) for part in came_parts], q_cols),
        grid=(1,),
        out_shape=(
            jax.ShapeDtypeStruct((places * rows, q_cols + kv_cols), jnp.bfloat16),
            jax.ShapeDtypeStruct((8, 2 * HD), jnp.float32),
        ),
        in_specs=[whole(array) for array in inputs]
        + [pl.BlockSpec((rows, k_cols), lambda i: (0, q_cols // k_cols))] * places
        + [whole(array) for array in turns],
        out_specs=(
            pl.BlockSpec((places * rows, q_cols + kv_cols), lambda i: (0, 0)),
            pl.BlockSpec((8, 2 * HD), lambda i: (0, 0)),
        ),
        cost_estimate=pl.CostEstimate(
            flops=places * rows * kv_cols * 400, bytes_accessed=places * rows * 4096, transcendentals=0
        ),
        name="heads_back",
    )(*inputs, *raw_chunks, *turns)


def feed_kernel(count, *refs):
    hidden_refs, grad_refs = refs[:count], refs[count : 2 * count]
    gate_ref, up_ref, down_ref, act_ref, dgate_ref, dup_ref, hidden, grads = refs[2 * count :]

    @pl.when(pl.program_id(0) == 0)
    def _():
        rows = hidden_refs[0].shape[0]
        for i in range(count):
            hidden[i * rows : (i + 1) * rows, :] = hidden_refs[i][...]
            grads[i * rows : (i + 1) * rows, :] = grad_refs[i][...]

    gate = matmul(hidden[...], gate_ref[...])
    up = matmul(hidden[...], up_ref[...])
    grad = matmul(grads[...], down_ref[...])
    sigmoid = 1.0 / (1.0 + jnp.exp(-gate))
    silu = gate * sigmoid
    act_ref[...] = (silu * up).astype(jnp.bfloat16)
    dgate_ref[...] = (grad * up * sigmoid * (1.0 + gate * (1.0 - sigmoid))).astype(jnp.bfloat16)
    dup_ref[...] = (grad * silu).astype(jnp.bfloat16)


def feed_rows(hidden_rows, grad_rows, gate, up, down_t, cols):
    count = len(hidden_rows)
    rows, width = hidden_rows[0].shape
    total = count * rows
    tile = min(cols, 512 if count == 1 else 256)
    steps = cols // tile
    row_spec = pl.BlockSpec((rows, width), lambda j: (0, 0))
    out_spec = pl.BlockSpec((total, tile), lambda j: (0, j))

    def weight_spec(weight):
        return pl.BlockSpec((width, tile), lambda j: (0, weight[1] * steps + j))

    return pl.pallas_call(
        functools.partial(feed_kernel, count),
        grid=(steps,),
        out_shape=tuple([jax.ShapeDtypeStruct((total, cols), jnp.bfloat16)] * 3),
        in_specs=[row_spec] * (2 * count)
        + [
            weight_spec(gate),
            weight_spec(up),
            weight_spec(down_t),
        ],
        out_specs=tuple([out_spec] * 3),
        scratch_shapes=[pltpu.VMEM((total, width), jnp.bfloat16)] * 2,
        cost_estimate=pl.CostEstimate(
            flops=6 * total * width * cols,
            bytes_accessed=6 * width * cols + 4 * total * width + 6 * total * cols,
            transcendentals=total * cols,
        ),
        name="feed_rows",
    )(*hidden_rows, *grad_rows, gate[0], up[0], down_t[0])


def fill_rows(parts, whole):
    row = 0
    for line in parts:
        col = 0
        for ref in line:
            rows, cols = ref.shape
            whole[row : row + rows, col : col + cols] = ref[...]
            col += cols
        row += rows


def rows_nt_kernel(layouts, *refs):
    count = len(layouts)
    parts = []
    for lines, cols in layouts:
        parts.append([refs[i * cols : (i + 1) * cols] for i in range(lines)])
        refs = refs[lines * cols :]
    weight_refs, out_refs, wholes = refs[:count], refs[count:-count], refs[-count:]

    @pl.when(pl.program_id(0) == 0)
    def _():
        for part, whole in zip(parts, wholes):
            fill_rows(part, whole)

    result = matmul_nt(wholes[0][...], weight_refs[0][...])
    for weight_ref, whole in zip(weight_refs[1:], wholes[1:]):
        result = result + matmul_nt(whole[...], weight_ref[...])
    rows = out_refs[0].shape[0]
    for i, out_ref in enumerate(out_refs):
        out_ref[...] = result[i * rows : (i + 1) * rows].astype(out_ref.dtype)


def rows_nt(addends, kind, outs, rows_each, tile=512):
    layouts, parts, depths = [], [], []
    for lines, _ in addends:
        layouts.append((len(lines), len(lines[0])))
        parts.extend(part for line in lines for part in line)
        depths.append(sum(part[0].shape[1] for part in lines[0]))
    rows = rows_each * len(addends[0][0])
    weights = [weight for _, weight in addends]
    width = weights[0][0].shape[0]

    def part_spec(part):
        return pl.BlockSpec((rows_each, part[0].shape[1]), lambda j: (part[1], 0))

    def weight_spec(weight, depth):
        return pl.BlockSpec((tile, depth), lambda j: (j, weight[1]))

    results = pl.pallas_call(
        functools.partial(rows_nt_kernel, layouts),
        grid=(width // tile,),
        out_shape=tuple([jax.ShapeDtypeStruct((rows // outs, width), kind)] * outs),
        in_specs=[part_spec(part) for part in parts]
        + [weight_spec(weight, depth) for weight, depth in zip(weights, depths)],
        out_specs=tuple([pl.BlockSpec((rows // outs, tile), lambda j: (0, j))] * outs),
        scratch_shapes=[pltpu.VMEM((rows, depth), jnp.bfloat16) for depth in depths],
        cost_estimate=pl.CostEstimate(
            flops=2 * rows * sum(depths) * width,
            bytes_accessed=2 * sum(depths) * (rows + width) + 2 * rows * width,
            transcendentals=0,
        ),
        name="rows_nt",
    )(*[part[0] for part in parts], *[weight[0] for weight in weights])
    return list(results)


def add_kernel(one_ref, two_ref, out_ref):
    out_ref[...] = (one_ref[...].astype(jnp.float32) + two_ref[...].astype(jnp.float32)).astype(
        out_ref.dtype
    )


def add_rows(one, two, tile=1024):
    rows, cols = one.shape
    spec = pl.BlockSpec((rows, tile), lambda j: (0, j))
    return pl.pallas_call(
        add_kernel,
        grid=(cols // tile,),
        out_shape=jax.ShapeDtypeStruct(one.shape, one.dtype),
        in_specs=[spec, spec],
        out_specs=spec,
        cost_estimate=pl.CostEstimate(flops=rows * cols, bytes_accessed=6 * rows * cols, transcendentals=0),
        name="add_rows",
    )(one, two)


def split_kernel(rows_ref, weight_ref, *out_refs):
    result = matmul(rows_ref[...], weight_ref[...]).astype(jnp.bfloat16)
    for i, out_ref in enumerate(out_refs):

        @pl.when(pl.program_id(0) == i)
        def _():
            out_ref[...] = result


def split_columns(rows, weight, first, count, cols):
    total, depth = rows.shape
    return pl.pallas_call(
        split_kernel,
        grid=(count,),
        out_shape=tuple([jax.ShapeDtypeStruct((total, cols), jnp.bfloat16)] * count),
        in_specs=[
            pl.BlockSpec((total, depth), lambda j: (0, 0)),
            pl.BlockSpec((depth, cols), lambda j: (0, first + j)),
        ],
        out_specs=tuple([pl.BlockSpec((total, cols), lambda j: (0, 0))] * count),
        cost_estimate=pl.CostEstimate(
            flops=2 * total * depth * cols * count,
            bytes_accessed=2 * (total * depth + depth * cols * count + total * cols * count),
            transcendentals=0,
        ),
        name="split_columns",
    )(rows, weight)


def product_kernel(left_count, right_counts, blocks, skip, first_ref, *refs):
    left_refs, refs = refs[:left_count], refs[left_count:]
    rights = []
    for count in right_counts:
        rights.append(refs[:count])
        refs = refs[count:]
    out_ref, left, right = refs[skip:]
    steps = pl.num_programs(0) // len(rights)

    @pl.when(pl.program_id(0) == 0)
    def _():
        if blocks:
            cols = left.shape[1] // blocks
            row = 0
            for ref in left_refs:
                rows = ref.shape[0]
                for i in range(blocks):
                    start = pl.multiple_of((2 * i + first_ref[0]) * cols, cols)
                    left[row : row + rows, i * cols : (i + 1) * cols] = ref[:, pl.ds(start, cols)]
                row += rows
        else:
            fill_rows([[ref] for ref in left_refs], left)

    for i, refs in enumerate(rights):

        @pl.when(pl.program_id(0) // steps == i)
        def _():
            fill_rows([[ref] for ref in refs], right)

    out_ref[...] = matmul_tn(left[...], right[...]).astype(jnp.bfloat16)


def product(left, rights, tile=512, first=None, blocks=0, more=0, into=None, share=1.0):
    width, cols = left[0].shape[1], rights[0][0].shape[1]
    depth = sum(part.shape[0] for part in left)
    tile = min(tile, cols)
    steps = cols // tile
    out_rows = width // 2 if blocks else width
    first = jnp.zeros((1,), jnp.int32) if first is None else first
    taken = [] if into is None else [into]
    out_cols = into.shape[1] if taken else cols * (len(rights) + more)
    skipped = out_cols // tile - steps * len(rights) if taken else 0
    operands = 1 + len(left) + sum(len(parts) for parts in rights)

    def right_spec(part, index):
        return pl.BlockSpec(
            (part.shape[0], tile), lambda j: (0, jnp.clip(j - index * steps, 0, steps - 1))
        )

    return pl.pallas_call(
        functools.partial(
            product_kernel, len(left), [len(parts) for parts in rights], blocks, len(taken)
        ),
        grid=(steps * len(rights),),
        out_shape=jax.ShapeDtypeStruct((out_rows, out_cols), jnp.bfloat16),
        in_specs=[pl.BlockSpec(memory_space=pltpu.SMEM)]
        + [pl.BlockSpec(part.shape, lambda j: (0, 0)) for part in left]
        + [right_spec(part, index) for index, parts in enumerate(rights) for part in parts]
        + [pl.BlockSpec(memory_space=pl.ANY)] * len(taken),
        out_specs=pl.BlockSpec((out_rows, tile), lambda j: (0, skipped + j)),
        input_output_aliases={operands: 0} if taken else {},
        scratch_shapes=[
            pltpu.VMEM((depth, out_rows), jnp.bfloat16),
            pltpu.VMEM((depth, tile), jnp.bfloat16),
        ],
        cost_estimate=pl.CostEstimate(
            flops=int(share * 2 * depth * out_rows * cols * len(rights)),
            bytes_accessed=int(share * 2 * (depth * width + (depth + out_rows) * cols * len(rights))),
            transcendentals=0,
        ),
        name="product",
    )(first, *left, *[part for parts in rights for part in parts], *taken)


def unit_of(values):
    scale = lax.rsqrt(jnp.mean(values * values, axis=-1, keepdims=True) + NORM_EPS)
    return values * scale, scale


def norm_kernel(rows_ref, more_ref, sum_ref, unit_ref):
    values = rows_ref[...].astype(jnp.float32) + more_ref[...]
    sum_ref[...] = values
    unit_ref[...] = unit_of(values)[0].astype(jnp.bfloat16)


def add_and_norm(rows, more, tile=64):
    count, width = rows.shape
    spec = pl.BlockSpec((tile, width), lambda i: (i, 0))
    return pl.pallas_call(
        norm_kernel,
        grid=(count // tile,),
        out_shape=(
            jax.ShapeDtypeStruct(rows.shape, jnp.float32),
            jax.ShapeDtypeStruct(rows.shape, jnp.bfloat16),
        ),
        in_specs=[spec, spec],
        out_specs=(spec, spec),
        cost_estimate=pl.CostEstimate(
            flops=5 * count * width, bytes_accessed=12 * count * width, transcendentals=0
        ),
        name="add_and_norm",
    )(rows, more)


def norm_back_kernel(one_ref, two_ref, rows_ref, base_ref, *out_refs):
    scaled = one_ref[...].astype(jnp.float32) + two_ref[...].astype(jnp.float32)
    unit, scale = unit_of(rows_ref[...].astype(jnp.float32))
    result = base_ref[...].astype(jnp.float32) + scale * (
        scaled - unit * jnp.mean(scaled * unit, axis=-1, keepdims=True)
    )
    for out_ref in out_refs:
        out_ref[...] = result.astype(out_ref.dtype)


def norm_back(one, two, rows, base, kinds, tile=64):
    count, width = rows.shape
    spec = pl.BlockSpec((tile, width), lambda i: (i, 0))
    return pl.pallas_call(
        norm_back_kernel,
        grid=(count // tile,),
        out_shape=tuple(jax.ShapeDtypeStruct(rows.shape, kind) for kind in kinds),
        in_specs=[spec] * 4,
        out_specs=tuple([spec] * len(kinds)),
        cost_estimate=pl.CostEstimate(
            flops=10 * count * width, bytes_accessed=14 * count * width, transcendentals=0
        ),
        name="norm_back",
    )(one, two, rows, base)


def per_device(
    block_in,
    segments,
    positions,
    attention_gain,
    query_weight,
    key_weight,
    value_weight,
    query_gain,
    key_gain,
    output_weight,
    hidden_gain,
    gate_weight,
    up_weight,
    down_weight,
    cotangent,
):
    tp_count = lax.axis_size("tp")
    tp_index = lax.axis_index("tp")
    ctx_index = lax.axis_index(CTX)
    batch, own_rows, width = block_in.shape
    rows = batch * own_rows
    ctx_rows = own_rows * tp_count
    places = range(tp_count)
    order = [*range(1, tp_count), 0]
    masks = ctx_masks()
    q_cols = query_weight.shape[1]
    k_cols = key_weight.shape[1]
    qkv_cols = q_cols + 2 * k_cols
    hidden_cols = gate_weight.shape[1]
    q_gain = jnp.tile(query_gain.astype(jnp.float32), 2)[None]
    k_gain = jnp.tile(key_gain.astype(jnp.float32), 2)[None]

    block = width // (lax.axis_size("dp") * lax.axis_size(CTX))
    paired = block % 128 == 0
    pair_first = lax.rem(ctx_index, 2).astype(jnp.int32)[None]

    def meet(arrays):
        return [*arrays, *[ctx_swap(array, 1) for array in arrays]] if paired else list(arrays)

    def grad_product(left, rights, more=0, into=None, tile=512, share=1.0):
        blocks = width // block // 2 if paired else 0
        return product(left, rights, tile, pair_first, blocks, more, into, share)

    def scatter_sum(addend):
        axes = ("dp", CTX[0]) if paired else ("dp", *CTX)
        return lax.psum_scatter(addend, axes, scatter_dimension=0, tiled=True)

    back_places = [(tp_count - place) % tp_count for place in places]
    attention_rows = attention_gain.astype(jnp.float32)[:, None]
    hidden_gain_rows = hidden_gain.astype(jnp.float32)[:, None]
    qkv_weight = jnp.concatenate([query_weight, key_weight, value_weight], axis=1).astype(jnp.float32)
    first_weight = jnp.concatenate(
        [
            (gate_weight.astype(jnp.float32) * hidden_gain_rows).astype(jnp.bfloat16),
            (qkv_weight * attention_rows).astype(jnp.bfloat16),
        ],
        axis=1,
    )
    full_first = gather_weight(first_weight)
    full_qkv = full_first[:, hidden_cols:]

    def chunk_start(place):
        owner = lax.rem(tp_index - place + tp_count, tp_count)
        return owner * own_rows

    def own_part(table, start):
        return lax.dynamic_slice_in_dim(table, start, own_rows, 1)

    iota = jnp.arange(own_rows, dtype=jnp.int32)
    row_starts = [ctx_index * ctx_rows + chunk_start(place) for place in places]
    low = jnp.concatenate([own_part(segments, start) for start in row_starts], axis=1)[:, None]
    high = jnp.concatenate([start + iota for start in row_starts])[None, None]
    starts = jnp.stack(
        [
            jnp.bitwise_xor(ctx_index, mask) * ctx_rows + chunk_start(place)
            for mask in masks
            for place in places
        ]
    ).astype(jnp.int32)
    position = jnp.stack([own_part(positions, start).reshape(rows) for start in row_starts])
    half = HD // 2
    frequency = ROPE_BASE ** (-2.0 * jnp.arange(half, dtype=jnp.float32) / HD)
    sign = jnp.where(jnp.arange(2 * HD) % HD < half, -1.0, 1.0).astype(jnp.float32)
    angles = position.astype(jnp.float32)[..., None] * jnp.tile(frequency, 4)
    cos_wide, sin_wide = jnp.cos(angles), jnp.sin(angles) * sign

    def project(place):
        values = matmul(normed_rows[place], full_qkv)
        query_rot, kv = make_heads(
            values, cos_wide[place], sin_wide[place], q_gain, k_gain, q_cols, k_cols
        )
        return values, query_rot, kv

    def project_and_send(place):
        values, query_rot, kv = project(place)
        blocks = ctx_gather(kv)
        return values, query_rot, blocks

    tokens = block_in.reshape(rows, width)
    normed = unit_of(tokens.astype(jnp.float32))[0].astype(jnp.bfloat16)
    normed, out_own = together(normed, output_weight.T)
    normed_rows, heads = [normed], []
    out_pieces = [out_own]
    for _ in range(1, tp_count):
        out_pieces.append(shift(out_pieces[-1], -1))
    for place in range(1, tp_count):
        came = ring_hop(normed_rows[-1])
        ready = range(tp_count - 2) if place == tp_count - 1 else []
        work = [project_and_send(mine) for mine in ready]
        came, work = together(came, work)
        if place == 1:
            came, out_pieces = together(came, out_pieces)
            second_weight = jnp.concatenate(
                [*out_pieces, (up_weight.astype(jnp.float32) * hidden_gain_rows).astype(jnp.bfloat16)],
                axis=1,
            )
            full_second = gather_weight(second_weight)
        heads.extend(work)
        normed_rows.append(came)
    last_weight, normed_rows[-1] = together(down_weight.T, normed_rows[-1])
    full_down_t = gather_weight(last_weight)
    full_out, full_gate, full_up, full_down = (full_second, 0), (full_first, 0), (full_second, 1), (full_down_t, 0)

    grad_own, normed_rows[-1] = together(cotangent.reshape(rows, width), normed_rows[-1])
    came = ring_hop(grad_own)
    work = [project_and_send(mine) for mine in range(len(heads), tp_count)]
    came, work = together(came, work)
    heads.extend(work)
    raw, queries, gathered = ([h[i] for h in heads] for i in range(3))
    blocks = [[gathered[place][i] for place in places] for i in range(len(masks))]
    grad_rows = [grad_own, came]
    came = ring_hop(grad_rows[-1])
    attended = attend(starts, low, high, queries, blocks, batch)
    met_normed, mine_qkv = meet(normed_rows), full_qkv
    if paired:
        mine_qkv = lax.dynamic_index_in_dim(
            full_qkv.reshape(width // block // 2, 2, block, qkv_cols), pair_first[0], 1, False
        ).reshape(width // 2, qkv_cols)
    late_qkv, came, attended, met_normed, mine_qkv = together(
        full_qkv, came, attended, met_normed, mine_qkv
    )
    grad_rows.append(came)
    attended_rows, totals = attended[:tp_count], attended[tp_count]
    mine = [attended_rows[0]] + [shift(attended_rows[place], -place) for place in range(1, tp_count)]
    grad_rows[-1], mine = together(grad_rows[-1], mine)
    for _ in range(len(grad_rows), tp_count):
        grad_rows.append(ring_hop(grad_rows[-1]))
    met_grads = meet(grad_rows)
    (mixed_in,) = rows_nt([([[(piece, 0) for piece in mine]], full_out)], jnp.float32, 1, rows)
    met_mine = [meet([piece]) for piece in mine]
    hidden, unit_hidden = add_and_norm(tokens, mixed_in)

    def feed(group):
        return feed_rows(
            [hidden_rows[place] for place in group],
            [grad_rows[place] for place in group],
            full_gate,
            full_up,
            full_down,
            hidden_cols,
        )

    def hidden_terms(fed):
        halves = range(tp_count // 2)
        gates, ups = ([[(fed[part], half)] for half in halves] for part in (1, 2))
        return rows_nt([(gates, full_gate), (ups, full_up)], jnp.bfloat16, len(halves), rows)

    first, second = list(places)[: tp_count // 2], list(places)[tp_count // 2 :]
    hidden_rows = [unit_hidden]
    fed_first, terms_first = None, None
    for place in range(1, tp_count):
        came = ring_hop(hidden_rows[-1])
        if place == len(first):
            fed_first = feed(first)
            came, fed_first, met_grads, met_mine = together(came, fed_first, met_grads, met_mine)
        if place == len(first) + 1:
            met_first = [meet([fed]) for fed in fed_first]
            terms_first = hidden_terms(fed_first)
            came, terms_first, met_first = together(came, terms_first, met_first)
        hidden_rows.append(came)

    came = ring_hop(terms_first[1])
    met_hidden = meet(hidden_rows)
    fed_second = feed(second)
    feed_terms = rows_nt([([[(fed_first[0], 1)]], full_down)], jnp.bfloat16, 1, rows)
    came, fed_second, met_hidden, feed_terms = together(came, fed_second, met_hidden, feed_terms)
    feed_came = ring_hop(feed_terms[0])
    met_fed = [old + meet([fed]) for old, fed in zip(met_first, fed_second)]
    if paired:
        met_fed = [[fed[0], fed[2], fed[1], fed[3]] for fed in met_fed]
    terms_second, feed_came = together(hidden_terms(fed_second), feed_came)
    came = ring_hop(add_rows(came, terms_second[0]))
    down_product = grad_product(met_grads, [met_fed[0]])
    feed_terms += rows_nt([([[(fed_second[0], 0)]], full_down)], jnp.bfloat16, 1, rows)
    came, down_product, feed_terms = together(came, down_product, feed_terms)
    came = ring_hop(add_rows(came, terms_second[1]))
    down_shard = scatter_sum(down_product)
    pair_product = grad_product(met_hidden, [met_fed[1]], more=1)
    feed_rest = rows_nt(
        [([[(fed_second[0], 1)], [(fed_first[0], 0)]], full_down)], jnp.bfloat16, 2, rows
    )
    came, pair_product, feed_rest = together(came, pair_product, feed_rest)
    feed_terms = dict(zip(order, feed_terms + feed_rest))

    grad_hidden, branch = norm_back(
        came, terms_first[0], hidden, grad_own, (jnp.float32, jnp.bfloat16)
    )
    pieces = split_columns(branch, full_second, 0, tp_count, q_cols)
    pieces, branch = together(pieces, branch)
    grad_att = [pieces[0]] + [shift(pieces[place], place) for place in range(1, tp_count)]
    met_branch = meet([branch])
    out_product = grad_product(met_branch, met_mine, share=0.1)
    out_product, pair_product = together(out_product, pair_product)
    pair_product = grad_product(met_hidden, [met_fed[2]], into=pair_product, share=0.1)
    grad_att, pair_product, out_product = together(grad_att, pair_product, out_product)
    out_shard = scatter_sum(out_product)
    pair_shard = scatter_sum(pair_product)

    half_count = len(masks) // 2
    kinds = [
        [jnp.float32] * half_count + [jnp.bfloat16] * half_count,
        [jnp.float32] + [jnp.bfloat16] * (len(masks) - 1),
    ]
    query_gain_sum = jnp.zeros((8, 2 * HD), jnp.float32)
    dq_parts, own_parts, came_parts = [], [], []
    came = feed_came
    for step, place in enumerate(order[1:]):
        if place:
            came = ring_hop(add_rows(came, feed_terms[place]))
        if step < 2:
            dq, back, addend = attend_back(
                starts,
                low,
                high,
                totals,
                cos_wide,
                sin_wide,
                q_gain,
                queries,
                raw,
                grad_att,
                attended_rows,
                blocks,
                kinds[step],
                batch,
                [0, batch - batch // 4][step],
                [batch - batch // 4, batch // 4][step],
            )
            if step == 0:
                came, dq, back, addend, grad_att, down_shard = together(
                    came, dq, back, addend, grad_att, down_shard
                )
            else:
                dq, back, addend, own_parts, came_parts = together(
                    dq, back, addend, own_parts, came_parts
                )
            query_gain_sum = query_gain_sum + addend
            dq_parts.append(dq)
            own_parts.append(back[0])
            if step:
                came_parts.append([ctx_swap(part, mask) for part, mask in zip(back[1:], masks[1:])])
                continue
            bit = 1
            while len(back) > 2:
                half_count = len(back) // 2
                back = [
                    back[i] + ctx_swap(back[half_count + i].astype(jnp.bfloat16), bit).astype(jnp.float32)
                    for i in range(half_count)
                ]
                bit *= 2
            own_parts[0] = back[0]
            came_parts.append([ctx_swap(back[1].astype(jnp.bfloat16), bit)])
        else:
            grad_qkv, key_gain_sum = heads_back(
                dq_parts, own_parts, came_parts, raw, cos_wide, sin_wide, k_gain
            )
            came, grad_qkv, out_shard = together(came, grad_qkv, out_shard)
    feed_out = came.astype(jnp.float32) + feed_terms[0].astype(jnp.float32)
    block_out = (hidden + feed_out).astype(jnp.bfloat16).reshape(block_in.shape)

    def out_hop(total, place):
        start = back_places[place] * q_cols
        total = ring_hop(total).astype(jnp.float32) + out_shard[:, start : start + q_cols].astype(
            jnp.float32
        )
        return total.astype(jnp.bfloat16) if place else total

    met_qkv = meet([grad_qkv])
    row_terms = rows_nt(
        [([[(grad_qkv, place)] for place in places], (late_qkv, 0))], jnp.bfloat16, tp_count, rows
    )
    head_sums = jnp.stack([query_gain_sum, key_gain_sum]).sum(axis=1).reshape(2, 2, HD).sum(axis=1)
    total, met_qkv = together(row_terms[1], met_qkv)
    out_total = out_shard[:, back_places[1] * q_cols : (back_places[1] + 1) * q_cols]
    for step, place in enumerate(order[1:]):
        came = ring_hop(total)
        if step == 2:
            out_total, pair_shard, qkv_product = together(out_total, pair_shard, qkv_product)
            qkv_shard = scatter_sum(qkv_product)
        out_total = out_hop(out_total, place)
        if step < 2:
            came, out_total = together(came, out_total)
        if step == 0:
            head_sums = all_sum(head_sums, (CTX, "dp"))
            qkv_product = grad_product(met_normed, [met_qkv], tile=qkv_cols)
            attention_sum = jnp.sum(qkv_product.astype(jnp.float32) * mine_qkv.astype(jnp.float32), axis=1)
            came, head_sums, qkv_product, attention_sum = together(
                came, head_sums, qkv_product, attention_sum
            )
            small_sums = jnp.concatenate([attention_sum, head_sums.reshape(-1)])
        if step == 1:
            small_sums = all_sum(small_sums, ("tp",))
            came, small_sums = together(came, small_sums)
            head_sums = small_sums[-2 * HD :].reshape(2, HD)
            column = jnp.pad(small_sums[: -2 * HD].astype(jnp.bfloat16)[:, None], ((0, 0), (0, 127)))
            qkv_product = jnp.concatenate([qkv_product, column], axis=1)
        if place:
            total = add_rows(came, row_terms[place])
    pair_sums = pair_shard.astype(jnp.float32)
    gate_sums, up_sums = pair_sums[:, :hidden_cols], pair_sums[:, hidden_cols:]
    hidden_sums = jnp.sum(
        gate_sums * gate_weight.astype(jnp.float32) + up_sums * up_weight.astype(jnp.float32), axis=1
    )
    hidden_gain_grad = all_sum(hidden_sums, ("tp",))
    qkv_sums = qkv_shard[:, :qkv_cols].astype(jnp.float32)
    attention_gain_grad = qkv_shard[:, qkv_cols].astype(jnp.float32) / attention_rows[:, 0]
    (input_grad,) = norm_back(came, row_terms[0], tokens, grad_hidden, (jnp.float32,))
    output_grad = out_total.T
    down_grad = down_shard.astype(jnp.float32).T
    gate_grad, up_grad = gate_sums * hidden_gain_rows, up_sums * hidden_gain_rows
    qkv_grad = qkv_sums * attention_rows
    return (
        block_out,
        input_grad.reshape(block_in.shape),
        attention_gain_grad,
        qkv_grad[:, :q_cols],
        qkv_grad[:, q_cols : q_cols + k_cols],
        qkv_grad[:, q_cols + k_cols :],
        head_sums[0],
        head_sums[1],
        output_grad,
        hidden_gain_grad,
        gate_grad,
        up_grad,
        down_grad,
    )


def solution(mesh):
    in_specs = (
        P(None, ("dp", *CTX, "tp"), None),
        P(None, "dp"),
        P(None, "dp"),
        P(("dp", *CTX)),
        P(("dp", *CTX), "tp"),
        P(("dp", *CTX), "tp"),
        P(("dp", *CTX), "tp"),
        P(),
        P(),
        P("tp", ("dp", *CTX)),
        P(("dp", *CTX)),
        P(("dp", *CTX), "tp"),
        P(("dp", *CTX), "tp"),
        P("tp", ("dp", *CTX)),
        P(None, ("dp", *CTX, "tp"), None),
    )
    out_specs = (
        P(None, ("dp", *CTX, "tp"), None),
        P(None, ("dp", *CTX, "tp"), None),
        P(("dp", *CTX)),
        P(("dp", *CTX), "tp"),
        P(("dp", *CTX), "tp"),
        P(("dp", *CTX), "tp"),
        P(),
        P(),
        P("tp", ("dp", *CTX)),
        P(("dp", *CTX)),
        P(("dp", *CTX), "tp"),
        P(("dp", *CTX), "tp"),
        P("tp", ("dp", *CTX)),
    )
    shape = (mesh.shape["dp"], mesh.shape["ctx"] // 2, 2, mesh.shape["tp"])
    split = Mesh(mesh.devices.reshape(shape), ("dp", *CTX, "tp"))
    return jax.shard_map(
        per_device, mesh=split, in_specs=in_specs, out_specs=out_specs, check_vma=False
    )
```

```python
import functools
import math

import jax
import jax.numpy as jnp
from jax import lax
from jax.experimental import pallas as pl
from jax.experimental.pallas import tpu as pltpu
from jax.sharding import Mesh
from jax.sharding import PartitionSpec as P

D = 2048
HD = 64


NORM_EPS = 1e-05
ROPE_BASE = 1000000.0
MASKED = -1e30
CTX = ("ctx_pair", "ctx_place")


def matmul(left_mat, right_mat):
    return jnp.dot(left_mat, right_mat, preferred_element_type=jnp.float32)


def matmul_tn(left_mat, right_mat):
    return lax.dot_general(
        left_mat, right_mat, (((0,), (0,)), ((), ())), preferred_element_type=jnp.float32
    )


def matmul_nt(left_mat, right_mat):
    return lax.dot_general(
        left_mat, right_mat, (((1,), (1,)), ((), ())), preferred_element_type=jnp.float32
    )


def ring_hop(values):
    count = lax.axis_size("tp")
    return lax.ppermute(values, "tp", [(i, (i + 1) % count) for i in range(count)])


def ctx_swap(values, mask):
    count = lax.axis_size(CTX)
    return lax.ppermute(values, CTX, [(i, i ^ mask) for i in range(count)])


def ctx_masks():
    masks = [0]
    bit = lax.axis_size(CTX) // 2
    while bit:
        masks = masks + [mask ^ bit for mask in masks]
        bit //= 2
    return masks


def ctx_gather(own):
    blocks = [own]
    bit = lax.axis_size(CTX) // 2
    while bit:
        blocks = blocks + [ctx_swap(block, bit) for block in blocks]
        bit //= 2
    return blocks


def gather_weight(shard):
    return lax.all_gather(shard, ("dp", *CTX), axis=0, tiled=True)


def all_sum(values, axes):
    for axis in axes:
        count = lax.axis_size(axis)
        bit = 1
        while bit < count:
            values = values + lax.ppermute(values, axis, [(i, i ^ bit) for i in range(count)])
            bit *= 2
    return values


def shift(values, places):
    count = lax.axis_size("tp")
    return lax.ppermute(values, "tp", [(i, (i + places) % count) for i in range(count)])


def together(*values):
    return lax.optimization_barrier(values)


def lane_iota(shape):
    return lax.broadcasted_iota(jnp.int32, shape, 1)


def head_means(values):
    width = values.shape[1]
    row = lax.broadcasted_iota(jnp.int32, (width, width), 0) // HD
    col = lax.broadcasted_iota(jnp.int32, (width, width), 1) // HD
    pick = jnp.where(row == col, 1.0 / HD, 0.0).astype(jnp.float32)
    return jnp.dot(
        values, pick, precision=lax.Precision.HIGHEST, preferred_element_type=jnp.float32
    )


def half_swap(values):
    width, half = values.shape[1], HD // 2
    first = lax.rem(lane_iota(values.shape), HD) < half
    return jnp.where(
        first, pltpu.roll(values, width - half, 1), pltpu.roll(values, half, 1)
    )


def other_head(values):
    return pltpu.roll(values, HD, 1)


def twice(values, head):
    wide = values.astype(jnp.float32)
    low = lane_iota(wide.shape) < HD
    other = other_head(wide)
    both = jnp.where(low, wide, other) if head == 0 else jnp.where(low, other, wide)
    return both.astype(values.dtype)


def apart(values):
    wide = values.astype(jnp.float32)
    low = lane_iota(wide.shape) < HD
    zero = jnp.zeros_like(wide)
    return jnp.concatenate(
        [jnp.where(low, wide, zero), jnp.where(low, zero, wide)], axis=0
    ).astype(values.dtype)


def heads_kernel(raw_ref, cos_ref, sin_ref, q_gain_ref, k_gain_ref, q_ref, kv_ref):
    pair = 2 * HD
    q_cols = q_ref.shape[1]
    k_cols = kv_ref.shape[1] // 2
    cos, sin = cos_ref[...], sin_ref[...]
    for first in range(0, q_cols + k_cols, pair):
        values = raw_ref[:, first : first + pair]
        gain = q_gain_ref[...] if first < q_cols else k_gain_ref[...]
        normed = values * lax.rsqrt(head_means(values * values) + NORM_EPS) * gain
        turned = (normed * cos + half_swap(normed) * sin).astype(jnp.bfloat16)
        if first < q_cols:
            q_ref[:, first : first + pair] = turned
        else:
            kv_ref[:, first - q_cols : first - q_cols + pair] = turned
    kv_ref[:, k_cols:] = raw_ref[:, q_cols + k_cols :].astype(jnp.bfloat16)


def make_heads(raw, cos_wide, sin_wide, q_gain, k_gain, q_cols, k_cols):
    rows = raw.shape[0]
    return pl.pallas_call(
        heads_kernel,
        out_shape=(
            jax.ShapeDtypeStruct((rows, q_cols), jnp.bfloat16),
            jax.ShapeDtypeStruct((rows, 2 * k_cols), jnp.bfloat16),
        ),
        cost_estimate=pl.CostEstimate(
            flops=rows * raw.shape[1] * 400, bytes_accessed=rows * raw.shape[1] * 7, transcendentals=0
        ),
        name="make_heads",
    )(raw, cos_wide, sin_wide, q_gain, k_gain)


def turn_back(grad, values, gain, cos, sin):
    turned = grad * cos - half_swap(grad) * sin
    scale = lax.rsqrt(head_means(values * values) + NORM_EPS)
    unit = values * scale
    scaled = turned * gain
    return scale * (scaled - unit * head_means(scaled * unit)), turned * unit


def fill_bias(starts_ref, low_ref, high_ref, bias_ref, piece):
    low, high = low_ref[0], high_ref[0]
    for i in range(bias_ref.shape[0] // piece):
        place = starts_ref[i] + lax.broadcasted_iota(jnp.int32, (piece, low.shape[1]), 0)
        linked = (place >= low) & (place <= high)
        bias = jnp.where(linked, 0.0, MASKED)
        bias_ref[i * piece : (i + 1) * piece, : low.shape[1]] = bias
        bias_ref[i * piece : (i + 1) * piece, low.shape[1] :] = bias


def attend_kernel(places, blocks, block_keys, *refs):
    starts_ref, low_ref, high_ref = refs[:3]
    q_refs = refs[3 : 3 + places]
    kv_refs = refs[3 + places : 3 + places + blocks * places]
    refs = refs[3 + places + blocks * places :]
    out_refs = refs[:places]
    total_ref, bias_ref, key_ref, value_ref = refs[places:]
    pair = 2 * HD
    piece, q_cols = q_refs[0].shape
    rows = places * piece
    k_cols = kv_refs[0].shape[1] // 2
    k_heads = k_cols // HD
    group = q_cols // k_cols
    scale = math.log2(math.e) / math.sqrt(HD)
    fill_bias(starts_ref, low_ref, high_ref, bias_ref, piece)
    for block in range(blocks):
        mine = kv_refs[block * places : (block + 1) * places]
        for head in range(k_heads):
            cols = slice(head // 2 * pair, head // 2 * pair + pair)
            vcols = slice(k_cols + head // 2 * pair, k_cols + head // 2 * pair + pair)
            where = slice(block * block_keys, (block + 1) * block_keys)
            keys = jnp.concatenate([ref[:, cols] for ref in mine], axis=0)
            key_ref[head, where, :] = twice(keys, head % 2)
            if head % 2 == 0:
                values = jnp.concatenate([ref[:, vcols] for ref in mine], axis=0)
                value_ref[head // 2, :, where] = values.astype(jnp.float32).T.astype(jnp.bfloat16)
    for first in range(0, q_cols, pair):
        head = first // HD // group
        queries = apart(jnp.concatenate([q_ref[:, first : first + pair] for q_ref in q_refs], axis=0))

        mixed = jnp.zeros((HD, 2 * rows), jnp.float32)
        total = jnp.zeros((1, 2 * rows), jnp.float32)
        for block in range(blocks):
            where = slice(block * block_keys, (block + 1) * block_keys)
            scores = matmul_nt(key_ref[head, where, :], queries)
            weight = jnp.exp2(scores * scale + bias_ref[where, :])
            total = total + jnp.sum(weight, axis=0, keepdims=True)
            values = value_ref[head // 2, head % 2 * HD : (head % 2 + 1) * HD, where]
            mixed = mixed + matmul(values, weight.astype(jnp.bfloat16))
        mixed = mixed / total
        out = jnp.concatenate([mixed[:, :rows], mixed[:, rows:]], axis=0).T.astype(jnp.bfloat16)
        for place in range(places):
            out_refs[place][:, first : first + pair] = out[place * piece : (place + 1) * piece]
        total_ref[0, first // pair, :] = jnp.log2(total)[0]


def attend(starts, low, high, q_chunks, kv_blocks, batch):
    places, blocks = len(q_chunks), len(kv_blocks)
    kv_flat = [kv for block in kv_blocks for kv in block]
    rows, q_cols = q_chunks[0].shape
    piece = rows // batch
    kv_cols = kv_flat[0].shape[1]
    k_cols = kv_cols // 2
    keys = blocks * places * piece
    q_rows = places * piece
    pairs = q_cols // (2 * HD)
    q_spec = pl.BlockSpec((piece, q_cols), lambda b: (b, 0))
    kv_spec = pl.BlockSpec((piece, kv_cols), lambda b: (b, 0))
    line_spec = pl.BlockSpec((1, 1, q_rows), lambda b: (b, 0, 0))
    work = batch * q_cols // HD * q_rows * keys
    results = pl.pallas_call(
        functools.partial(attend_kernel, places, blocks, places * piece),
        grid=(batch,),
        out_shape=tuple(
            [jax.ShapeDtypeStruct((rows, q_cols), jnp.bfloat16)] * places
            + [jax.ShapeDtypeStruct((batch, pairs, 2 * q_rows), jnp.float32)]
        ),
        in_specs=[
            pl.BlockSpec(memory_space=pltpu.SMEM),
            line_spec,
            pl.BlockSpec((1, 1, q_rows), lambda b: (0, 0, 0)),
        ]
        + [q_spec] * places
        + [kv_spec] * len(kv_flat),
        out_specs=tuple(
            [q_spec] * places + [pl.BlockSpec((1, pairs, 2 * q_rows), lambda b: (b, 0, 0))]
        ),
        scratch_shapes=[
            pltpu.VMEM((keys, 2 * q_rows), jnp.float32),
            pltpu.VMEM((k_cols // HD, keys, 2 * HD), jnp.bfloat16),
            pltpu.VMEM((k_cols // HD // 2, 2 * HD, keys), jnp.bfloat16),
        ],
        cost_estimate=pl.CostEstimate(
            flops=work * 4 * HD * 4, bytes_accessed=batch * q_rows * q_cols * 8, transcendentals=work
        ),
        name="attend",
    )(starts, low, high, *q_chunks, *kv_flat)
    return list(results)


def attend_back_kernel(places, blocks, block_keys, *refs):
    starts_ref, low_ref, high_ref, total_ref, cos_ref, sin_ref, gain_ref = refs[:7]
    refs = refs[7:]
    q_refs, refs = refs[:places], refs[places:]
    raw_refs, refs = refs[:places], refs[places:]
    grad_refs, refs = refs[:places], refs[places:]
    mixed_refs, refs = refs[:places], refs[places:]
    kv_refs, refs = refs[: blocks * places], refs[blocks * places :]
    dq_ref, refs = refs[0], refs[1:]
    dkv_refs, refs = refs[:blocks], refs[blocks:]
    gain_sum_ref, bias_ref, key_ref, turned_ref, value_ref, dkey_ref, dvalue_ref = refs
    pair = 2 * HD
    piece, q_cols = q_refs[0].shape
    rows = places * piece
    k_cols = kv_refs[0].shape[1] // 2
    k_heads = k_cols // HD
    group = q_cols // k_cols
    inv_root = 1.0 / math.sqrt(HD)
    scale = math.log2(math.e) * inv_root
    fill_bias(starts_ref, low_ref, high_ref, bias_ref, piece)

    @pl.when(pl.program_id(0) == 0)
    def _():
        gain_sum_ref[...] = jnp.zeros_like(gain_sum_ref)

    for block in range(blocks):
        mine = kv_refs[block * places : (block + 1) * places]
        for head in range(k_heads):
            cols = slice(head // 2 * pair, head // 2 * pair + pair)
            vcols = slice(k_cols + head // 2 * pair, k_cols + head // 2 * pair + pair)
            where = slice(block * block_keys, (block + 1) * block_keys)
            keys = jnp.concatenate([ref[:, cols] for ref in mine], axis=0)
            values = jnp.concatenate([ref[:, vcols] for ref in mine], axis=0)
            key_ref[head, where, :] = twice(keys, head % 2)
            value_ref[head, where, :] = twice(values, head % 2)
            if head % 2 == 0:
                turned_ref[head // 2, :, where] = keys.astype(jnp.float32).T.astype(jnp.bfloat16)
    for first in range(0, q_cols, pair):
        head = first // HD // group
        fresh = first % (group * HD) == 0
        queries = apart(jnp.concatenate([q_ref[:, first : first + pair] for q_ref in q_refs], axis=0))
        grads = apart(jnp.concatenate([g_ref[:, first : first + pair] for g_ref in grad_refs], axis=0))
        total = total_ref[0, first // pair : first // pair + 1, :]

        mixed = apart(jnp.concatenate([m_ref[:, first : first + pair] for m_ref in mixed_refs], axis=0))
        delta = jnp.sum((grads.astype(jnp.float32) * mixed.astype(jnp.float32)).T, axis=0, keepdims=True)
        dquery = jnp.zeros((HD, 2 * rows), jnp.float32)
        for block in range(blocks):
            where = slice(block * block_keys, (block + 1) * block_keys)
            scores = matmul_nt(key_ref[head, where, :], queries)
            dprob = matmul_nt(value_ref[head, where, :], grads)
            prob = jnp.exp2(scores * scale + bias_ref[where, :] - total)
            dscore = (prob * (dprob - delta)).astype(jnp.bfloat16)
            dvalue = matmul(prob.astype(jnp.bfloat16), grads)
            dkey = matmul(dscore, queries)
            if fresh:
                dvalue_ref[head, where, :] = dvalue
                dkey_ref[head, where, :] = dkey
            else:
                dvalue_ref[head, where, :] += dvalue
                dkey_ref[head, where, :] += dkey
            keys = turned_ref[head // 2, head % 2 * HD : (head % 2 + 1) * HD, where]
            dquery = dquery + matmul(keys, dscore)
        dquery = dquery * inv_root
        dquery = jnp.concatenate([dquery[:, :rows], dquery[:, rows:]], axis=0).T
        raw = jnp.concatenate([raw_ref[:, first : first + pair] for raw_ref in raw_refs], axis=0)
        dq, addend = turn_back(
            dquery, raw, gain_ref[...], cos_ref[...].reshape(rows, pair), sin_ref[...].reshape(rows, pair)
        )
        gain_sum_ref[...] += jnp.sum(addend.reshape(-1, 8, pair), axis=0)
        dq_ref[:, :, first : first + pair] = dq.reshape(places, piece, pair).astype(jnp.bfloat16)
    low = lane_iota((block_keys, pair)) < HD
    for block in range(blocks):
        where = slice(block * block_keys, (block + 1) * block_keys)
        for first in range(0, k_heads, 2):
            for shift, ref, factor in ((0, dkey_ref, inv_root), (k_cols, dvalue_ref, 1.0)):
                one, two = ref[first, where, :], ref[first + 1, where, :]
                sums = jnp.where(low, one + other_head(one), two + other_head(two)) * factor
                cols = slice(shift + first // 2 * pair, shift + first // 2 * pair + pair)
                dkv_refs[block][:, :, cols] = sums.reshape(places, piece, pair).astype(
                    dkv_refs[block].dtype
                )


def attend_back(
    starts,
    low,
    high,
    totals,
    cos_wide,
    sin_wide,
    q_gain,
    q_chunks,
    raw_chunks,
    grad_chunks,
    mixed_chunks,
    kv_blocks,
    kinds,
    batch,
    base,
    count,
):
    places, blocks = len(q_chunks), len(kv_blocks)
    kv_flat = [kv for block in kv_blocks for kv in block]
    rows, q_cols = q_chunks[0].shape
    piece = rows // batch
    kv_cols = kv_flat[0].shape[1]
    k_cols = kv_cols // 2
    keys = blocks * places * piece
    q_rows = places * piece
    pairs = q_cols // (2 * HD)
    k_heads = k_cols // HD
    q_spec = pl.BlockSpec((piece, q_cols), lambda b: (base + b, 0))
    kv_spec = pl.BlockSpec((piece, kv_cols), lambda b: (base + b, 0))
    line_spec = pl.BlockSpec((1, 1, q_rows), lambda b: (base + b, 0, 0))
    turn_spec = pl.BlockSpec((places, piece, 2 * HD), lambda b: (0, base + b, 0))
    work = count * q_cols // HD * q_rows * keys
    results = pl.pallas_call(
        functools.partial(attend_back_kernel, places, blocks, places * piece),
        grid=(count,),
        out_shape=tuple(
            [jax.ShapeDtypeStruct((places, count * piece, q_cols), jnp.bfloat16)]
            + [jax.ShapeDtypeStruct((places, count * piece, kv_cols), kind) for kind in kinds]
            + [jax.ShapeDtypeStruct((8, 2 * HD), jnp.float32)]
        ),
        in_specs=[
            pl.BlockSpec(memory_space=pltpu.SMEM),
            line_spec,
            pl.BlockSpec((1, 1, q_rows), lambda b: (0, 0, 0)),
            pl.BlockSpec((1, pairs, 2 * q_rows), lambda b: (base + b, 0, 0)),
            turn_spec,
            turn_spec,
            pl.BlockSpec((1, 2 * HD), lambda b: (0, 0)),
        ]
        + [q_spec] * (4 * places)
        + [kv_spec] * len(kv_flat),
        out_specs=tuple(
            [pl.BlockSpec((places, piece, q_cols), lambda b: (0, b, 0))]
            + [pl.BlockSpec((places, piece, kv_cols), lambda b: (0, b, 0))] * blocks
            + [pl.BlockSpec((8, 2 * HD), lambda b: (0, 0))]
        ),
        scratch_shapes=[
            pltpu.VMEM((keys, 2 * q_rows), jnp.float32),
            pltpu.VMEM((k_heads, keys, 2 * HD), jnp.bfloat16),
            pltpu.VMEM((k_heads // 2, 2 * HD, keys), jnp.bfloat16),
            pltpu.VMEM((k_heads, keys, 2 * HD), jnp.bfloat16),
            pltpu.VMEM((k_heads, keys, 2 * HD), jnp.float32),
            pltpu.VMEM((k_heads, keys, 2 * HD), jnp.float32),
        ],
        cost_estimate=pl.CostEstimate(
            flops=work * 10 * HD * 4, bytes_accessed=count * q_rows * q_cols * 16, transcendentals=work
        ),
        name="attend_back",
    )(
        starts,
        low,
        high,
        totals,
        cos_wide,
        sin_wide,
        q_gain,
        *q_chunks,
        *raw_chunks,
        *grad_chunks,
        *mixed_chunks,
        *kv_flat,
    )
    return results[0], list(results[1:-1]), results[-1]


def heads_back_kernel(places, came_counts, q_cols, *refs):
    parts = len(came_counts)
    dq_refs, refs = refs[:parts], refs[parts:]
    own_refs, refs = refs[:parts], refs[parts:]
    came_refs = []
    for count in came_counts:
        came_refs.append(refs[:count])
        refs = refs[count:]
    raw_refs, refs = refs[:places], refs[places:]
    cos_ref, sin_ref, gain_ref, out_ref, gain_sum_ref = refs
    rows = raw_refs[0].shape[0]
    k_cols = own_refs[0].shape[2] // 2
    pair = 2 * HD
    addends = jnp.zeros((8, pair), jnp.float32)
    for place in range(places):
        start = 0
        for part in range(parts):
            stop = start + own_refs[part].shape[1]
            mine = slice(start, stop)
            out = slice(place * rows + start, place * rows + stop)
            start = stop
            out_ref[out, :q_cols] = dq_refs[part][place]
            grads = own_refs[part][place]
            for came_ref in came_refs[part]:
                grads = grads + came_ref[place].astype(jnp.float32)
            for first in range(0, k_cols, pair):
                cols = slice(first, first + pair)
                dk, addend = turn_back(
                    grads[:, cols],
                    raw_refs[place][mine, cols],
                    gain_ref[...],
                    cos_ref[place, mine],
                    sin_ref[place, mine],
                )
                out_ref[out, q_cols + first : q_cols + first + pair] = dk.astype(jnp.bfloat16)
                addends = addends + jnp.sum(addend.reshape(-1, 8, pair), axis=0)
            out_ref[out, q_cols + k_cols :] = grads[:, k_cols:].astype(jnp.bfloat16)
    gain_sum_ref[...] = addends


def heads_back(dq_parts, own_parts, came_parts, raw_chunks, cos_wide, sin_wide, k_gain):
    parts, places = len(dq_parts), len(raw_chunks)
    rows = raw_chunks[0].shape[0]
    q_cols, kv_cols = dq_parts[0].shape[2], own_parts[0].shape[2]
    k_cols = kv_cols // 2

    def whole(array):
        return pl.BlockSpec(array.shape, lambda i: (0,) * array.ndim)

    inputs = [*dq_parts, *own_parts, *[came for part in came_parts for came in part]]
    turns = [cos_wide, sin_wide, k_gain]
    return pl.pallas_call(
        functools.partial(heads_back_kernel, places, [len(part) for part in came_parts], q_cols),
        grid=(1,),
        out_shape=(
            jax.ShapeDtypeStruct((places * rows, q_cols + kv_cols), jnp.bfloat16),
            jax.ShapeDtypeStruct((8, 2 * HD), jnp.float32),
        ),
        in_specs=[whole(array) for array in inputs]
        + [pl.BlockSpec((rows, k_cols), lambda i: (0, q_cols // k_cols))] * places
        + [whole(array) for array in turns],
        out_specs=(
            pl.BlockSpec((places * rows, q_cols + kv_cols), lambda i: (0, 0)),
            pl.BlockSpec((8, 2 * HD), lambda i: (0, 0)),
        ),
        cost_estimate=pl.CostEstimate(
            flops=places * rows * kv_cols * 400, bytes_accessed=places * rows * 4096, transcendentals=0
        ),
        name="heads_back",
    )(*inputs, *raw_chunks, *turns)


def feed_kernel(count, *refs):
    hidden_refs, grad_refs = refs[:count], refs[count : 2 * count]
    gate_ref, up_ref, down_ref, act_ref, dgate_ref, dup_ref, hidden, grads = refs[2 * count :]

    @pl.when(pl.program_id(0) == 0)
    def _():
        rows = hidden_refs[0].shape[0]
        for i in range(count):
            hidden[i * rows : (i + 1) * rows, :] = hidden_refs[i][...]
            grads[i * rows : (i + 1) * rows, :] = grad_refs[i][...]

    gate = matmul(hidden[...], gate_ref[...])
    up = matmul(hidden[...], up_ref[...])
    grad = matmul(grads[...], down_ref[...])
    sigmoid = 1.0 / (1.0 + jnp.exp(-gate))
    silu = gate * sigmoid
    act_ref[...] = (silu * up).astype(jnp.bfloat16)
    dgate_ref[...] = (grad * up * sigmoid * (1.0 + gate * (1.0 - sigmoid))).astype(jnp.bfloat16)
    dup_ref[...] = (grad * silu).astype(jnp.bfloat16)


def feed_rows(hidden_rows, grad_rows, gate, up, down_t, cols):
    count = len(hidden_rows)
    rows, width = hidden_rows[0].shape
    total = count * rows
    tile = min(cols, 512 if count == 1 else 256)
    steps = cols // tile
    row_spec = pl.BlockSpec((rows, width), lambda j: (0, 0))
    out_spec = pl.BlockSpec((total, tile), lambda j: (0, j))

    def weight_spec(weight):
        return pl.BlockSpec((width, tile), lambda j: (0, weight[1] * steps + j))

    return pl.pallas_call(
        functools.partial(feed_kernel, count),
        grid=(steps,),
        out_shape=tuple([jax.ShapeDtypeStruct((total, cols), jnp.bfloat16)] * 3),
        in_specs=[row_spec] * (2 * count)
        + [
            weight_spec(gate),
            weight_spec(up),
            weight_spec(down_t),
        ],
        out_specs=tuple([out_spec] * 3),
        scratch_shapes=[pltpu.VMEM((total, width), jnp.bfloat16)] * 2,
        cost_estimate=pl.CostEstimate(
            flops=6 * total * width * cols,
            bytes_accessed=6 * width * cols + 4 * total * width + 6 * total * cols,
            transcendentals=total * cols,
        ),
        name="feed_rows",
    )(*hidden_rows, *grad_rows, gate[0], up[0], down_t[0])


def fill_rows(parts, whole):
    row = 0
    for line in parts:
        col = 0
        for ref in line:
            rows, cols = ref.shape
            whole[row : row + rows, col : col + cols] = ref[...]
            col += cols
        row += rows


def rows_nt_kernel(layouts, *refs):
    count = len(layouts)
    parts = []
    for lines, cols in layouts:
        parts.append([refs[i * cols : (i + 1) * cols] for i in range(lines)])
        refs = refs[lines * cols :]
    weight_refs, out_refs, wholes = refs[:count], refs[count:-count], refs[-count:]

    @pl.when(pl.program_id(0) == 0)
    def _():
        for part, whole in zip(parts, wholes):
            fill_rows(part, whole)

    result = matmul_nt(wholes[0][...], weight_refs[0][...])
    for weight_ref, whole in zip(weight_refs[1:], wholes[1:]):
        result = result + matmul_nt(whole[...], weight_ref[...])
    rows = out_refs[0].shape[0]
    for i, out_ref in enumerate(out_refs):
        out_ref[...] = result[i * rows : (i + 1) * rows].astype(out_ref.dtype)


def rows_nt(addends, kind, outs, rows_each, tile=512):
    layouts, parts, depths = [], [], []
    for lines, _ in addends:
        layouts.append((len(lines), len(lines[0])))
        parts.extend(part for line in lines for part in line)
        depths.append(sum(part[0].shape[1] for part in lines[0]))
    rows = rows_each * len(addends[0][0])
    weights = [weight for _, weight in addends]
    width = weights[0][0].shape[0]

    def part_spec(part):
        return pl.BlockSpec((rows_each, part[0].shape[1]), lambda j: (part[1], 0))

    def weight_spec(weight, depth):
        return pl.BlockSpec((tile, depth), lambda j: (j, weight[1]))

    results = pl.pallas_call(
        functools.partial(rows_nt_kernel, layouts),
        grid=(width // tile,),
        out_shape=tuple([jax.ShapeDtypeStruct((rows // outs, width), kind)] * outs),
        in_specs=[part_spec(part) for part in parts]
        + [weight_spec(weight, depth) for weight, depth in zip(weights, depths)],
        out_specs=tuple([pl.BlockSpec((rows // outs, tile), lambda j: (0, j))] * outs),
        scratch_shapes=[pltpu.VMEM((rows, depth), jnp.bfloat16) for depth in depths],
        cost_estimate=pl.CostEstimate(
            flops=2 * rows * sum(depths) * width,
            bytes_accessed=2 * sum(depths) * (rows + width) + 2 * rows * width,
            transcendentals=0,
        ),
        name="rows_nt",
    )(*[part[0] for part in parts], *[weight[0] for weight in weights])
    return list(results)


def add_kernel(one_ref, two_ref, out_ref):
    out_ref[...] = (one_ref[...].astype(jnp.float32) + two_ref[...].astype(jnp.float32)).astype(
        out_ref.dtype
    )


def add_rows(one, two, tile=1024):
    rows, cols = one.shape
    spec = pl.BlockSpec((rows, tile), lambda j: (0, j))
    return pl.pallas_call(
        add_kernel,
        grid=(cols // tile,),
        out_shape=jax.ShapeDtypeStruct(one.shape, one.dtype),
        in_specs=[spec, spec],
        out_specs=spec,
        cost_estimate=pl.CostEstimate(flops=rows * cols, bytes_accessed=6 * rows * cols, transcendentals=0),
        name="add_rows",
    )(one, two)


def split_kernel(rows_ref, weight_ref, *out_refs):
    result = matmul(rows_ref[...], weight_ref[...]).astype(jnp.bfloat16)
    for i, out_ref in enumerate(out_refs):

        @pl.when(pl.program_id(0) == i)
        def _():
            out_ref[...] = result


def split_columns(rows, weight, first, count, cols):
    total, depth = rows.shape
    return pl.pallas_call(
        split_kernel,
        grid=(count,),
        out_shape=tuple([jax.ShapeDtypeStruct((total, cols), jnp.bfloat16)] * count),
        in_specs=[
            pl.BlockSpec((total, depth), lambda j: (0, 0)),
            pl.BlockSpec((depth, cols), lambda j: (0, first + j)),
        ],
        out_specs=tuple([pl.BlockSpec((total, cols), lambda j: (0, 0))] * count),
        cost_estimate=pl.CostEstimate(
            flops=2 * total * depth * cols * count,
            bytes_accessed=2 * (total * depth + depth * cols * count + total * cols * count),
            transcendentals=0,
        ),
        name="split_columns",
    )(rows, weight)


def product_kernel(left_count, right_counts, blocks, skip, first_ref, *refs):
    left_refs, refs = refs[:left_count], refs[left_count:]
    rights = []
    for count in right_counts:
        rights.append(refs[:count])
        refs = refs[count:]
    out_ref, left, right = refs[skip:]
    steps = pl.num_programs(0) // len(rights)

    @pl.when(pl.program_id(0) == 0)
    def _():
        if blocks:
            cols = left.shape[1] // blocks
            row = 0
            for ref in left_refs:
                rows = ref.shape[0]
                for i in range(blocks):
                    start = pl.multiple_of((2 * i + first_ref[0]) * cols, cols)
                    left[row : row + rows, i * cols : (i + 1) * cols] = ref[:, pl.ds(start, cols)]
                row += rows
        else:
            fill_rows([[ref] for ref in left_refs], left)

    for i, refs in enumerate(rights):

        @pl.when(pl.program_id(0) // steps == i)
        def _():
            fill_rows([[ref] for ref in refs], right)

    out_ref[...] = matmul_tn(left[...], right[...]).astype(jnp.bfloat16)


def product(left, rights, tile=512, first=None, blocks=0, more=0, into=None, share=1.0):
    width, cols = left[0].shape[1], rights[0][0].shape[1]
    depth = sum(part.shape[0] for part in left)
    tile = min(tile, cols)
    steps = cols // tile
    out_rows = width // 2 if blocks else width
    first = jnp.zeros((1,), jnp.int32) if first is None else first
    taken = [] if into is None else [into]
    out_cols = into.shape[1] if taken else cols * (len(rights) + more)
    skipped = out_cols // tile - steps * len(rights) if taken else 0
    operands = 1 + len(left) + sum(len(parts) for parts in rights)

    def right_spec(part, index):
        return pl.BlockSpec(
            (part.shape[0], tile), lambda j: (0, jnp.clip(j - index * steps, 0, steps - 1))
        )

    return pl.pallas_call(
        functools.partial(
            product_kernel, len(left), [len(parts) for parts in rights], blocks, len(taken)
        ),
        grid=(steps * len(rights),),
        out_shape=jax.ShapeDtypeStruct((out_rows, out_cols), jnp.bfloat16),
        in_specs=[pl.BlockSpec(memory_space=pltpu.SMEM)]
        + [pl.BlockSpec(part.shape, lambda j: (0, 0)) for part in left]
        + [right_spec(part, index) for index, parts in enumerate(rights) for part in parts]
        + [pl.BlockSpec(memory_space=pl.ANY)] * len(taken),
        out_specs=pl.BlockSpec((out_rows, tile), lambda j: (0, skipped + j)),
        input_output_aliases={operands: 0} if taken else {},
        scratch_shapes=[
            pltpu.VMEM((depth, out_rows), jnp.bfloat16),
            pltpu.VMEM((depth, tile), jnp.bfloat16),
        ],
        cost_estimate=pl.CostEstimate(
            flops=int(share * 2 * depth * out_rows * cols * len(rights)),
            bytes_accessed=int(share * 2 * (depth * width + (depth + out_rows) * cols * len(rights))),
            transcendentals=0,
        ),
        name="product",
    )(first, *left, *[part for parts in rights for part in parts], *taken)


def unit_of(values):
    scale = lax.rsqrt(jnp.mean(values * values, axis=-1, keepdims=True) + NORM_EPS)
    return values * scale, scale


def norm_kernel(rows_ref, more_ref, sum_ref, unit_ref):
    values = rows_ref[...].astype(jnp.float32) + more_ref[...]
    sum_ref[...] = values
    unit_ref[...] = unit_of(values)[0].astype(jnp.bfloat16)


def add_and_norm(rows, more, tile=64):
    count, width = rows.shape
    spec = pl.BlockSpec((tile, width), lambda i: (i, 0))
    return pl.pallas_call(
        norm_kernel,
        grid=(count // tile,),
        out_shape=(
            jax.ShapeDtypeStruct(rows.shape, jnp.float32),
            jax.ShapeDtypeStruct(rows.shape, jnp.bfloat16),
        ),
        in_specs=[spec, spec],
        out_specs=(spec, spec),
        cost_estimate=pl.CostEstimate(
            flops=5 * count * width, bytes_accessed=12 * count * width, transcendentals=0
        ),
        name="add_and_norm",
    )(rows, more)


def norm_back_kernel(one_ref, two_ref, rows_ref, base_ref, *out_refs):
    scaled = one_ref[...].astype(jnp.float32) + two_ref[...].astype(jnp.float32)
    unit, scale = unit_of(rows_ref[...].astype(jnp.float32))
    result = base_ref[...].astype(jnp.float32) + scale * (
        scaled - unit * jnp.mean(scaled * unit, axis=-1, keepdims=True)
    )
    for out_ref in out_refs:
        out_ref[...] = result.astype(out_ref.dtype)


def norm_back(one, two, rows, base, kinds, tile=64):
    count, width = rows.shape
    spec = pl.BlockSpec((tile, width), lambda i: (i, 0))
    return pl.pallas_call(
        norm_back_kernel,
        grid=(count // tile,),
        out_shape=tuple(jax.ShapeDtypeStruct(rows.shape, kind) for kind in kinds),
        in_specs=[spec] * 4,
        out_specs=tuple([spec] * len(kinds)),
        cost_estimate=pl.CostEstimate(
            flops=10 * count * width, bytes_accessed=14 * count * width, transcendentals=0
        ),
        name="norm_back",
    )(one, two, rows, base)


def per_device(
    block_in,
    segments,
    positions,
    attention_gain,
    query_weight,
    key_weight,
    value_weight,
    query_gain,
    key_gain,
    output_weight,
    hidden_gain,
    gate_weight,
    up_weight,
    down_weight,
    cotangent,
):
    tp_count = lax.axis_size("tp")
    tp_index = lax.axis_index("tp")
    ctx_index = lax.axis_index(CTX)
    batch, own_rows, width = block_in.shape
    rows = batch * own_rows
    ctx_rows = own_rows * tp_count
    places = range(tp_count)
    order = [*range(1, tp_count), 0]
    masks = ctx_masks()
    q_cols = query_weight.shape[1]
    k_cols = key_weight.shape[1]
    qkv_cols = q_cols + 2 * k_cols
    hidden_cols = gate_weight.shape[1]
    q_gain = jnp.tile(query_gain.astype(jnp.float32), 2)[None]
    k_gain = jnp.tile(key_gain.astype(jnp.float32), 2)[None]

    block = width // (lax.axis_size("dp") * lax.axis_size(CTX))
    paired = block % 128 == 0
    pair_first = lax.rem(ctx_index, 2).astype(jnp.int32)[None]

    def meet(arrays):
        return [*arrays, *[ctx_swap(array, 1) for array in arrays]] if paired else list(arrays)

    def grad_product(left, rights, more=0, into=None, tile=512, share=1.0):
        blocks = width // block // 2 if paired else 0
        return product(left, rights, tile, pair_first, blocks, more, into, share)

    def scatter_sum(addend):
        axes = ("dp", CTX[0]) if paired else ("dp", *CTX)
        return lax.psum_scatter(addend, axes, scatter_dimension=0, tiled=True)

    back_places = [(tp_count - place) % tp_count for place in places]
    attention_rows = attention_gain.astype(jnp.float32)[:, None]
    hidden_gain_rows = hidden_gain.astype(jnp.float32)[:, None]
    qkv_weight = jnp.concatenate([query_weight, key_weight, value_weight], axis=1).astype(jnp.float32)
    first_weight = jnp.concatenate(
        [
            (gate_weight.astype(jnp.float32) * hidden_gain_rows).astype(jnp.bfloat16),
            (qkv_weight * attention_rows).astype(jnp.bfloat16),
        ],
        axis=1,
    )
    full_first = gather_weight(first_weight)
    full_qkv = full_first[:, hidden_cols:]

    def chunk_start(place):
        owner = lax.rem(tp_index - place + tp_count, tp_count)
        return owner * own_rows

    def own_part(table, start):
        return lax.dynamic_slice_in_dim(table, start, own_rows, 1)

    iota = jnp.arange(own_rows, dtype=jnp.int32)
    row_starts = [ctx_index * ctx_rows + chunk_start(place) for place in places]
    low = jnp.concatenate([own_part(segments, start) for start in row_starts], axis=1)[:, None]
    high = jnp.concatenate([start + iota for start in row_starts])[None, None]
    starts = jnp.stack(
        [
            jnp.bitwise_xor(ctx_index, mask) * ctx_rows + chunk_start(place)
            for mask in masks
            for place in places
        ]
    ).astype(jnp.int32)
    position = jnp.stack([own_part(positions, start).reshape(rows) for start in row_starts])
    half = HD // 2
    frequency = ROPE_BASE ** (-2.0 * jnp.arange(half, dtype=jnp.float32) / HD)
    sign = jnp.where(jnp.arange(2 * HD) % HD < half, -1.0, 1.0).astype(jnp.float32)
    angles = position.astype(jnp.float32)[..., None] * jnp.tile(frequency, 4)
    cos_wide, sin_wide = jnp.cos(angles), jnp.sin(angles) * sign

    def project(place):
        values = matmul(normed_rows[place], full_qkv)
        query_rot, kv = make_heads(
            values, cos_wide[place], sin_wide[place], q_gain, k_gain, q_cols, k_cols
        )
        return values, query_rot, kv

    def project_and_send(place):
        values, query_rot, kv = project(place)
        blocks = ctx_gather(kv)
        return values, query_rot, blocks

    tokens = block_in.reshape(rows, width)
    normed = unit_of(tokens.astype(jnp.float32))[0].astype(jnp.bfloat16)
    normed, out_own = together(normed, output_weight.T)
    normed_rows, heads = [normed], []
    out_pieces = [out_own]
    for _ in range(2, tp_count):
        out_pieces.append(shift(out_pieces[-1], -1))
    for place in range(1, tp_count):
        came = ring_hop(normed_rows[-1])
        ready = range(tp_count - 2) if place == tp_count - 1 else []
        work = [project_and_send(mine) for mine in ready]
        came, work = together(came, work)
        if place == 1:
            came, out_pieces = together(came, out_pieces)
            out_pieces.append(shift(out_pieces[-1], -1))
            second_weight = jnp.concatenate(
                [*out_pieces, (up_weight.astype(jnp.float32) * hidden_gain_rows).astype(jnp.bfloat16)],
                axis=1,
            )
            full_second = gather_weight(second_weight)
        heads.extend(work)
        normed_rows.append(came)
    last_weight, normed_rows[-1] = together(down_weight.T, normed_rows[-1])
    full_down_t = gather_weight(last_weight)
    full_out, full_gate, full_up, full_down = (full_second, 0), (full_first, 0), (full_second, 1), (full_down_t, 0)

    grad_own, normed_rows[-1] = together(cotangent.reshape(rows, width), normed_rows[-1])
    came = ring_hop(grad_own)
    work = [project_and_send(mine) for mine in range(len(heads), tp_count)]
    came, work = together(came, work)
    heads.extend(work)
    raw, queries, gathered = ([h[i] for h in heads] for i in range(3))
    blocks = [[gathered[place][i] for place in places] for i in range(len(masks))]
    grad_rows = [grad_own, came]
    came = ring_hop(grad_rows[-1])
    attended = attend(starts, low, high, queries, blocks, batch)
    met_normed, mine_qkv = meet(normed_rows), full_qkv
    if paired:
        mine_qkv = lax.dynamic_index_in_dim(
            full_qkv.reshape(width // block // 2, 2, block, qkv_cols), pair_first[0], 1, False
        ).reshape(width // 2, qkv_cols)
    late_qkv, came, attended, met_normed, mine_qkv = together(
        full_qkv, came, attended, met_normed, mine_qkv
    )
    grad_rows.append(came)
    attended_rows, totals = attended[:tp_count], attended[tp_count]
    mine = [attended_rows[0]] + [shift(attended_rows[place], -place) for place in range(1, tp_count)]
    grad_rows[-1], mine = together(grad_rows[-1], mine)
    for _ in range(len(grad_rows), tp_count):
        grad_rows.append(ring_hop(grad_rows[-1]))
    met_grads = meet(grad_rows)
    (mixed_in,) = rows_nt([([[(piece, 0) for piece in mine]], full_out)], jnp.float32, 1, rows)
    met_mine = [meet([piece]) for piece in mine]
    hidden, unit_hidden = add_and_norm(tokens, mixed_in)

    def feed(group):
        return feed_rows(
            [hidden_rows[place] for place in group],
            [grad_rows[place] for place in group],
            full_gate,
            full_up,
            full_down,
            hidden_cols,
        )

    def hidden_terms(fed):
        halves = range(tp_count // 2)
        gates, ups = ([[(fed[part], half)] for half in halves] for part in (1, 2))
        return rows_nt([(gates, full_gate), (ups, full_up)], jnp.bfloat16, len(halves), rows)

    first, second = list(places)[: tp_count // 2], list(places)[tp_count // 2 :]
    hidden_rows = [unit_hidden]
    fed_first, terms_first = None, None
    for place in range(1, tp_count):
        came = ring_hop(hidden_rows[-1])
        if place == len(first):
            fed_first = feed(first)
            came, fed_first, met_grads, met_mine = together(came, fed_first, met_grads, met_mine)
        if place == len(first) + 1:
            met_first = [meet([fed]) for fed in fed_first]
            terms_first = hidden_terms(fed_first)
            came, terms_first, met_first = together(came, terms_first, met_first)
        hidden_rows.append(came)

    came = ring_hop(terms_first[1])
    met_hidden = meet(hidden_rows)
    fed_second = feed(second)
    feed_terms = rows_nt([([[(fed_first[0], 1)]], full_down)], jnp.bfloat16, 1, rows)
    came, fed_second, met_hidden, feed_terms = together(came, fed_second, met_hidden, feed_terms)
    feed_came = ring_hop(feed_terms[0])
    met_fed = [old + meet([fed]) for old, fed in zip(met_first, fed_second)]
    if paired:
        met_fed = [[fed[0], fed[2], fed[1], fed[3]] for fed in met_fed]
    terms_second, feed_came = together(hidden_terms(fed_second), feed_came)
    came = ring_hop(add_rows(came, terms_second[0]))
    down_product = grad_product(met_grads, [met_fed[0]])
    feed_terms += rows_nt([([[(fed_second[0], 0)]], full_down)], jnp.bfloat16, 1, rows)
    came, down_product, feed_terms = together(came, down_product, feed_terms)
    came = ring_hop(add_rows(came, terms_second[1]))
    down_shard = scatter_sum(down_product)
    pair_product = grad_product(met_hidden, [met_fed[1]], more=1)
    feed_rest = rows_nt(
        [([[(fed_second[0], 1)], [(fed_first[0], 0)]], full_down)], jnp.bfloat16, 2, rows
    )
    came, pair_product, feed_rest = together(came, pair_product, feed_rest)
    feed_terms = dict(zip(order, feed_terms + feed_rest))

    grad_hidden, branch = norm_back(
        came, terms_first[0], hidden, grad_own, (jnp.float32, jnp.bfloat16)
    )
    pieces = split_columns(branch, full_second, 0, tp_count, q_cols)
    pieces, branch = together(pieces, branch)
    grad_att = [pieces[0]] + [shift(pieces[place], place) for place in range(1, tp_count)]
    met_branch = meet([branch])
    out_product = grad_product(met_branch, met_mine, share=0.1)
    out_product, pair_product = together(out_product, pair_product)
    pair_product = grad_product(met_hidden, [met_fed[2]], into=pair_product, share=0.1)
    grad_att, pair_product, out_product = together(grad_att, pair_product, out_product)
    out_shard = scatter_sum(out_product)
    pair_shard = scatter_sum(pair_product)

    half_count = len(masks) // 2
    kinds = [
        [jnp.float32] * half_count + [jnp.bfloat16] * half_count,
        [jnp.float32] + [jnp.bfloat16] * (len(masks) - 1),
    ]
    query_gain_sum = jnp.zeros((8, 2 * HD), jnp.float32)
    dq_parts, own_parts, came_parts = [], [], []
    came = feed_came
    for step, place in enumerate(order[1:]):
        if place:
            came = ring_hop(add_rows(came, feed_terms[place]))
        if step < 2:
            dq, back, addend = attend_back(
                starts,
                low,
                high,
                totals,
                cos_wide,
                sin_wide,
                q_gain,
                queries,
                raw,
                grad_att,
                attended_rows,
                blocks,
                kinds[step],
                batch,
                [0, batch - batch // 4][step],
                [batch - batch // 4, batch // 4][step],
            )
            if step == 0:
                came, dq, back, addend, grad_att, down_shard = together(
                    came, dq, back, addend, grad_att, down_shard
                )
            else:
                dq, back, addend, own_parts, came_parts = together(
                    dq, back, addend, own_parts, came_parts
                )
            query_gain_sum = query_gain_sum + addend
            dq_parts.append(dq)
            own_parts.append(back[0])
            if step:
                came_parts.append([ctx_swap(part, mask) for part, mask in zip(back[1:], masks[1:])])
                continue
            bit = 1
            while len(back) > 2:
                half_count = len(back) // 2
                back = [
                    back[i] + ctx_swap(back[half_count + i].astype(jnp.bfloat16), bit).astype(jnp.float32)
                    for i in range(half_count)
                ]
                bit *= 2
            own_parts[0] = back[0]
            came_parts.append([ctx_swap(back[1].astype(jnp.bfloat16), bit)])
        else:
            grad_qkv, key_gain_sum = heads_back(
                dq_parts, own_parts, came_parts, raw, cos_wide, sin_wide, k_gain
            )
            came, grad_qkv, out_shard = together(came, grad_qkv, out_shard)
    feed_out = came.astype(jnp.float32) + feed_terms[0].astype(jnp.float32)
    block_out = (hidden + feed_out).astype(jnp.bfloat16).reshape(block_in.shape)

    def out_hop(total, place):
        start = back_places[place] * q_cols
        total = ring_hop(total).astype(jnp.float32) + out_shard[:, start : start + q_cols].astype(
            jnp.float32
        )
        return total.astype(jnp.bfloat16) if place else total

    met_qkv = meet([grad_qkv])
    row_terms = rows_nt(
        [([[(grad_qkv, place)] for place in places], (late_qkv, 0))], jnp.bfloat16, tp_count, rows
    )
    head_sums = jnp.stack([query_gain_sum, key_gain_sum]).sum(axis=1).reshape(2, 2, HD).sum(axis=1)
    total, met_qkv = together(row_terms[1], met_qkv)
    out_total = out_shard[:, back_places[1] * q_cols : (back_places[1] + 1) * q_cols]
    for step, place in enumerate(order[1:]):
        came = ring_hop(total)
        if step == 2:
            out_total, pair_shard, qkv_product = together(out_total, pair_shard, qkv_product)
            qkv_shard = scatter_sum(qkv_product)
        out_total = out_hop(out_total, place)
        if step < 2:
            came, out_total = together(came, out_total)
        if step == 0:
            head_sums = all_sum(head_sums, (CTX, "dp"))
            qkv_product = grad_product(met_normed, [met_qkv], tile=qkv_cols)
            attention_sum = jnp.sum(qkv_product.astype(jnp.float32) * mine_qkv.astype(jnp.float32), axis=1)
            came, head_sums, qkv_product, attention_sum = together(
                came, head_sums, qkv_product, attention_sum
            )
            small_sums = jnp.concatenate([attention_sum, head_sums.reshape(-1)])
        if step == 1:
            small_sums = all_sum(small_sums, ("tp",))
            came, small_sums = together(came, small_sums)
            head_sums = small_sums[-2 * HD :].reshape(2, HD)
            column = jnp.pad(small_sums[: -2 * HD].astype(jnp.bfloat16)[:, None], ((0, 0), (0, 127)))
            qkv_product = jnp.concatenate([qkv_product, column], axis=1)
        if place:
            total = add_rows(came, row_terms[place])
    pair_sums = pair_shard.astype(jnp.float32)
    gate_sums, up_sums = pair_sums[:, :hidden_cols], pair_sums[:, hidden_cols:]
    hidden_sums = jnp.sum(
        gate_sums * gate_weight.astype(jnp.float32) + up_sums * up_weight.astype(jnp.float32), axis=1
    )
    hidden_gain_grad = hidden_sums
    stages = []
    for stage in range(tp_count.bit_length() - 1):
        stages.append([(i, i ^ (1 << stage)) for i in range(tp_count)])
    hidden_gain_grad = hidden_gain_grad + lax.ppermute(hidden_gain_grad, "tp", stages[0])
    qkv_sums = qkv_shard[:, :qkv_cols].astype(jnp.float32)
    attention_gain_grad = qkv_shard[:, qkv_cols].astype(jnp.float32) / attention_rows[:, 0]
    (input_grad,) = norm_back(came, row_terms[0], tokens, grad_hidden, (jnp.float32,))
    input_grad, hidden_gain_grad = together(input_grad, hidden_gain_grad)
    for pairs in stages[1:]:
        hidden_gain_grad = hidden_gain_grad + lax.ppermute(hidden_gain_grad, "tp", pairs)
    output_grad = out_total.T
    down_grad = down_shard.astype(jnp.float32).T
    gate_grad, up_grad = gate_sums * hidden_gain_rows, up_sums * hidden_gain_rows
    qkv_grad = qkv_sums * attention_rows
    return (
        block_out,
        input_grad.reshape(block_in.shape),
        attention_gain_grad,
        qkv_grad[:, :q_cols],
        qkv_grad[:, q_cols : q_cols + k_cols],
        qkv_grad[:, q_cols + k_cols :],
        head_sums[0],
        head_sums[1],
        output_grad,
        hidden_gain_grad,
        gate_grad,
        up_grad,
        down_grad,
    )


def solution(mesh):
    in_specs = (
        P(None, ("dp", *CTX, "tp"), None),
        P(None, "dp"),
        P(None, "dp"),
        P(("dp", *CTX)),
        P(("dp", *CTX), "tp"),
        P(("dp", *CTX), "tp"),
        P(("dp", *CTX), "tp"),
        P(),
        P(),
        P("tp", ("dp", *CTX)),
        P(("dp", *CTX)),
        P(("dp", *CTX), "tp"),
        P(("dp", *CTX), "tp"),
        P("tp", ("dp", *CTX)),
        P(None, ("dp", *CTX, "tp"), None),
    )
    out_specs = (
        P(None, ("dp", *CTX, "tp"), None),
        P(None, ("dp", *CTX, "tp"), None),
        P(("dp", *CTX)),
        P(("dp", *CTX), "tp"),
        P(("dp", *CTX), "tp"),
        P(("dp", *CTX), "tp"),
        P(),
        P(),
        P("tp", ("dp", *CTX)),
        P(("dp", *CTX)),
        P(("dp", *CTX), "tp"),
        P(("dp", *CTX), "tp"),
        P("tp", ("dp", *CTX)),
    )
    shape = (mesh.shape["dp"], mesh.shape["ctx"] // 2, 2, mesh.shape["tp"])
    split = Mesh(mesh.devices.reshape(shape), ("dp", *CTX, "tp"))
    return jax.shard_map(
        per_device, mesh=split, in_specs=in_specs, out_specs=out_specs, check_vma=False
    )
```

```python
import functools
import math

import jax
import jax.numpy as jnp
from jax import lax
from jax.experimental import pallas as pl
from jax.experimental.pallas import tpu as pltpu
from jax.sharding import Mesh
from jax.sharding import PartitionSpec as P

D = 2048
HD = 64


NORM_EPS = 1e-05
ROPE_BASE = 1000000.0
MASKED = -1e30
CTX = ("ctx_pair", "ctx_place")


def matmul(left_mat, right_mat):
    return jnp.dot(left_mat, right_mat, preferred_element_type=jnp.float32)


def matmul_tn(left_mat, right_mat):
    return lax.dot_general(
        left_mat, right_mat, (((0,), (0,)), ((), ())), preferred_element_type=jnp.float32
    )


def matmul_nt(left_mat, right_mat):
    return lax.dot_general(
        left_mat, right_mat, (((1,), (1,)), ((), ())), preferred_element_type=jnp.float32
    )


def ring_hop(values):
    count = lax.axis_size("tp")
    return lax.ppermute(values, "tp", [(i, (i + 1) % count) for i in range(count)])


def ctx_swap(values, mask):
    count = lax.axis_size(CTX)
    return lax.ppermute(values, CTX, [(i, i ^ mask) for i in range(count)])


def ctx_masks():
    masks = [0]
    bit = lax.axis_size(CTX) // 2
    while bit:
        masks = masks + [mask ^ bit for mask in masks]
        bit //= 2
    return masks


def ctx_gather(own):
    blocks = [own]
    bit = lax.axis_size(CTX) // 2
    while bit:
        blocks = blocks + [ctx_swap(block, bit) for block in blocks]
        bit //= 2
    return blocks


def gather_weight(shard):
    return lax.all_gather(shard, ("dp", *CTX), axis=0, tiled=True)


def all_sum(values, axes):
    for axis in axes:
        count = lax.axis_size(axis)
        bit = 1
        while bit < count:
            values = values + lax.ppermute(values, axis, [(i, i ^ bit) for i in range(count)])
            bit *= 2
    return values


def shift(values, places):
    count = lax.axis_size("tp")
    return lax.ppermute(values, "tp", [(i, (i + places) % count) for i in range(count)])


def together(*values):
    return lax.optimization_barrier(values)


def lane_iota(shape):
    return lax.broadcasted_iota(jnp.int32, shape, 1)


def head_means(values):
    width = values.shape[1]
    row = lax.broadcasted_iota(jnp.int32, (width, width), 0) // HD
    col = lax.broadcasted_iota(jnp.int32, (width, width), 1) // HD
    pick = jnp.where(row == col, 1.0 / HD, 0.0).astype(jnp.float32)
    return jnp.dot(
        values, pick, precision=lax.Precision.HIGHEST, preferred_element_type=jnp.float32
    )


def half_swap(values):
    width, half = values.shape[1], HD // 2
    first = lax.rem(lane_iota(values.shape), HD) < half
    return jnp.where(
        first, pltpu.roll(values, width - half, 1), pltpu.roll(values, half, 1)
    )


def other_head(values):
    return pltpu.roll(values, HD, 1)


def twice(values, head):
    wide = values.astype(jnp.float32)
    low = lane_iota(wide.shape) < HD
    other = other_head(wide)
    both = jnp.where(low, wide, other) if head == 0 else jnp.where(low, other, wide)
    return both.astype(values.dtype)


def apart(values):
    wide = values.astype(jnp.float32)
    low = lane_iota(wide.shape) < HD
    zero = jnp.zeros_like(wide)
    return jnp.concatenate(
        [jnp.where(low, wide, zero), jnp.where(low, zero, wide)], axis=0
    ).astype(values.dtype)


def heads_kernel(raw_ref, cos_ref, sin_ref, q_gain_ref, k_gain_ref, q_ref, kv_ref):
    pair = 2 * HD
    q_cols = q_ref.shape[1]
    k_cols = kv_ref.shape[1] // 2
    cos, sin = cos_ref[...], sin_ref[...]
    for first in range(0, q_cols + k_cols, pair):
        values = raw_ref[:, first : first + pair]
        gain = q_gain_ref[...] if first < q_cols else k_gain_ref[...]
        normed = values * lax.rsqrt(head_means(values * values) + NORM_EPS) * gain
        turned = (normed * cos + half_swap(normed) * sin).astype(jnp.bfloat16)
        if first < q_cols:
            q_ref[:, first : first + pair] = turned
        else:
            kv_ref[:, first - q_cols : first - q_cols + pair] = turned
    kv_ref[:, k_cols:] = raw_ref[:, q_cols + k_cols :].astype(jnp.bfloat16)


def make_heads(raw, cos_wide, sin_wide, q_gain, k_gain, q_cols, k_cols):
    rows = raw.shape[0]
    return pl.pallas_call(
        heads_kernel,
        out_shape=(
            jax.ShapeDtypeStruct((rows, q_cols), jnp.bfloat16),
            jax.ShapeDtypeStruct((rows, 2 * k_cols), jnp.bfloat16),
        ),
        cost_estimate=pl.CostEstimate(
            flops=rows * raw.shape[1] * 400, bytes_accessed=rows * raw.shape[1] * 7, transcendentals=0
        ),
        name="make_heads",
    )(raw, cos_wide, sin_wide, q_gain, k_gain)


def turn_back(grad, values, gain, cos, sin):
    turned = grad * cos - half_swap(grad) * sin
    scale = lax.rsqrt(head_means(values * values) + NORM_EPS)
    unit = values * scale
    scaled = turned * gain
    return scale * (scaled - unit * head_means(scaled * unit)), turned * unit


def fill_bias(starts_ref, low_ref, high_ref, bias_ref, piece):
    low, high = low_ref[0], high_ref[0]
    for i in range(bias_ref.shape[0] // piece):
        place = starts_ref[i] + lax.broadcasted_iota(jnp.int32, (piece, low.shape[1]), 0)
        linked = (place >= low) & (place <= high)
        bias = jnp.where(linked, 0.0, MASKED)
        bias_ref[i * piece : (i + 1) * piece, : low.shape[1]] = bias
        bias_ref[i * piece : (i + 1) * piece, low.shape[1] :] = bias


def attend_kernel(places, blocks, block_keys, *refs):
    starts_ref, low_ref, high_ref = refs[:3]
    q_refs = refs[3 : 3 + places]
    kv_refs = refs[3 + places : 3 + places + blocks * places]
    refs = refs[3 + places + blocks * places :]
    out_refs = refs[:places]
    total_ref, bias_ref, key_ref, value_ref = refs[places:]
    pair = 2 * HD
    piece, q_cols = q_refs[0].shape
    rows = places * piece
    k_cols = kv_refs[0].shape[1] // 2
    k_heads = k_cols // HD
    group = q_cols // k_cols
    scale = math.log2(math.e) / math.sqrt(HD)
    fill_bias(starts_ref, low_ref, high_ref, bias_ref, piece)
    for block in range(blocks):
        mine = kv_refs[block * places : (block + 1) * places]
        for head in range(k_heads):
            cols = slice(head // 2 * pair, head // 2 * pair + pair)
            vcols = slice(k_cols + head // 2 * pair, k_cols + head // 2 * pair + pair)
            where = slice(block * block_keys, (block + 1) * block_keys)
            keys = jnp.concatenate([ref[:, cols] for ref in mine], axis=0)
            key_ref[head, where, :] = twice(keys, head % 2)
            if head % 2 == 0:
                values = jnp.concatenate([ref[:, vcols] for ref in mine], axis=0)
                value_ref[head // 2, :, where] = values.astype(jnp.float32).T.astype(jnp.bfloat16)
    for first in range(0, q_cols, pair):
        head = first // HD // group
        queries = apart(jnp.concatenate([q_ref[:, first : first + pair] for q_ref in q_refs], axis=0))

        mixed = jnp.zeros((HD, 2 * rows), jnp.float32)
        total = jnp.zeros((1, 2 * rows), jnp.float32)
        for block in range(blocks):
            where = slice(block * block_keys, (block + 1) * block_keys)
            scores = matmul_nt(key_ref[head, where, :], queries)
            weight = jnp.exp2(scores * scale + bias_ref[where, :])
            total = total + jnp.sum(weight, axis=0, keepdims=True)
            values = value_ref[head // 2, head % 2 * HD : (head % 2 + 1) * HD, where]
            mixed = mixed + matmul(values, weight.astype(jnp.bfloat16))
        mixed = mixed / total
        out = jnp.concatenate([mixed[:, :rows], mixed[:, rows:]], axis=0).T.astype(jnp.bfloat16)
        for place in range(places):
            out_refs[place][:, first : first + pair] = out[place * piece : (place + 1) * piece]
        total_ref[0, first // pair, :] = jnp.log2(total)[0]


def attend(starts, low, high, q_chunks, kv_blocks, batch):
    places, blocks = len(q_chunks), len(kv_blocks)
    kv_flat = [kv for block in kv_blocks for kv in block]
    rows, q_cols = q_chunks[0].shape
    piece = rows // batch
    kv_cols = kv_flat[0].shape[1]
    k_cols = kv_cols // 2
    keys = blocks * places * piece
    q_rows = places * piece
    pairs = q_cols // (2 * HD)
    q_spec = pl.BlockSpec((piece, q_cols), lambda b: (b, 0))
    kv_spec = pl.BlockSpec((piece, kv_cols), lambda b: (b, 0))
    line_spec = pl.BlockSpec((1, 1, q_rows), lambda b: (b, 0, 0))
    work = batch * q_cols // HD * q_rows * keys
    results = pl.pallas_call(
        functools.partial(attend_kernel, places, blocks, places * piece),
        grid=(batch,),
        out_shape=tuple(
            [jax.ShapeDtypeStruct((rows, q_cols), jnp.bfloat16)] * places
            + [jax.ShapeDtypeStruct((batch, pairs, 2 * q_rows), jnp.float32)]
        ),
        in_specs=[
            pl.BlockSpec(memory_space=pltpu.SMEM),
            line_spec,
            pl.BlockSpec((1, 1, q_rows), lambda b: (0, 0, 0)),
        ]
        + [q_spec] * places
        + [kv_spec] * len(kv_flat),
        out_specs=tuple(
            [q_spec] * places + [pl.BlockSpec((1, pairs, 2 * q_rows), lambda b: (b, 0, 0))]
        ),
        scratch_shapes=[
            pltpu.VMEM((keys, 2 * q_rows), jnp.float32),
            pltpu.VMEM((k_cols // HD, keys, 2 * HD), jnp.bfloat16),
            pltpu.VMEM((k_cols // HD // 2, 2 * HD, keys), jnp.bfloat16),
        ],
        cost_estimate=pl.CostEstimate(
            flops=work * 4 * HD * 4, bytes_accessed=batch * q_rows * q_cols * 8, transcendentals=work
        ),
        name="attend",
    )(starts, low, high, *q_chunks, *kv_flat)
    return list(results)


def attend_back_kernel(places, blocks, block_keys, *refs):
    starts_ref, low_ref, high_ref, total_ref, cos_ref, sin_ref, gain_ref = refs[:7]
    refs = refs[7:]
    q_refs, refs = refs[:places], refs[places:]
    raw_refs, refs = refs[:places], refs[places:]
    grad_refs, refs = refs[:places], refs[places:]
    mixed_refs, refs = refs[:places], refs[places:]
    kv_refs, refs = refs[: blocks * places], refs[blocks * places :]
    dq_ref, refs = refs[0], refs[1:]
    dkv_refs, refs = refs[:blocks], refs[blocks:]
    gain_sum_ref, bias_ref, key_ref, turned_ref, value_ref, dkey_ref, dvalue_ref = refs
    pair = 2 * HD
    piece, q_cols = q_refs[0].shape
    rows = places * piece
    k_cols = kv_refs[0].shape[1] // 2
    k_heads = k_cols // HD
    group = q_cols // k_cols
    inv_root = 1.0 / math.sqrt(HD)
    scale = math.log2(math.e) * inv_root
    fill_bias(starts_ref, low_ref, high_ref, bias_ref, piece)

    @pl.when(pl.program_id(0) == 0)
    def _():
        gain_sum_ref[...] = jnp.zeros_like(gain_sum_ref)

    for block in range(blocks):
        mine = kv_refs[block * places : (block + 1) * places]
        for head in range(k_heads):
            cols = slice(head // 2 * pair, head // 2 * pair + pair)
            vcols = slice(k_cols + head // 2 * pair, k_cols + head // 2 * pair + pair)
            where = slice(block * block_keys, (block + 1) * block_keys)
            keys = jnp.concatenate([ref[:, cols] for ref in mine], axis=0)
            values = jnp.concatenate([ref[:, vcols] for ref in mine], axis=0)
            key_ref[head, where, :] = twice(keys, head % 2)
            value_ref[head, where, :] = twice(values, head % 2)
            if head % 2 == 0:
                turned_ref[head // 2, :, where] = keys.astype(jnp.float32).T.astype(jnp.bfloat16)
    for first in range(0, q_cols, pair):
        head = first // HD // group
        fresh = first % (group * HD) == 0
        queries = apart(jnp.concatenate([q_ref[:, first : first + pair] for q_ref in q_refs], axis=0))
        grads = apart(jnp.concatenate([g_ref[:, first : first + pair] for g_ref in grad_refs], axis=0))
        total = total_ref[0, first // pair : first // pair + 1, :]

        mixed = apart(jnp.concatenate([m_ref[:, first : first + pair] for m_ref in mixed_refs], axis=0))
        delta = jnp.sum((grads.astype(jnp.float32) * mixed.astype(jnp.float32)).T, axis=0, keepdims=True)
        dquery = jnp.zeros((HD, 2 * rows), jnp.float32)
        for block in range(blocks):
            where = slice(block * block_keys, (block + 1) * block_keys)
            scores = matmul_nt(key_ref[head, where, :], queries)
            dprob = matmul_nt(value_ref[head, where, :], grads)
            prob = jnp.exp2(scores * scale + bias_ref[where, :] - total)
            dscore = (prob * (dprob - delta)).astype(jnp.bfloat16)
            dvalue = matmul(prob.astype(jnp.bfloat16), grads)
            dkey = matmul(dscore, queries)
            if fresh:
                dvalue_ref[head, where, :] = dvalue
                dkey_ref[head, where, :] = dkey
            else:
                dvalue_ref[head, where, :] += dvalue
                dkey_ref[head, where, :] += dkey
            keys = turned_ref[head // 2, head % 2 * HD : (head % 2 + 1) * HD, where]
            dquery = dquery + matmul(keys, dscore)
        dquery = dquery * inv_root
        dquery = jnp.concatenate([dquery[:, :rows], dquery[:, rows:]], axis=0).T
        raw = jnp.concatenate([raw_ref[:, first : first + pair] for raw_ref in raw_refs], axis=0)
        dq, addend = turn_back(
            dquery, raw, gain_ref[...], cos_ref[...].reshape(rows, pair), sin_ref[...].reshape(rows, pair)
        )
        gain_sum_ref[...] += jnp.sum(addend.reshape(-1, 8, pair), axis=0)
        dq_ref[:, :, first : first + pair] = dq.reshape(places, piece, pair).astype(jnp.bfloat16)
    low = lane_iota((block_keys, pair)) < HD
    for block in range(blocks):
        where = slice(block * block_keys, (block + 1) * block_keys)
        for first in range(0, k_heads, 2):
            for shift, ref, factor in ((0, dkey_ref, inv_root), (k_cols, dvalue_ref, 1.0)):
                one, two = ref[first, where, :], ref[first + 1, where, :]
                sums = jnp.where(low, one + other_head(one), two + other_head(two)) * factor
                cols = slice(shift + first // 2 * pair, shift + first // 2 * pair + pair)
                dkv_refs[block][:, :, cols] = sums.reshape(places, piece, pair).astype(
                    dkv_refs[block].dtype
                )


def attend_back(
    starts,
    low,
    high,
    totals,
    cos_wide,
    sin_wide,
    q_gain,
    q_chunks,
    raw_chunks,
    grad_chunks,
    mixed_chunks,
    kv_blocks,
    kinds,
    batch,
    base,
    count,
):
    places, blocks = len(q_chunks), len(kv_blocks)
    kv_flat = [kv for block in kv_blocks for kv in block]
    rows, q_cols = q_chunks[0].shape
    piece = rows // batch
    kv_cols = kv_flat[0].shape[1]
    k_cols = kv_cols // 2
    keys = blocks * places * piece
    q_rows = places * piece
    pairs = q_cols // (2 * HD)
    k_heads = k_cols // HD
    q_spec = pl.BlockSpec((piece, q_cols), lambda b: (base + b, 0))
    kv_spec = pl.BlockSpec((piece, kv_cols), lambda b: (base + b, 0))
    line_spec = pl.BlockSpec((1, 1, q_rows), lambda b: (base + b, 0, 0))
    turn_spec = pl.BlockSpec((places, piece, 2 * HD), lambda b: (0, base + b, 0))
    work = count * q_cols // HD * q_rows * keys
    results = pl.pallas_call(
        functools.partial(attend_back_kernel, places, blocks, places * piece),
        grid=(count,),
        out_shape=tuple(
            [jax.ShapeDtypeStruct((places, count * piece, q_cols), jnp.bfloat16)]
            + [jax.ShapeDtypeStruct((places, count * piece, kv_cols), kind) for kind in kinds]
            + [jax.ShapeDtypeStruct((8, 2 * HD), jnp.float32)]
        ),
        in_specs=[
            pl.BlockSpec(memory_space=pltpu.SMEM),
            line_spec,
            pl.BlockSpec((1, 1, q_rows), lambda b: (0, 0, 0)),
            pl.BlockSpec((1, pairs, 2 * q_rows), lambda b: (base + b, 0, 0)),
            turn_spec,
            turn_spec,
            pl.BlockSpec((1, 2 * HD), lambda b: (0, 0)),
        ]
        + [q_spec] * (4 * places)
        + [kv_spec] * len(kv_flat),
        out_specs=tuple(
            [pl.BlockSpec((places, piece, q_cols), lambda b: (0, b, 0))]
            + [pl.BlockSpec((places, piece, kv_cols), lambda b: (0, b, 0))] * blocks
            + [pl.BlockSpec((8, 2 * HD), lambda b: (0, 0))]
        ),
        scratch_shapes=[
            pltpu.VMEM((keys, 2 * q_rows), jnp.float32),
            pltpu.VMEM((k_heads, keys, 2 * HD), jnp.bfloat16),
            pltpu.VMEM((k_heads // 2, 2 * HD, keys), jnp.bfloat16),
            pltpu.VMEM((k_heads, keys, 2 * HD), jnp.bfloat16),
            pltpu.VMEM((k_heads, keys, 2 * HD), jnp.float32),
            pltpu.VMEM((k_heads, keys, 2 * HD), jnp.float32),
        ],
        cost_estimate=pl.CostEstimate(
            flops=work * 10 * HD * 4, bytes_accessed=count * q_rows * q_cols * 16, transcendentals=work
        ),
        name="attend_back",
    )(
        starts,
        low,
        high,
        totals,
        cos_wide,
        sin_wide,
        q_gain,
        *q_chunks,
        *raw_chunks,
        *grad_chunks,
        *mixed_chunks,
        *kv_flat,
    )
    return results[0], list(results[1:-1]), results[-1]


def heads_back_kernel(places, came_counts, q_cols, *refs):
    parts = len(came_counts)
    dq_refs, refs = refs[:parts], refs[parts:]
    own_refs, refs = refs[:parts], refs[parts:]
    came_refs = []
    for count in came_counts:
        came_refs.append(refs[:count])
        refs = refs[count:]
    raw_refs, refs = refs[:places], refs[places:]
    cos_ref, sin_ref, gain_ref, out_ref, gain_sum_ref = refs
    rows = raw_refs[0].shape[0]
    k_cols = own_refs[0].shape[2] // 2
    pair = 2 * HD
    addends = jnp.zeros((8, pair), jnp.float32)
    for place in range(places):
        start = 0
        for part in range(parts):
            stop = start + own_refs[part].shape[1]
            mine = slice(start, stop)
            out = slice(place * rows + start, place * rows + stop)
            start = stop
            out_ref[out, :q_cols] = dq_refs[part][place]
            grads = own_refs[part][place]
            for came_ref in came_refs[part]:
                grads = grads + came_ref[place].astype(jnp.float32)
            for first in range(0, k_cols, pair):
                cols = slice(first, first + pair)
                dk, addend = turn_back(
                    grads[:, cols],
                    raw_refs[place][mine, cols],
                    gain_ref[...],
                    cos_ref[place, mine],
                    sin_ref[place, mine],
                )
                out_ref[out, q_cols + first : q_cols + first + pair] = dk.astype(jnp.bfloat16)
                addends = addends + jnp.sum(addend.reshape(-1, 8, pair), axis=0)
            out_ref[out, q_cols + k_cols :] = grads[:, k_cols:].astype(jnp.bfloat16)
    gain_sum_ref[...] = addends


def heads_back(dq_parts, own_parts, came_parts, raw_chunks, cos_wide, sin_wide, k_gain):
    parts, places = len(dq_parts), len(raw_chunks)
    rows = raw_chunks[0].shape[0]
    q_cols, kv_cols = dq_parts[0].shape[2], own_parts[0].shape[2]
    k_cols = kv_cols // 2

    def whole(array):
        return pl.BlockSpec(array.shape, lambda i: (0,) * array.ndim)

    inputs = [*dq_parts, *own_parts, *[came for part in came_parts for came in part]]
    turns = [cos_wide, sin_wide, k_gain]
    return pl.pallas_call(
        functools.partial(heads_back_kernel, places, [len(part) for part in came_parts], q_cols),
        grid=(1,),
        out_shape=(
            jax.ShapeDtypeStruct((places * rows, q_cols + kv_cols), jnp.bfloat16),
            jax.ShapeDtypeStruct((8, 2 * HD), jnp.float32),
        ),
        in_specs=[whole(array) for array in inputs]
        + [pl.BlockSpec((rows, k_cols), lambda i: (0, q_cols // k_cols))] * places
        + [whole(array) for array in turns],
        out_specs=(
            pl.BlockSpec((places * rows, q_cols + kv_cols), lambda i: (0, 0)),
            pl.BlockSpec((8, 2 * HD), lambda i: (0, 0)),
        ),
        cost_estimate=pl.CostEstimate(
            flops=places * rows * kv_cols * 400, bytes_accessed=places * rows * 4096, transcendentals=0
        ),
        name="heads_back",
    )(*inputs, *raw_chunks, *turns)


def feed_kernel(count, *refs):
    hidden_refs, grad_refs = refs[:count], refs[count : 2 * count]
    gate_ref, up_ref, down_ref, act_ref, dgate_ref, dup_ref, hidden, grads = refs[2 * count :]

    @pl.when(pl.program_id(0) == 0)
    def _():
        rows = hidden_refs[0].shape[0]
        for i in range(count):
            hidden[i * rows : (i + 1) * rows, :] = hidden_refs[i][...]
            grads[i * rows : (i + 1) * rows, :] = grad_refs[i][...]

    gate = matmul(hidden[...], gate_ref[...])
    up = matmul(hidden[...], up_ref[...])
    grad = matmul(grads[...], down_ref[...])
    sigmoid = 1.0 / (1.0 + jnp.exp(-gate))
    silu = gate * sigmoid
    act_ref[...] = (silu * up).astype(jnp.bfloat16)
    dgate_ref[...] = (grad * up * sigmoid * (1.0 + gate * (1.0 - sigmoid))).astype(jnp.bfloat16)
    dup_ref[...] = (grad * silu).astype(jnp.bfloat16)


def feed_rows(hidden_rows, grad_rows, gate, up, down_t, cols):
    count = len(hidden_rows)
    rows, width = hidden_rows[0].shape
    total = count * rows
    tile = min(cols, 512 if count == 1 else 256)
    steps = cols // tile
    row_spec = pl.BlockSpec((rows, width), lambda j: (0, 0))
    out_spec = pl.BlockSpec((total, tile), lambda j: (0, j))

    def weight_spec(weight):
        return pl.BlockSpec((width, tile), lambda j: (0, weight[1] * steps + j))

    return pl.pallas_call(
        functools.partial(feed_kernel, count),
        grid=(steps,),
        out_shape=tuple([jax.ShapeDtypeStruct((total, cols), jnp.bfloat16)] * 3),
        in_specs=[row_spec] * (2 * count)
        + [
            weight_spec(gate),
            weight_spec(up),
            weight_spec(down_t),
        ],
        out_specs=tuple([out_spec] * 3),
        scratch_shapes=[pltpu.VMEM((total, width), jnp.bfloat16)] * 2,
        cost_estimate=pl.CostEstimate(
            flops=6 * total * width * cols,
            bytes_accessed=6 * width * cols + 4 * total * width + 6 * total * cols,
            transcendentals=total * cols,
        ),
        name="feed_rows",
    )(*hidden_rows, *grad_rows, gate[0], up[0], down_t[0])


def fill_rows(parts, whole):
    row = 0
    for line in parts:
        col = 0
        for ref in line:
            rows, cols = ref.shape
            whole[row : row + rows, col : col + cols] = ref[...]
            col += cols
        row += rows


def rows_nt_kernel(layouts, *refs):
    count = len(layouts)
    parts = []
    for lines, cols in layouts:
        parts.append([refs[i * cols : (i + 1) * cols] for i in range(lines)])
        refs = refs[lines * cols :]
    weight_refs, out_refs, wholes = refs[:count], refs[count:-count], refs[-count:]

    @pl.when(pl.program_id(0) == 0)
    def _():
        for part, whole in zip(parts, wholes):
            fill_rows(part, whole)

    result = matmul_nt(wholes[0][...], weight_refs[0][...])
    for weight_ref, whole in zip(weight_refs[1:], wholes[1:]):
        result = result + matmul_nt(whole[...], weight_ref[...])
    rows = out_refs[0].shape[0]
    for i, out_ref in enumerate(out_refs):
        out_ref[...] = result[i * rows : (i + 1) * rows].astype(out_ref.dtype)


def rows_nt(addends, kind, outs, rows_each, tile=512):
    layouts, parts, depths = [], [], []
    for lines, _ in addends:
        layouts.append((len(lines), len(lines[0])))
        parts.extend(part for line in lines for part in line)
        depths.append(sum(part[0].shape[1] for part in lines[0]))
    rows = rows_each * len(addends[0][0])
    weights = [weight for _, weight in addends]
    width = weights[0][0].shape[0]

    def part_spec(part):
        return pl.BlockSpec((rows_each, part[0].shape[1]), lambda j: (part[1], 0))

    def weight_spec(weight, depth):
        return pl.BlockSpec((tile, depth), lambda j: (j, weight[1]))

    results = pl.pallas_call(
        functools.partial(rows_nt_kernel, layouts),
        grid=(width // tile,),
        out_shape=tuple([jax.ShapeDtypeStruct((rows // outs, width), kind)] * outs),
        in_specs=[part_spec(part) for part in parts]
        + [weight_spec(weight, depth) for weight, depth in zip(weights, depths)],
        out_specs=tuple([pl.BlockSpec((rows // outs, tile), lambda j: (0, j))] * outs),
        scratch_shapes=[pltpu.VMEM((rows, depth), jnp.bfloat16) for depth in depths],
        cost_estimate=pl.CostEstimate(
            flops=2 * rows * sum(depths) * width,
            bytes_accessed=2 * sum(depths) * (rows + width) + 2 * rows * width,
            transcendentals=0,
        ),
        name="rows_nt",
    )(*[part[0] for part in parts], *[weight[0] for weight in weights])
    return list(results)


def add_kernel(one_ref, two_ref, out_ref):
    out_ref[...] = (one_ref[...].astype(jnp.float32) + two_ref[...].astype(jnp.float32)).astype(
        out_ref.dtype
    )


def add_rows(one, two, tile=1024):
    rows, cols = one.shape
    spec = pl.BlockSpec((rows, tile), lambda j: (0, j))
    return pl.pallas_call(
        add_kernel,
        grid=(cols // tile,),
        out_shape=jax.ShapeDtypeStruct(one.shape, one.dtype),
        in_specs=[spec, spec],
        out_specs=spec,
        cost_estimate=pl.CostEstimate(flops=rows * cols, bytes_accessed=6 * rows * cols, transcendentals=0),
        name="add_rows",
    )(one, two)


def split_kernel(rows_ref, weight_ref, *out_refs):
    result = matmul(rows_ref[...], weight_ref[...]).astype(jnp.bfloat16)
    for i, out_ref in enumerate(out_refs):

        @pl.when(pl.program_id(0) == i)
        def _():
            out_ref[...] = result


def split_columns(rows, weight, first, count, cols):
    total, depth = rows.shape
    return pl.pallas_call(
        split_kernel,
        grid=(count,),
        out_shape=tuple([jax.ShapeDtypeStruct((total, cols), jnp.bfloat16)] * count),
        in_specs=[
            pl.BlockSpec((total, depth), lambda j: (0, 0)),
            pl.BlockSpec((depth, cols), lambda j: (0, first + j)),
        ],
        out_specs=tuple([pl.BlockSpec((total, cols), lambda j: (0, 0))] * count),
        cost_estimate=pl.CostEstimate(
            flops=2 * total * depth * cols * count,
            bytes_accessed=2 * (total * depth + depth * cols * count + total * cols * count),
            transcendentals=0,
        ),
        name="split_columns",
    )(rows, weight)


def product_kernel(left_count, right_counts, blocks, skip, first_ref, *refs):
    left_refs, refs = refs[:left_count], refs[left_count:]
    rights = []
    for count in right_counts:
        rights.append(refs[:count])
        refs = refs[count:]
    out_ref, left, right = refs[skip:]
    steps = pl.num_programs(0) // len(rights)

    @pl.when(pl.program_id(0) == 0)
    def _():
        if blocks:
            cols = left.shape[1] // blocks
            row = 0
            for ref in left_refs:
                rows = ref.shape[0]
                for i in range(blocks):
                    start = pl.multiple_of((2 * i + first_ref[0]) * cols, cols)
                    left[row : row + rows, i * cols : (i + 1) * cols] = ref[:, pl.ds(start, cols)]
                row += rows
        else:
            fill_rows([[ref] for ref in left_refs], left)

    for i, refs in enumerate(rights):

        @pl.when(pl.program_id(0) // steps == i)
        def _():
            fill_rows([[ref] for ref in refs], right)

    out_ref[...] = matmul_tn(left[...], right[...]).astype(jnp.bfloat16)


def product(left, rights, tile=512, first=None, blocks=0, more=0, into=None, share=1.0):
    width, cols = left[0].shape[1], rights[0][0].shape[1]
    depth = sum(part.shape[0] for part in left)
    tile = min(tile, cols)
    steps = cols // tile
    out_rows = width // 2 if blocks else width
    first = jnp.zeros((1,), jnp.int32) if first is None else first
    taken = [] if into is None else [into]
    out_cols = into.shape[1] if taken else cols * (len(rights) + more)
    skipped = out_cols // tile - steps * len(rights) if taken else 0
    operands = 1 + len(left) + sum(len(parts) for parts in rights)

    def right_spec(part, index):
        return pl.BlockSpec(
            (part.shape[0], tile), lambda j: (0, jnp.clip(j - index * steps, 0, steps - 1))
        )

    return pl.pallas_call(
        functools.partial(
            product_kernel, len(left), [len(parts) for parts in rights], blocks, len(taken)
        ),
        grid=(steps * len(rights),),
        out_shape=jax.ShapeDtypeStruct((out_rows, out_cols), jnp.bfloat16),
        in_specs=[pl.BlockSpec(memory_space=pltpu.SMEM)]
        + [pl.BlockSpec(part.shape, lambda j: (0, 0)) for part in left]
        + [right_spec(part, index) for index, parts in enumerate(rights) for part in parts]
        + [pl.BlockSpec(memory_space=pl.ANY)] * len(taken),
        out_specs=pl.BlockSpec((out_rows, tile), lambda j: (0, skipped + j)),
        input_output_aliases={operands: 0} if taken else {},
        scratch_shapes=[
            pltpu.VMEM((depth, out_rows), jnp.bfloat16),
            pltpu.VMEM((depth, tile), jnp.bfloat16),
        ],
        cost_estimate=pl.CostEstimate(
            flops=int(share * 2 * depth * out_rows * cols * len(rights)),
            bytes_accessed=int(share * 2 * (depth * width + (depth + out_rows) * cols * len(rights))),
            transcendentals=0,
        ),
        name="product",
    )(first, *left, *[part for parts in rights for part in parts], *taken)


def unit_of(values):
    scale = lax.rsqrt(jnp.mean(values * values, axis=-1, keepdims=True) + NORM_EPS)
    return values * scale, scale


def norm_kernel(rows_ref, more_ref, sum_ref, unit_ref):
    values = rows_ref[...].astype(jnp.float32) + more_ref[...]
    sum_ref[...] = values
    unit_ref[...] = unit_of(values)[0].astype(jnp.bfloat16)


def add_and_norm(rows, more, tile=64):
    count, width = rows.shape
    spec = pl.BlockSpec((tile, width), lambda i: (i, 0))
    return pl.pallas_call(
        norm_kernel,
        grid=(count // tile,),
        out_shape=(
            jax.ShapeDtypeStruct(rows.shape, jnp.float32),
            jax.ShapeDtypeStruct(rows.shape, jnp.bfloat16),
        ),
        in_specs=[spec, spec],
        out_specs=(spec, spec),
        cost_estimate=pl.CostEstimate(
            flops=5 * count * width, bytes_accessed=12 * count * width, transcendentals=0
        ),
        name="add_and_norm",
    )(rows, more)


def norm_back_kernel(one_ref, two_ref, rows_ref, base_ref, *out_refs):
    scaled = one_ref[...].astype(jnp.float32) + two_ref[...].astype(jnp.float32)
    unit, scale = unit_of(rows_ref[...].astype(jnp.float32))
    result = base_ref[...].astype(jnp.float32) + scale * (
        scaled - unit * jnp.mean(scaled * unit, axis=-1, keepdims=True)
    )
    for out_ref in out_refs:
        out_ref[...] = result.astype(out_ref.dtype)


def norm_back(one, two, rows, base, kinds, tile=64):
    count, width = rows.shape
    spec = pl.BlockSpec((tile, width), lambda i: (i, 0))
    return pl.pallas_call(
        norm_back_kernel,
        grid=(count // tile,),
        out_shape=tuple(jax.ShapeDtypeStruct(rows.shape, kind) for kind in kinds),
        in_specs=[spec] * 4,
        out_specs=tuple([spec] * len(kinds)),
        cost_estimate=pl.CostEstimate(
            flops=10 * count * width, bytes_accessed=14 * count * width, transcendentals=0
        ),
        name="norm_back",
    )(one, two, rows, base)


def per_device(
    block_in,
    segments,
    positions,
    attention_gain,
    query_weight,
    key_weight,
    value_weight,
    query_gain,
    key_gain,
    output_weight,
    hidden_gain,
    gate_weight,
    up_weight,
    down_weight,
    cotangent,
):
    tp_count = lax.axis_size("tp")
    tp_index = lax.axis_index("tp")
    ctx_index = lax.axis_index(CTX)
    batch, own_rows, width = block_in.shape
    rows = batch * own_rows
    ctx_rows = own_rows * tp_count
    places = range(tp_count)
    order = [*range(1, tp_count), 0]
    masks = ctx_masks()
    q_cols = query_weight.shape[1]
    k_cols = key_weight.shape[1]
    qkv_cols = q_cols + 2 * k_cols
    hidden_cols = gate_weight.shape[1]
    q_gain = jnp.tile(query_gain.astype(jnp.float32), 2)[None]
    k_gain = jnp.tile(key_gain.astype(jnp.float32), 2)[None]

    block = width // (lax.axis_size("dp") * lax.axis_size(CTX))
    paired = block % 128 == 0
    pair_first = lax.rem(ctx_index, 2).astype(jnp.int32)[None]

    def meet(arrays):
        return [*arrays, *[ctx_swap(array, 1) for array in arrays]] if paired else list(arrays)

    def grad_product(left, rights, more=0, into=None, tile=512, share=1.0):
        blocks = width // block // 2 if paired else 0
        return product(left, rights, tile, pair_first, blocks, more, into, share)

    def scatter_sum(addend):
        axes = ("dp", CTX[0]) if paired else ("dp", *CTX)
        return lax.psum_scatter(addend, axes, scatter_dimension=0, tiled=True)

    back_places = [(tp_count - place) % tp_count for place in places]
    attention_rows = attention_gain.astype(jnp.float32)[:, None]
    hidden_gain_rows = hidden_gain.astype(jnp.float32)[:, None]
    qkv_weight = jnp.concatenate([query_weight, key_weight, value_weight], axis=1).astype(jnp.float32)
    first_weight = jnp.concatenate(
        [
            (gate_weight.astype(jnp.float32) * hidden_gain_rows).astype(jnp.bfloat16),
            (qkv_weight * attention_rows).astype(jnp.bfloat16),
        ],
        axis=1,
    )
    full_first = gather_weight(first_weight)
    full_qkv = full_first[:, hidden_cols:]

    def chunk_start(place):
        owner = lax.rem(tp_index - place + tp_count, tp_count)
        return owner * own_rows

    def own_part(table, start):
        return lax.dynamic_slice_in_dim(table, start, own_rows, 1)

    iota = jnp.arange(own_rows, dtype=jnp.int32)
    row_starts = [ctx_index * ctx_rows + chunk_start(place) for place in places]
    low = jnp.concatenate([own_part(segments, start) for start in row_starts], axis=1)[:, None]
    high = jnp.concatenate([start + iota for start in row_starts])[None, None]
    starts = jnp.stack(
        [
            jnp.bitwise_xor(ctx_index, mask) * ctx_rows + chunk_start(place)
            for mask in masks
            for place in places
        ]
    ).astype(jnp.int32)
    position = jnp.stack([own_part(positions, start).reshape(rows) for start in row_starts])
    half = HD // 2
    frequency = ROPE_BASE ** (-2.0 * jnp.arange(half, dtype=jnp.float32) / HD)
    sign = jnp.where(jnp.arange(2 * HD) % HD < half, -1.0, 1.0).astype(jnp.float32)
    angles = position.astype(jnp.float32)[..., None] * jnp.tile(frequency, 4)
    cos_wide, sin_wide = jnp.cos(angles), jnp.sin(angles) * sign

    def project(place):
        values = matmul(normed_rows[place], full_qkv)
        query_rot, kv = make_heads(
            values, cos_wide[place], sin_wide[place], q_gain, k_gain, q_cols, k_cols
        )
        return values, query_rot, kv

    def project_and_send(place):
        values, query_rot, kv = project(place)
        blocks = ctx_gather(kv)
        return values, query_rot, blocks

    tokens = block_in.reshape(rows, width)
    normed = unit_of(tokens.astype(jnp.float32))[0].astype(jnp.bfloat16)
    normed, out_own = together(normed, output_weight.T)
    normed_rows, heads = [normed], []
    out_pieces = [out_own]
    for _ in range(2, tp_count):
        out_pieces.append(shift(out_pieces[-1], -1))
    for place in range(1, tp_count):
        came = ring_hop(normed_rows[-1])
        ready = range(tp_count - 2) if place == tp_count - 1 else []
        work = [project_and_send(mine) for mine in ready]
        came, work = together(came, work)
        if place == 1:
            came, out_pieces = together(came, out_pieces)
            out_pieces.append(shift(out_pieces[-1], -1))
            second_weight = jnp.concatenate(
                [*out_pieces, (up_weight.astype(jnp.float32) * hidden_gain_rows).astype(jnp.bfloat16)],
                axis=1,
            )
            full_second = gather_weight(second_weight)
        heads.extend(work)
        normed_rows.append(came)
    last_weight, normed_rows[-1] = together(down_weight.T, normed_rows[-1])
    full_down_t = gather_weight(last_weight)
    full_out, full_gate, full_up, full_down = (full_second, 0), (full_first, 0), (full_second, 1), (full_down_t, 0)

    grad_own, normed_rows[-1] = together(cotangent.reshape(rows, width), normed_rows[-1])
    came = ring_hop(grad_own)
    work = [project_and_send(mine) for mine in range(len(heads), tp_count)]
    came, work = together(came, work)
    heads.extend(work)
    raw, queries, gathered = ([h[i] for h in heads] for i in range(3))
    blocks = [[gathered[place][i] for place in places] for i in range(len(masks))]
    grad_rows = [grad_own, came]
    came = ring_hop(grad_rows[-1])
    attended = attend(starts, low, high, queries, blocks, batch)
    met_normed, mine_qkv = meet(normed_rows), full_qkv
    if paired:
        mine_qkv = lax.dynamic_index_in_dim(
            full_qkv.reshape(width // block // 2, 2, block, qkv_cols), pair_first[0], 1, False
        ).reshape(width // 2, qkv_cols)
    late_qkv, came, attended, met_normed, mine_qkv = together(
        full_qkv, came, attended, met_normed, mine_qkv
    )
    grad_rows.append(came)
    attended_rows, totals = attended[:tp_count], attended[tp_count]
    mine = [attended_rows[0]] + [shift(attended_rows[place], -place) for place in range(1, tp_count)]
    grad_rows[-1], mine = together(grad_rows[-1], mine)
    for _ in range(len(grad_rows), tp_count):
        grad_rows.append(ring_hop(grad_rows[-1]))
    met_grads = meet(grad_rows)
    (mixed_in,) = rows_nt([([[(piece, 0) for piece in mine]], full_out)], jnp.float32, 1, rows)
    met_mine = [meet([piece]) for piece in mine]
    hidden, unit_hidden = add_and_norm(tokens, mixed_in)

    def feed(group):
        return feed_rows(
            [hidden_rows[place] for place in group],
            [grad_rows[place] for place in group],
            full_gate,
            full_up,
            full_down,
            hidden_cols,
        )

    def hidden_terms(fed):
        halves = range(tp_count // 2)
        gates, ups = ([[(fed[part], half)] for half in halves] for part in (1, 2))
        return rows_nt([(gates, full_gate), (ups, full_up)], jnp.bfloat16, len(halves), rows)

    first, second = list(places)[: tp_count // 2], list(places)[tp_count // 2 :]
    hidden_rows = [unit_hidden]
    fed_first, terms_first = None, None
    for place in range(1, tp_count):
        came = ring_hop(hidden_rows[-1])
        if place == len(first):
            fed_first = feed(first)
            came, fed_first, met_grads, met_mine = together(came, fed_first, met_grads, met_mine)
        if place == len(first) + 1:
            met_first = [meet([fed]) for fed in fed_first]
            terms_first = hidden_terms(fed_first)
            came, terms_first, met_first = together(came, terms_first, met_first)
        hidden_rows.append(came)

    came = ring_hop(terms_first[1])
    met_hidden = meet(hidden_rows)
    fed_second = feed(second)
    feed_terms = rows_nt([([[(fed_first[0], 1)]], full_down)], jnp.bfloat16, 1, rows)
    came, fed_second, met_hidden, feed_terms = together(came, fed_second, met_hidden, feed_terms)
    feed_came = ring_hop(feed_terms[0])
    met_fed = [old + meet([fed]) for old, fed in zip(met_first, fed_second)]
    if paired:
        met_fed = [[fed[0], fed[2], fed[1], fed[3]] for fed in met_fed]
    terms_second, feed_came = together(hidden_terms(fed_second), feed_came)
    came = ring_hop(add_rows(came, terms_second[0]))
    down_product = grad_product(met_grads, [met_fed[0]])
    feed_terms += rows_nt([([[(fed_second[0], 0)]], full_down)], jnp.bfloat16, 1, rows)
    came, down_product, feed_terms = together(came, down_product, feed_terms)
    came = ring_hop(add_rows(came, terms_second[1]))
    down_shard = scatter_sum(down_product)
    pair_product = grad_product(met_hidden, [met_fed[1]], more=1)
    feed_rest = rows_nt(
        [([[(fed_second[0], 1)], [(fed_first[0], 0)]], full_down)], jnp.bfloat16, 2, rows
    )
    came, pair_product, feed_rest = together(came, pair_product, feed_rest)
    feed_terms = dict(zip(order, feed_terms + feed_rest))

    grad_hidden, branch = norm_back(
        came, terms_first[0], hidden, grad_own, (jnp.float32, jnp.bfloat16)
    )
    pieces = split_columns(branch, full_second, 0, tp_count, q_cols)
    pieces, branch = together(pieces, branch)
    grad_att = [pieces[0]] + [shift(pieces[place], place) for place in range(1, tp_count)]
    met_branch = meet([branch])
    out_product = grad_product(met_branch, met_mine, share=0.1)
    out_product, pair_product = together(out_product, pair_product)
    pair_product = grad_product(met_hidden, [met_fed[2]], into=pair_product, share=0.1)
    grad_att, pair_product, out_product = together(grad_att, pair_product, out_product)
    out_shard = scatter_sum(out_product)
    pair_shard = scatter_sum(pair_product)

    half_count = len(masks) // 2
    kinds = [
        [jnp.float32] * half_count + [jnp.bfloat16] * half_count,
        [jnp.float32] + [jnp.bfloat16] * (len(masks) - 1),
    ]
    query_gain_sum = jnp.zeros((8, 2 * HD), jnp.float32)
    dq_parts, own_parts, came_parts = [], [], []
    came = feed_came
    for step, place in enumerate(order[1:]):
        if place:
            came = ring_hop(add_rows(came, feed_terms[place]))
        if step < 2:
            dq, back, addend = attend_back(
                starts,
                low,
                high,
                totals,
                cos_wide,
                sin_wide,
                q_gain,
                queries,
                raw,
                grad_att,
                attended_rows,
                blocks,
                kinds[step],
                batch,
                [0, batch - batch // 4][step],
                [batch - batch // 4, batch // 4][step],
            )
            if step == 0:
                came, dq, back, addend, grad_att, down_shard = together(
                    came, dq, back, addend, grad_att, down_shard
                )
            else:
                dq, back, addend, own_parts, came_parts = together(
                    dq, back, addend, own_parts, came_parts
                )
            query_gain_sum = query_gain_sum + addend
            dq_parts.append(dq)
            own_parts.append(back[0])
            if step:
                came_parts.append([ctx_swap(part, mask) for part, mask in zip(back[1:], masks[1:])])
                continue
            bit = 1
            while len(back) > 2:
                half_count = len(back) // 2
                back = [
                    back[i] + ctx_swap(back[half_count + i].astype(jnp.bfloat16), bit).astype(jnp.float32)
                    for i in range(half_count)
                ]
                bit *= 2
            own_parts[0] = back[0]
            came_parts.append([ctx_swap(back[1].astype(jnp.bfloat16), bit)])
        else:
            grad_qkv, key_gain_sum = heads_back(
                dq_parts, own_parts, came_parts, raw, cos_wide, sin_wide, k_gain
            )
            came, grad_qkv, out_shard = together(came, grad_qkv, out_shard)
    feed_out = came.astype(jnp.float32) + feed_terms[0].astype(jnp.float32)
    block_out = (hidden + feed_out).astype(jnp.bfloat16).reshape(block_in.shape)

    def out_hop(total, place):
        start = back_places[place] * q_cols
        total = ring_hop(total).astype(jnp.float32) + out_shard[:, start : start + q_cols].astype(
            jnp.float32
        )
        return total.astype(jnp.bfloat16) if place else total

    met_qkv = meet([grad_qkv])
    (first_term,) = rows_nt([([[(grad_qkv, order[0])]], (late_qkv, 0))], jnp.bfloat16, 1, rows)
    head_sums = jnp.stack([query_gain_sum, key_gain_sum]).sum(axis=1).reshape(2, 2, HD).sum(axis=1)
    total, met_qkv, grad_qkv = together(first_term, met_qkv, grad_qkv)
    lines = [[(grad_qkv, place)] for place in order[1:]]
    out_total = out_shard[:, back_places[1] * q_cols : (back_places[1] + 1) * q_cols]
    for step, place in enumerate(order[1:]):
        came = ring_hop(total)
        if step == 2:
            out_total, pair_shard, qkv_product = together(out_total, pair_shard, qkv_product)
            qkv_shard = scatter_sum(qkv_product)
        out_total = out_hop(out_total, place)
        if step < 2:
            came, out_total = together(came, out_total)
        if step == 0:
            head_sums = all_sum(head_sums, (CTX, "dp"))
            qkv_product = grad_product(met_normed, [met_qkv], tile=qkv_cols)
            attention_sum = jnp.sum(qkv_product.astype(jnp.float32) * mine_qkv.astype(jnp.float32), axis=1)
            row_terms = rows_nt([(lines, (late_qkv, 0))], jnp.bfloat16, len(lines), rows)
            came, head_sums, qkv_product, attention_sum, row_terms = together(
                came, head_sums, qkv_product, attention_sum, row_terms
            )
            row_terms = dict(zip(order[1:], row_terms))
            small_sums = jnp.concatenate([attention_sum, head_sums.reshape(-1)])
        if step == 1:
            small_sums = all_sum(small_sums, ("tp",))
            came, small_sums = together(came, small_sums)
            head_sums = small_sums[-2 * HD :].reshape(2, HD)
            column = jnp.pad(small_sums[: -2 * HD].astype(jnp.bfloat16)[:, None], ((0, 0), (0, 127)))
            qkv_product = jnp.concatenate([qkv_product, column], axis=1)
        if place:
            total = add_rows(came, row_terms[place])
    pair_sums = pair_shard.astype(jnp.float32)
    gate_sums, up_sums = pair_sums[:, :hidden_cols], pair_sums[:, hidden_cols:]
    hidden_sums = jnp.sum(
        gate_sums * gate_weight.astype(jnp.float32) + up_sums * up_weight.astype(jnp.float32), axis=1
    )
    hidden_gain_grad = hidden_sums
    stages = []
    for stage in range(tp_count.bit_length() - 1):
        stages.append([(i, i ^ (1 << stage)) for i in range(tp_count)])
    hidden_gain_grad = hidden_gain_grad + lax.ppermute(hidden_gain_grad, "tp", stages[0])
    qkv_sums = qkv_shard[:, :qkv_cols].astype(jnp.float32)
    attention_gain_grad = qkv_shard[:, qkv_cols].astype(jnp.float32) / attention_rows[:, 0]
    (input_grad,) = norm_back(came, row_terms[0], tokens, grad_hidden, (jnp.float32,))
    input_grad, hidden_gain_grad = together(input_grad, hidden_gain_grad)
    for pairs in stages[1:]:
        hidden_gain_grad = hidden_gain_grad + lax.ppermute(hidden_gain_grad, "tp", pairs)
    output_grad = out_total.T
    down_grad = down_shard.astype(jnp.float32).T
    gate_grad, up_grad = gate_sums * hidden_gain_rows, up_sums * hidden_gain_rows
    qkv_grad = qkv_sums * attention_rows
    return (
        block_out,
        input_grad.reshape(block_in.shape),
        attention_gain_grad,
        qkv_grad[:, :q_cols],
        qkv_grad[:, q_cols : q_cols + k_cols],
        qkv_grad[:, q_cols + k_cols :],
        head_sums[0],
        head_sums[1],
        output_grad,
        hidden_gain_grad,
        gate_grad,
        up_grad,
        down_grad,
    )


def solution(mesh):
    in_specs = (
        P(None, ("dp", *CTX, "tp"), None),
        P(None, "dp"),
        P(None, "dp"),
        P(("dp", *CTX)),
        P(("dp", *CTX), "tp"),
        P(("dp", *CTX), "tp"),
        P(("dp", *CTX), "tp"),
        P(),
        P(),
        P("tp", ("dp", *CTX)),
        P(("dp", *CTX)),
        P(("dp", *CTX), "tp"),
        P(("dp", *CTX), "tp"),
        P("tp", ("dp", *CTX)),
        P(None, ("dp", *CTX, "tp"), None),
    )
    out_specs = (
        P(None, ("dp", *CTX, "tp"), None),
        P(None, ("dp", *CTX, "tp"), None),
        P(("dp", *CTX)),
        P(("dp", *CTX), "tp"),
        P(("dp", *CTX), "tp"),
        P(("dp", *CTX), "tp"),
        P(),
        P(),
        P("tp", ("dp", *CTX)),
        P(("dp", *CTX)),
        P(("dp", *CTX), "tp"),
        P(("dp", *CTX), "tp"),
        P("tp", ("dp", *CTX)),
    )
    shape = (mesh.shape["dp"], mesh.shape["ctx"] // 2, 2, mesh.shape["tp"])
    split = Mesh(mesh.devices.reshape(shape), ("dp", *CTX, "tp"))
    return jax.shard_map(
        per_device, mesh=split, in_specs=in_specs, out_specs=out_specs, check_vma=False
    )
```
